32 devices in a mesh: seq: 16 (over z, y, x), head: 2 (over core).
Axes of the slice: x: 2, y: 2, z: 4, core: 2. Of those that a mesh axis runs over, the one named last changes fastest.
Arguments:
- queries: bfloat16 [8192, 2048], P(('seq', 'head')), may hold values from -6 to 6
- key_rows: bfloat16 [8192, 2048], P(('seq', 'head')), may hold values from -6 to 6
- values: bfloat16 [8192, 2048], P(('seq', 'head')), may hold values from -6 to 6
- out_grad: bfloat16 [8192, 2048], P(('seq', 'head')), may hold values from -6 to 6
- level_weights: float32 [16, 11], replicated, may hold values from 0.2 to 1
Outputs:
- query_grad: bfloat16 [8192, 2048], P(('seq', 'head'))
- key_grad: bfloat16 [8192, 2048], P(('seq', 'head'))
- value_grad: bfloat16 [8192, 2048], P(('seq', 'head'))
The draws below stay inside these ranges and needn't reach their ends.
All inputs are finite; a program needn't handle non-finite values.
Results may differ from the reference program's by a relative error of at most 0.003.
Values may be sent and summed in bfloat16 or wider, within the bound.
No kernel may reach another device: no remote copies, remote signals or barrier semaphores. Data moves between devices by JAX's collectives and lax.ppermute only.
A program may use at most 128 MiB of HBM per device.

```python
import math
import jax
import jax.numpy as jnp
from jax import lax

HEADS = 16
DH = 128
D = 2048
BLOCK = 128
LEVELS = 11
TOKENS = 8192


def shard_levels(rng, dims, split, least, high):
    level = 1.0
    for dim, blocks in split:
        steps = jax.random.uniform(jax.random.fold_in(jax.random.fold_in(rng, 6), dim), (blocks,), jnp.float32, least / len(split), high / len(split))
        level = level * jnp.repeat(jnp.exp(steps), dims[dim] // blocks).reshape((-1,) + (1,) * (len(dims) - 1 - dim))
    return level


def centred(stream_key, shape, width, most, cuts=(), kind=jnp.bfloat16):
    array = width * jax.random.normal(stream_key, shape, jnp.float32)
    if cuts:
        array = array * shard_levels(stream_key, shape, cuts, -0.22, 0.18)
    return jnp.clip(array, -most, most).astype(kind)


def setup_inputs(seed: int = 0) -> dict:
    splits = jax.random.split(jax.random.key(seed), 6)
    queries = centred(splits[0], (TOKENS, D), 1.0, 6.0, ((0, 32),))
    key_rows = centred(splits[1], (TOKENS, D), 1.0, 6.0, ((0, 32),))
    values = centred(splits[2], (TOKENS, D), 1.0, 6.0, ((0, 32),))
    out_grad = centred(splits[3], (TOKENS, D), 1.0, 6.0, ((0, 32),))
    level_weights = jnp.clip(jnp.exp(jax.random.uniform(splits[4], (HEADS, LEVELS), jnp.float32, math.log(0.2), math.log(1.0))), 0.2, 1.0)
    return dict(queries=queries, key_rows=key_rows, values=values, out_grad=out_grad, level_weights=level_weights)


def fenwick_local(kv_blocks, qo_blocks, level_scale):
    block_count = kv_blocks.shape[0]
    inner_shape = kv_blocks.shape[1:]
    earlier = jnp.zeros_like(kv_blocks)
    later = jnp.zeros_like(qo_blocks)
    for level_index in range(1, block_count.bit_length()):
        half_span = 1 << level_index - 1
        group_count = block_count >> level_index
        weight = level_scale[:, level_index][:, None, None]
        kv_groups = kv_blocks.reshape((group_count, 2, half_span) + inner_shape)
        qo_groups = qo_blocks.reshape((group_count, 2, half_span) + inner_shape)
        lower_sum = lax.optimization_barrier(jnp.sum(kv_groups[:, 0], axis=1)) * weight
        upper_sum = lax.optimization_barrier(jnp.sum(qo_groups[:, 1], axis=1)) * weight
        zero_block = jnp.zeros_like(lower_sum)
        add_earlier = jnp.stack([zero_block, lower_sum], axis=1)[:, :, None]
        add_later = jnp.stack([upper_sum, zero_block], axis=1)[:, :, None]
        full_shape = (group_count, 2, half_span) + inner_shape
        earlier = earlier + jnp.broadcast_to(add_earlier, full_shape).reshape(kv_blocks.shape)
        later = later + jnp.broadcast_to(add_later, full_shape).reshape(qo_blocks.shape)
    return (earlier, later)

def block_grads(query_blk, key_blk, value_blk, grad_blk, level_scale):
    high = lax.Precision.HIGHEST
    block_len = query_blk.shape[1]
    query_f = query_blk.astype(jnp.float32)
    key_f = key_blk.astype(jnp.float32)
    value_f = value_blk.astype(jnp.float32)
    grad_f = grad_blk.astype(jnp.float32)
    rows = lax.broadcasted_iota(jnp.int32, (block_len, block_len), 0)
    cols = lax.broadcasted_iota(jnp.int32, (block_len, block_len), 1)
    causal_mask = (rows >= cols).astype(jnp.float32)
    first_weight = level_scale[:, 0][None, :, None, None]
    scores = jnp.einsum('nthd,nshd->nhts', query_f, key_f, precision=high)
    weighted = (scores * causal_mask * first_weight).astype(jnp.bfloat16)
    grad_prob = jnp.einsum('nthe,nshe->nhts', grad_f, value_f, precision=high)
    grad_score = (grad_prob * causal_mask * first_weight).astype(jnp.bfloat16)
    weighted_f = weighted.astype(jnp.float32)
    grad_score_f = grad_score.astype(jnp.float32)
    value_local = jnp.einsum('nhts,nthe->nshe', weighted_f, grad_f, precision=high)
    query_local = jnp.einsum('nhts,nshd->nthd', grad_score_f, key_f, precision=high)
    key_local = jnp.einsum('nhts,nthd->nshd', grad_score_f, query_f, precision=high)
    kv_blocks = jnp.einsum('nshd,nshe->nhde', key_f, value_f, precision=high)
    qo_blocks = jnp.einsum('nthd,nthe->nhde', query_f, grad_f, precision=high)
    earlier, later = fenwick_local(kv_blocks, qo_blocks, level_scale)
    query_cross = jnp.einsum('nthe,nhde->nthd', grad_f, earlier, precision=high)
    key_cross = jnp.einsum('nshe,nhde->nshd', value_f, later, precision=high)
    value_cross = jnp.einsum('nshd,nhde->nshe', key_f, later, precision=high)
    return ((query_local + query_cross).astype(jnp.bfloat16), (key_local + key_cross).astype(jnp.bfloat16), (value_local + value_cross).astype(jnp.bfloat16))

def reference(queries, key_rows, values, out_grad, level_weights):
    level_ids = jnp.arange(LEVELS, dtype=jnp.float32)
    level_scale = level_weights * jnp.exp2((1.0 - level_ids) / 2.0)[None, :] / jnp.sqrt(jnp.float32(DH * BLOCK))

    def per_head(packed):
        return packed.reshape(TOKENS // BLOCK, BLOCK, HEADS, DH).transpose(2, 0, 1, 3)[:, :, :, None, :]

    def one_head(items):
        query_blk, key_blk, value_blk, grad_blk, head_scale = items
        return block_grads(query_blk, key_blk, value_blk, grad_blk, head_scale)
    results = lax.map(one_head, (per_head(queries), per_head(key_rows), per_head(values), per_head(out_grad), level_scale[:, None, :]))

    def unpack(stacked):
        return stacked[:, :, :, 0, :].transpose(1, 2, 0, 3).reshape(TOKENS, HEADS * DH)
    return (unpack(results[0]), unpack(results[1]), unpack(results[2]))
```

```python
import functools
import math

import jax
import jax.numpy as jnp
from jax import lax
from jax.experimental import pallas as pl
from jax.experimental.pallas import tpu as pltpu
from jax.sharding import PartitionSpec as P

DH = 128
BLOCK = 128
F32 = jnp.float32
BF16 = jnp.bfloat16
NT = (((1,), (1,)), ((), ()))
TN = (((0,), (0,)), ((), ()))


def dot(a, b, dims=None):
    if dims is None:
        dims = (((1,), (0,)), ((), ()))
    return lax.dot_general(a, b, dims, preferred_element_type=F32)


def split(x):
    hi = x.astype(BF16)
    return hi, (x - hi.astype(F32)).astype(BF16)


def partner(array, axis, distance):
    return lax.ppermute(array, axis, [(i, i ^ distance) for i in range(lax.axis_size(axis))])


def state_kernel(pos_ref, q_ref, k_ref, v_ref, o_ref, out_ref):
    for j in range(out_ref.shape[2]):
        cols = slice(j * DH, (j + 1) * DH)
        out_ref[0, 0, j] = dot(v_ref[:, cols], k_ref[:, cols], TN)
        out_ref[0, 1, j] = dot(o_ref[:, cols], q_ref[:, cols], TN)


def device_states(pos, q, k, v, o, slices, width):
    tokens = q.shape[0]
    spec = pl.BlockSpec(
        (tokens, width * DH), lambda d, pos: (0, pos[0] * slices + (pos[1] ^ d))
    )
    return pl.pallas_call(
        state_kernel,
        grid_spec=pltpu.PrefetchScalarGridSpec(
            num_scalar_prefetch=1,
            grid=(slices,),
            in_specs=[spec] * 4,
            out_specs=pl.BlockSpec((1, 2, width, DH, DH), lambda d, pos: (d, 0, 0, 0, 0)),
        ),
        out_shape=jax.ShapeDtypeStruct((slices, 2, width, DH, DH), F32),
        cost_estimate=pl.CostEstimate(
            flops=4 * slices * width * tokens * DH * DH,
            bytes_accessed=8 * slices * width * DH * (tokens + DH),
            transcendentals=0,
        ),
        name="states",
    )(pos, q, k, v, o)


def local_kernel(scale_ref, q_ref, k_ref, v_ref, o_ref, qg_ref, kg_ref, vg_ref):
    tokens = q_ref.shape[0]
    blocks = tokens // BLOCK
    width = q_ref.shape[1] // DH
    step = pl.program_id(0)
    rows = lax.broadcasted_iota(jnp.int32, (BLOCK, BLOCK), 0)
    cols = lax.broadcasted_iota(jnp.int32, (BLOCK, BLOCK), 1)
    lower = rows >= cols
    upper = rows <= cols
    for j in range(width):
        head = step * width + j
        cs = slice(j * DH, (j + 1) * DH)
        for n in range(blocks):
            here = slice(n * BLOCK, (n + 1) * BLOCK)
            q, k, v, o = q_ref[here, cs], k_ref[here, cs], v_ref[here, cs], o_ref[here, cs]
            first = scale_ref[head, 0]
            score_t = jnp.where(upper, dot(k, q, NT) * first, 0.0).astype(BF16)
            grad = jnp.where(lower, dot(o, v, NT) * first, 0.0).astype(BF16)
            grad_t = jnp.where(upper, dot(v, o, NT) * first, 0.0).astype(BF16)
            vg = dot(score_t, o)
            qg = dot(grad, k)
            kg = dot(grad_t, q)
            for m in range(blocks):
                if m == n:
                    continue
                there = slice(m * BLOCK, (m + 1) * BLOCK)
                weight = scale_ref[head, (m ^ n).bit_length()]
                if m < n:
                    hi, lo = split(dot(o, v_ref[there, cs], NT) * weight)
                    other = k_ref[there, cs]
                    qg = qg + dot(hi, other) + dot(lo, other)
                else:
                    hi, lo = split(dot(v, o_ref[there, cs], NT) * weight)
                    other = q_ref[there, cs]
                    kg = kg + dot(hi, other) + dot(lo, other)
                    hi, lo = split(dot(k, q_ref[there, cs], NT) * weight)
                    other = o_ref[there, cs]
                    vg = vg + dot(hi, other) + dot(lo, other)
            qg_ref[here, cs] = qg
            kg_ref[here, cs] = kg
            vg_ref[here, cs] = vg


def local_grads(level_scale, q, k, v, o, width):
    tokens, model = q.shape
    spec = pl.BlockSpec((tokens, width * DH), lambda i: (0, i))
    return pl.pallas_call(
        local_kernel,
        grid=(model // (width * DH),),
        in_specs=[pl.BlockSpec(memory_space=pltpu.SMEM)] + [spec] * 4,
        out_specs=[spec] * 3,
        out_shape=[jax.ShapeDtypeStruct((tokens, model), F32)] * 3,
        cost_estimate=pl.CostEstimate(
            flops=24 * tokens * BLOCK * model, bytes_accessed=20 * tokens * model, transcendentals=0
        ),
        name="local",
    )(level_scale, q, k, v, o)


def cross_kernel(pos_ref, mine_ref, other_ref, k_ref, v_ref, o_ref, ql_ref, kl_ref, vl_ref, qg_ref, kg_ref, vg_ref):
    width = mine_ref.shape[2]
    own = pl.program_id(0) == 0
    for j in range(width):
        cs = slice(j * DH, (j + 1) * DH)
        early = jnp.where(own, mine_ref[0, 0, j], other_ref[0, 0, j])
        late = jnp.where(own, mine_ref[0, 1, j], other_ref[0, 1, j])
        hi, lo = split(early)
        o = o_ref[:, cs]
        qg_ref[:, cs] = (ql_ref[:, cs] + (dot(o, hi) + dot(o, lo))).astype(BF16)
        hi, lo = split(late)
        v = v_ref[:, cs]
        kg_ref[:, cs] = (kl_ref[:, cs] + (dot(v, hi) + dot(v, lo))).astype(BF16)
        k = k_ref[:, cs]
        vg_ref[:, cs] = (vl_ref[:, cs] + (dot(k, hi, NT) + dot(k, lo, NT))).astype(BF16)


def finish(pos, mine, other, k, v, o, local, slices, width):
    tokens, model = k.shape
    spec = pl.BlockSpec(
        (tokens, width * DH),
        lambda half, d, pos: (0, (pos[0] ^ half) * slices + (pos[1] ^ d)),
    )
    state = (1, 2, width, DH, DH)
    last = slices - 1
    return pl.pallas_call(
        cross_kernel,
        grid_spec=pltpu.PrefetchScalarGridSpec(
            num_scalar_prefetch=1,
            grid=(2, slices),
            in_specs=[
                pl.BlockSpec(state, lambda half, d, pos: (d * (1 - half) + last * half, 0, 0, 0, 0)),
                pl.BlockSpec(state, lambda half, d, pos: (d * half, 0, 0, 0, 0)),
            ]
            + [spec] * 6,
            out_specs=[spec] * 3,
        ),
        out_shape=[jax.ShapeDtypeStruct((tokens, model), BF16)] * 3,
        cost_estimate=pl.CostEstimate(
            flops=12 * tokens * DH * model, bytes_accessed=24 * tokens * model, transcendentals=0
        ),
        name="finish",
    )(pos, mine, other, k, v, o, *local)


def body(queries, key_rows, values, out_grad, level_weights):
    level_ids = jnp.arange(level_weights.shape[1], dtype=F32)
    level_scale = level_weights * jnp.exp2((1.0 - level_ids) / 2.0)[None, :] / jnp.sqrt(F32(DH * BLOCK))
    heads = level_weights.shape[0]
    tokens = queries.shape[0]
    chain = lax.axis_size("seq")
    halves = lax.axis_size("head")
    bits = chain.bit_length() - 1
    plane_bits = min(2, bits)
    slices = 1 << plane_bits
    width = heads // (halves * slices)
    local_levels = (tokens // BLOCK).bit_length() - 1
    core = lax.axis_index("head")
    seq = lax.axis_index("seq")
    place = seq % slices
    row = seq // slices

    args = (queries, key_rows, values, out_grad)
    sent = device_states(jnp.stack([1 - core, place]).astype(jnp.int32), *args, slices, width)
    other = partner(sent, "head", 1)
    pos = jnp.stack([core, place]).astype(jnp.int32)
    own = device_states(pos, *args, slices, width)
    local = local_grads(level_scale, *args, width)

    by_slice = level_scale.reshape(halves, slices, width, -1)[core]
    relative = jnp.stack([by_slice[place ^ d] for d in range(slices)])
    mine_scale = relative[0]

    def weigh(level):
        return mine_scale[:, level][:, None, None]

    def bit_of(value, index):
        return ((value >> index) & 1).astype(F32)

    base = local_levels + 2
    chip = own + other
    parts = [chip[0]] + [partner(chip[d], "seq", d) for d in range(1, slices)]
    earlier = [jnp.zeros((width, DH, DH), F32) for _ in range(slices)]
    later = [jnp.zeros((width, DH, DH), F32) for _ in range(slices)]
    for d in range(slices):
        for e in range(slices):
            if e == d:
                continue
            top = (d ^ e).bit_length() - 1
            up = bit_of(place ^ d, top)
            earlier[d] = earlier[d] + (up * weigh(base + top)) * parts[e][0]
            later[d] = later[d] + ((1.0 - up) * weigh(base + top)) * parts[e][1]
    total = functools.reduce(jnp.add, parts)
    far_early = jnp.zeros((width, DH, DH), F32)
    far_late = jnp.zeros((width, DH, DH), F32)
    rest = bits - plane_bits
    direct = min(2, rest)
    for index in range(rest - direct):
        got = partner(total, "seq", slices << index)
        up = bit_of(row, index)
        weight = weigh(base + plane_bits + index)
        far_early = far_early + up * weight * got[0]
        far_late = far_late + (1.0 - up) * weight * got[1]
        total = total + got
    for step in range(1, 1 << direct):
        top = step.bit_length() - 1 + rest - direct
        up = bit_of(row, top)
        give = jnp.where(up > 0, total[1], total[0])
        got = partner(give, "seq", slices << (rest - direct) if step == 1 else (slices << (rest - direct)) * step)
        weight = weigh(base + plane_bits + top)
        far_early = far_early + (up * weight) * got
        far_late = far_late + ((1.0 - up) * weight) * got
    result = [jnp.stack([earlier[d] + far_early, later[d] + far_late]) for d in range(slices)]
    back = [result[0]] + [partner(result[d], "seq", d) for d in range(1, slices)]
    states = jnp.stack(back)
    weight = relative[:, :, local_levels + 1]
    second = core.astype(F32)
    to_other = jnp.stack([(1.0 - second) * weight, second * weight], axis=1)[..., None, None]
    to_mine = jnp.stack([second * weight, (1.0 - second) * weight], axis=1)[..., None, None]
    theirs = partner(states + to_other * own, "head", 1)
    mine = states + to_mine * other
    return tuple(finish(pos, mine, theirs, key_rows, values, out_grad, local, slices, width))


def solution(mesh):
    rows = P(("seq", "head"), None)
    return jax.shard_map(
        body,
        mesh=mesh,
        in_specs=(rows, rows, rows, rows, P()),
        out_specs=(rows, rows, rows),
        check_vma=False,
    )
```

```python
import functools
import math

import jax
import jax.numpy as jnp
from jax import lax
from jax.experimental import pallas as pl
from jax.experimental.pallas import tpu as pltpu
from jax.sharding import PartitionSpec as P

DH = 128
BLOCK = 128
F32 = jnp.float32
BF16 = jnp.bfloat16
NT = (((1,), (1,)), ((), ()))
TN = (((0,), (0,)), ((), ()))


def dot(a, b, dims=None):
    if dims is None:
        dims = (((1,), (0,)), ((), ()))
    return lax.dot_general(a, b, dims, preferred_element_type=F32)


def split(x):
    hi = x.astype(BF16)
    return hi, (x - hi.astype(F32)).astype(BF16)


def partner(array, axis, distance):
    return lax.ppermute(array, axis, [(i, i ^ distance) for i in range(lax.axis_size(axis))])


VMEM = pl.BlockSpec(memory_space=pltpu.VMEM)
SMEM = pl.BlockSpec(memory_space=pltpu.SMEM)
HBM = pl.BlockSpec(memory_space=pl.ANY)


def columns(half, place, slices, width):
    core = lax.axis_index("head") ^ half
    return pl.multiple_of((core * slices + place) * (width * DH), DH)


def group_place(slices):
    return lax.axis_index("seq") & (slices - 1)


def state_kernel(half, q_ref, k_ref, v_ref, o_ref, out_ref):
    slices, _, width = out_ref.shape[:3]
    place = group_place(slices)
    for d in range(slices):
        start = columns(half, place ^ d, slices, width)
        for j in range(width):
            cols = pl.ds(pl.multiple_of(start + j * DH, DH), DH)
            out_ref[d, 0, j] = dot(v_ref[:, cols], k_ref[:, cols], TN)
            out_ref[d, 1, j] = dot(o_ref[:, cols], q_ref[:, cols], TN)


def device_states(half, q, k, v, o, slices, width):
    tokens = q.shape[0]
    return pl.pallas_call(
        functools.partial(state_kernel, half),
        in_specs=[VMEM] * 4,
        out_specs=VMEM,
        out_shape=pltpu.VMEM((slices, 2, width, DH, DH), F32),
        compiler_params=pltpu.CompilerParams(vmem_limit_bytes=4 << 20),
        cost_estimate=pl.CostEstimate(
            flops=4 * slices * width * tokens * DH * DH,
            bytes_accessed=8 * slices * width * DH * (tokens + DH),
            transcendentals=0,
        ),
        name=f"states_{half}",
    )(q, k, v, o)


def local_kernel(first_head, heads, scale_ref, q_ref, k_ref, v_ref, o_ref, qg_ref, kg_ref, vg_ref):
    tokens = q_ref.shape[0]
    blocks = tokens // BLOCK
    rows = lax.broadcasted_iota(jnp.int32, (BLOCK, BLOCK), 0)
    cols = lax.broadcasted_iota(jnp.int32, (BLOCK, BLOCK), 1)

    def blk(n, m=None):
        return slice(n * BLOCK, (n + 1 if m is None else m) * BLOCK)

    def product(left, right, weight, values, n, low, high, mask):
        raw = dot(left[blk(n)], right[blk(low, high)], NT)
        parts, rest = [], []
        for m in range(low, high):
            part = raw[:, blk(m - low)]
            if m == n:
                parts.append(jnp.where(mask, part * weight(0), 0.0).astype(BF16))
            else:
                hi, lo = split(part * weight((m ^ n).bit_length()))
                parts.append(hi)
                rest.append((m, lo))
        out = dot(jnp.concatenate(parts, axis=1) if len(parts) > 1 else parts[0], values[blk(low, high)])
        for m, lo in rest:
            out = out + dot(lo, values[blk(m)])
        return out

    def one(index, _):
        head = first_head + index
        here = pl.ds(pl.multiple_of(head * DH, DH), DH)
        there = pl.ds(pl.multiple_of(index * DH, DH), DH)
        q, k, v, o = q_ref[:, here], k_ref[:, here], v_ref[:, here], o_ref[:, here]

        def weight(level):
            return scale_ref[head, level]

        for n in range(blocks):
            vg_ref[blk(n), there] = product(k, q, weight, o, n, n, blocks, rows <= cols)
            kg_ref[blk(n), there] = product(v, o, weight, q, n, n, blocks, rows <= cols)
            qg_ref[blk(n), there] = product(o, v, weight, k, n, 0, n + 1, rows >= cols)
        return 0

    lax.fori_loop(0, heads, one, 0, unroll=2)


def local_grads(level_scale, q, k, v, o, first_head, heads):
    tokens = q.shape[0]
    out = pltpu.VMEM((tokens, heads * DH), F32)
    return pl.pallas_call(
        functools.partial(local_kernel, first_head, heads),
        in_specs=[SMEM] + [VMEM] * 4,
        out_specs=[VMEM] * 3,
        out_shape=[out] * 3,
        compiler_params=pltpu.CompilerParams(vmem_limit_bytes=4 << 20),
        cost_estimate=pl.CostEstimate(
            flops=24 * tokens * BLOCK * heads * DH, bytes_accessed=20 * tokens * heads * DH, transcendentals=0
        ),
        name=f"local_{first_head}",
    )(level_scale, q, k, v, o)


def cross_kernel(count, mine_ref, other_ref, k_ref, v_ref, o_ref, *refs):
    slices, _, width = mine_ref.shape[:3]
    place = group_place(slices)
    local = [refs[3 * i : 3 * i + 3] for i in range(count)]
    outs = refs[3 * count : 3 * count + 3]
    held = refs[3 * count + 3 : 3 * count + 6]
    sems = refs[3 * count + 6]
    heads = k_ref.shape[1] // DH
    per = heads // count
    copies = []
    for half in range(2):
        state_ref = (mine_ref, other_ref)[half]
        for d in range(slices):
            start = columns(half, place ^ d, slices, width)
            for j in range(width):
                at = pl.multiple_of(start + j * DH, DH)
                cs = pl.ds(at, DH)
                o, v, k = o_ref[:, cs], v_ref[:, cs], k_ref[:, cs]
                hi, lo = split(state_ref[d, 0, j])
                qg = dot(o, hi) + dot(o, lo)
                hi, lo = split(state_ref[d, 1, j])
                kg = dot(v, hi) + dot(v, lo)
                vg = dot(k, hi, NT) + dot(k, lo, NT)
                for i, cross in enumerate((qg, kg, vg)):
                    held[i][:, cs] = (cross + local[0][i][:, cs]).astype(BF16)
            cs = pl.ds(start, width * DH)
            for i in range(3):
                copy = pltpu.make_async_copy(
                    held[i].at[:, cs], outs[i].at[:, cs], sems.at[half * slices + d, i]
                )
                copy.start()
                copies.append(copy)
    for copy in copies:
        copy.wait()


def finish(mine, other, k, v, o, local):
    tokens, model = k.shape
    slices = mine.shape[0]
    flat = [part for group in local for part in group]
    return pl.pallas_call(
        functools.partial(cross_kernel, len(local)),
        in_specs=[VMEM] * (5 + len(flat)),
        out_specs=[HBM] * 3,
        out_shape=[jax.ShapeDtypeStruct((tokens, model), BF16)] * 3,
        scratch_shapes=[pltpu.VMEM((tokens, model), BF16)] * 3 + [pltpu.SemaphoreType.DMA((2 * slices, 3))],
        compiler_params=pltpu.CompilerParams(vmem_limit_bytes=8 << 20),
        cost_estimate=pl.CostEstimate(
            flops=12 * tokens * DH * model, bytes_accessed=24 * tokens * model, transcendentals=0
        ),
        name="finish",
    )(mine, other, k, v, o, *flat)


def body(queries, key_rows, values, out_grad, level_weights):
    level_ids = jnp.arange(level_weights.shape[1], dtype=F32)
    level_scale = level_weights * jnp.exp2((1.0 - level_ids) / 2.0)[None, :] / jnp.sqrt(F32(DH * BLOCK))
    heads = level_weights.shape[0]
    tokens = queries.shape[0]
    chain = lax.axis_size("seq")
    halves = lax.axis_size("head")
    bits = chain.bit_length() - 1
    plane_bits = min(2, bits)
    slices = 1 << plane_bits
    width = heads // (halves * slices)
    local_levels = (tokens // BLOCK).bit_length() - 1
    core = lax.axis_index("head")
    seq = lax.axis_index("seq")
    place = seq % slices
    row = seq // slices

    args = (queries, key_rows, values, out_grad)
    sent = device_states(1, *args, slices, width)
    other = partner(sent, "head", 1)
    own = device_states(0, *args, slices, width)
    local = [local_grads(level_scale, *args, 0, heads)]

    by_slice = level_scale.reshape(halves, slices, width, -1)[core]
    relative = jnp.stack([by_slice[place ^ d] for d in range(slices)])
    mine_scale = relative[0]

    def weigh(level):
        return mine_scale[:, level][:, None, None]

    def bit_of(value, index):
        return ((value >> index) & 1).astype(F32)

    base = local_levels + 2
    chip = own + other
    parts = [chip[0]] + [partner(chip[d], "seq", d) for d in range(1, slices)]
    earlier = [jnp.zeros((width, DH, DH), F32) for _ in range(slices)]
    later = [jnp.zeros((width, DH, DH), F32) for _ in range(slices)]
    for d in range(slices):
        for e in range(slices):
            if e == d:
                continue
            top = (d ^ e).bit_length() - 1
            up = bit_of(place ^ d, top)
            earlier[d] = earlier[d] + (up * weigh(base + top)) * parts[e][0]
            later[d] = later[d] + ((1.0 - up) * weigh(base + top)) * parts[e][1]
    total = functools.reduce(jnp.add, parts)
    far_early = jnp.zeros((width, DH, DH), F32)
    far_late = jnp.zeros((width, DH, DH), F32)
    rest = bits - plane_bits
    direct = min(2, rest)
    for index in range(rest - direct):
        got = partner(total, "seq", slices << index)
        up = bit_of(row, index)
        weight = weigh(base + plane_bits + index)
        far_early = far_early + up * weight * got[0]
        far_late = far_late + (1.0 - up) * weight * got[1]
        total = total + got
    for step in range(1, 1 << direct):
        top = step.bit_length() - 1 + rest - direct
        up = bit_of(row, top)
        give = jnp.where(up > 0, total[1], total[0])
        got = partner(give, "seq", slices << (rest - direct) if step == 1 else (slices << (rest - direct)) * step)
        weight = weigh(base + plane_bits + top)
        far_early = far_early + (up * weight) * got
        far_late = far_late + ((1.0 - up) * weight) * got
    result = [jnp.stack([earlier[d] + far_early, later[d] + far_late]) for d in range(slices)]
    back = [result[0]] + [partner(result[d], "seq", d) for d in range(1, slices)]
    states = jnp.stack(back)
    weight = relative[:, :, local_levels + 1]
    second = core.astype(F32)
    to_other = jnp.stack([(1.0 - second) * weight, second * weight], axis=1)[..., None, None]
    to_mine = jnp.stack([second * weight, (1.0 - second) * weight], axis=1)[..., None, None]
    theirs = partner(states + to_other * own, "head", 1)
    mine = states + to_mine * other
    return tuple(finish(mine, theirs, key_rows, values, out_grad, local))


def solution(mesh):
    rows = P(("seq", "head"), None)
    return jax.shard_map(
        body,
        mesh=mesh,
        in_specs=(rows, rows, rows, rows, P()),
        out_specs=(rows, rows, rows),
        check_vma=False,
    )
```

```python
import functools

import jax
import jax.numpy as jnp
from jax import lax
from jax.experimental import pallas as pl
from jax.experimental.pallas import tpu as pltpu
from jax.sharding import PartitionSpec as P

DH = 128
BLOCK = 128
EXTRA = 16
TOP = 14.0
F32 = jnp.float32
BF16 = jnp.bfloat16
F16 = jnp.float16
NT = (((1,), (1,)), ((), ()))
TN = (((0,), (0,)), ((), ()))
VMEM = pl.BlockSpec(memory_space=pltpu.VMEM)
SMEM = pl.BlockSpec(memory_space=pltpu.SMEM)
HBM = pl.BlockSpec(memory_space=pltpu.HBM)


def dot(a, b, dims=None):
    if dims is None:
        dims = (((1,), (0,)), ((), ()))
    return lax.dot_general(a, b, dims, preferred_element_type=F32)


def split(x):
    hi = x.astype(BF16)
    return hi, (x - hi.astype(F32)).astype(BF16)


def call(kernel, outs, args, specs=None, out_specs=None, scratch=(), flops=0, limit=2):
    moved = sum(x.size * x.dtype.itemsize for x in args)
    return pl.pallas_call(
        kernel,
        in_specs=specs or [VMEM] * len(args),
        out_specs=out_specs or [VMEM] * len(outs),
        out_shape=list(outs),
        scratch_shapes=list(scratch),
        compiler_params=pltpu.CompilerParams(vmem_limit_bytes=limit << 20),
        cost_estimate=pl.CostEstimate(flops=flops, bytes_accessed=moved, transcendentals=0),
    )(*args)


def partner(array, axis, distance):
    return lax.ppermute(array, axis, [(i, i ^ distance) for i in range(lax.axis_size(axis))])


def narrow(array, axis, distance):
    return partner(array.astype(F16), axis, distance).astype(F32)


def pack(out_ref, values):
    rows = 0
    marks = []
    for value in values:
        most = jnp.maximum(jnp.max(jnp.abs(value)), 1e-30)
        power = TOP - jnp.ceil(jnp.log2(jnp.full((8, DH), most, F32)))
        flat = value.reshape(-1, DH)
        factor = jnp.exp2(power)[:1]
        out_ref[rows : rows + flat.shape[0]] = flat * factor
        rows += flat.shape[0]
        marks.append(power)
    for i in range(EXTRA // 8):
        out_ref[rows + 8 * i : rows + 8 * i + 8] = marks[min(i, len(marks) - 1)]


def unpack(ref, shape, count):
    size = (ref.shape[0] - EXTRA) // count
    out = []
    for i in range(count):
        factor = jnp.exp2(-ref[count * size + 8 * i : count * size + 8 * i + 1])
        out.append((ref[i * size : (i + 1) * size] * factor).reshape(shape))
    return out


def column(half, d, slices, width):
    core = lax.axis_index("head") ^ half
    place = (lax.axis_index("seq") & (slices - 1)) ^ d
    return pl.multiple_of((core * slices + place) * (width * DH), DH)


def state_kernel(half, *refs):
    srcs, (out_ref, q_ref, k_ref, v_ref, o_ref), sems = refs[:4], refs[4:9], refs[9]
    slices, _, width = out_ref.shape[:3]
    held = (q_ref, k_ref, v_ref, o_ref)
    copies = []
    for d in range(slices):
        cols = pl.ds(column(half, d, slices, width), width * DH)
        for i in range(4):
            copy = pltpu.make_async_copy(srcs[i].at[:, cols], held[i].at[d], sems.at[d, i])
            copy.start()
            copies.append(copy)
    for d in range(slices):
        for i in range(4):
            copies[4 * d + i].wait()
        for j in range(width):
            cols = slice(j * DH, (j + 1) * DH)
            out_ref[d, 0, j] = dot(v_ref[d, :, cols], k_ref[d, :, cols], TN)
            out_ref[d, 1, j] = dot(o_ref[d, :, cols], q_ref[d, :, cols], TN)


def device_states(half, args, slices, width):
    tokens = args[0].shape[0]
    return call(
        functools.partial(state_kernel, half),
        [pltpu.VMEM((slices, 2, width, DH, DH), F32)] + [pltpu.VMEM((slices, tokens, width * DH), BF16)] * 4,
        args,
        specs=[HBM] * 4,
        scratch=[pltpu.SemaphoreType.DMA((slices, 4))],
        flops=4 * slices * width * tokens * DH * DH,
    )


def local_kernel(half, slices, lots, scale_ref, q_ref, k_ref, v_ref, o_ref, out_ref):
    tokens = q_ref.shape[1]
    width = q_ref.shape[2] // DH
    blocks = tokens // BLOCK
    rows = lax.broadcasted_iota(jnp.int32, (BLOCK, BLOCK), 0)
    cols = lax.broadcasted_iota(jnp.int32, (BLOCK, BLOCK), 1)

    def blk(n, m=None):
        return slice(n * BLOCK, (n + 1 if m is None else m) * BLOCK)

    def product(left, right, weight, values, n, low, high, mask):
        raw = dot(left[blk(n)], right[blk(low, high)], NT)
        parts, rest = [], []
        for m in range(low, high):
            part = raw[:, blk(m - low)]
            if m == n:
                parts.append(jnp.where(mask, part * weight(0), 0.0).astype(BF16))
            else:
                hi, lo = split(part * weight((m ^ n).bit_length()))
                parts.append(hi)
                rest.append((m, lo))
        out = dot(jnp.concatenate(parts, axis=1) if len(parts) > 1 else parts[0], values[blk(low, high)])
        for m, lo in rest:
            out = out + dot(lo, values[blk(m)])
        return out

    for i, d in enumerate(lots):
        first = column(half, d, slices, width) // DH
        for j in range(width):
            at = slice(j * DH, (j + 1) * DH)
            q, k, v, o = q_ref[d, :, at], k_ref[d, :, at], v_ref[d, :, at], o_ref[d, :, at]

            def weight(level, head=first + j):
                return scale_ref[head, level]

            for n in range(blocks):
                out_ref[i, 2, blk(n), at] = product(k, q, weight, o, n, n, blocks, rows <= cols)
                out_ref[i, 1, blk(n), at] = product(v, o, weight, q, n, n, blocks, rows <= cols)
                out_ref[i, 0, blk(n), at] = product(o, v, weight, k, n, 0, n + 1, rows >= cols)


def local_grads(half, lots, level_scale, held, slices):
    tokens, model = held[0].shape[1:]
    return call(
        functools.partial(local_kernel, half, slices, lots),
        [pltpu.VMEM((len(lots), 3, tokens, model), F32)],
        [level_scale, *held],
        specs=[SMEM] + [VMEM] * 4,
        flops=24 * tokens * BLOCK * len(lots) * model,
    )[0]


def chip_kernel(own_ref, other_ref, keep_ref, *out_refs):
    keep_ref[...] = own_ref[0] + other_ref[0]
    for d, out_ref in enumerate(out_refs, 1):
        pack(out_ref, [own_ref[d, t] + other_ref[d, t] for t in range(2)])


def bit_of(value, index):
    return ((value >> index) & 1).astype(F32)


def head_weight(scale_ref, d, slices, width, j, level):
    return scale_ref[column(0, d, slices, width) // DH + j, level]


def plane_kernel(plane_bits, base, rest, scale_ref, keep_ref, *refs):
    slices = 1 << plane_bits
    parts = refs[: slices - 1]
    near_ref, total_ref = refs[slices - 1], refs[slices]
    outs = refs[slices + 1 :]
    width = keep_ref.shape[1]
    place = lax.axis_index("seq") & (slices - 1)
    got = [[keep_ref[0], keep_ref[1]]] + [unpack(p, (width, DH, DH), 2) for p in parts]
    for t in range(2):
        total_ref[t] = functools.reduce(jnp.add, [g[t] for g in got])
    for j in range(width):
        weights = [head_weight(scale_ref, 0, slices, width, j, base + b) for b in range(plane_bits)]
        for d in range(slices):
            early = jnp.zeros((DH, DH), F32)
            late = jnp.zeros((DH, DH), F32)
            for b in range(plane_bits):
                group = [e for e in range(slices) if (d ^ e).bit_length() == b + 1]
                up = bit_of(place ^ d, b)
                early = early + (up * weights[b]) * functools.reduce(jnp.add, [got[e][0][j] for e in group])
                late = late + ((1.0 - up) * weights[b]) * functools.reduce(jnp.add, [got[e][1][j] for e in group])
            near_ref[d, 0, j] = early
            near_ref[d, 1, j] = late
    far_out(outs, total_ref, rest, slices)


def far_out(outs, total_ref, rest, slices):
    row = lax.axis_index("seq") // slices
    for i, out_ref in enumerate(outs):
        up = bit_of(row, rest - len(outs) + i)
        pack(out_ref, [jnp.where(up > 0, total_ref[1], total_ref[0])])


def merge_kernel(slices, index, level, rest, scale_ref, near_ref, total_ref, got_ref, near_out, total_out, *outs):
    width = total_ref.shape[1]
    row = lax.axis_index("seq") // slices
    up = bit_of(row, index)
    got = unpack(got_ref, (width, DH, DH), 2)
    for j in range(width):
        weight = head_weight(scale_ref, 0, slices, width, j, level)
        for d in range(slices):
            near_out[d, 0, j] = near_ref[d, 0, j] + (up * weight) * got[0][j]
            near_out[d, 1, j] = near_ref[d, 1, j] + ((1.0 - up) * weight) * got[1][j]
    for t in range(2):
        total_out[t] = total_ref[t] + got[t]
    far_out(outs, total_out, rest, slices)


def back_kernel(slices, levels, bits, scale_ref, near_ref, *refs):
    count = len(levels)
    gots, (keep_ref, *outs) = refs[:count], refs[count:]
    width = near_ref.shape[2]
    row = lax.axis_index("seq") // slices
    early = [jnp.zeros((DH, DH), F32)] * width
    late = [jnp.zeros((DH, DH), F32)] * width
    for got_ref, level, bit in zip(gots, levels, bits):
        up = bit_of(row, bit)
        (got,) = unpack(got_ref, (width, DH, DH), 1)
        for j in range(width):
            weight = head_weight(scale_ref, 0, slices, width, j, level)
            early[j] = early[j] + (up * weight) * got[j]
            late[j] = late[j] + ((1.0 - up) * weight) * got[j]
    far = (jnp.stack(early), jnp.stack(late))
    for t in range(2):
        keep_ref[t] = near_ref[0, t] + far[t]
    for d, out_ref in enumerate(outs, 1):
        pack(out_ref, [near_ref[d, t] + far[t] for t in range(2)])


def core_kernel(level, scale_ref, own_ref, other_ref, keep_ref, *refs):
    parts, (mine_ref, theirs_ref) = refs[:-2], refs[-2:]
    slices, _, width = own_ref.shape[:3]
    second = lax.axis_index("head").astype(F32)
    for d in range(slices):
        got = [keep_ref[0], keep_ref[1]] if d == 0 else unpack(parts[d - 1], (width, DH, DH), 2)
        for j in range(width):
            weight = head_weight(scale_ref, d, slices, width, j, level)
            high, low = second * weight, (1.0 - second) * weight
            mine_ref[d, 0, j] = got[0][j] + high * other_ref[d, 0, j]
            mine_ref[d, 1, j] = got[1][j] + low * other_ref[d, 1, j]
            theirs_ref[d, 0, j] = got[0][j] + low * own_ref[d, 0, j]
            theirs_ref[d, 1, j] = got[1][j] + high * own_ref[d, 1, j]


def cross_kernel(where, state_refs, held_refs, local_refs, outs, temps, sems):
    slices, _, width = state_refs[0].shape[:3]
    copies = []
    for half in range(2):
        k_ref, v_ref, o_ref = held_refs[half]
        for d in range(slices):
            part, index = where[half, d]
            for j in range(width):
                cs = slice(j * DH, (j + 1) * DH)
                o, v, k = o_ref[d, :, cs], v_ref[d, :, cs], k_ref[d, :, cs]
                hi, lo = split(state_refs[half][d, 0, j])
                qg = dot(o, hi) + dot(o, lo)
                hi, lo = split(state_refs[half][d, 1, j])
                kg = dot(v, hi) + dot(v, lo)
                vg = dot(k, hi, NT) + dot(k, lo, NT)
                for i, cross in enumerate((qg, kg, vg)):
                    temps[half, d, i, :, cs] = (cross + local_refs[part][index, i, :, cs]).astype(BF16)
            cols = pl.ds(column(half, d, slices, width), width * DH)
            for i in range(3):
                copy = pltpu.make_async_copy(temps.at[half, d, i], outs[i].at[:, cols], sems.at[half * slices + d, i])
                copy.start()
                copies.append(copy)
    for copy in copies:
        copy.wait()


def finish(states, held, local, model):
    slices, tokens, cols = held[0][0].shape
    where, parts = {}, []
    for half, lots, part in local:
        for index, d in enumerate(lots):
            where[half, d] = (len(parts), index)
        parts.append(part)

    def kernel(*refs):
        count = 8 + len(parts)
        ins, (o0, o1, o2, temps, sems) = refs[:count], refs[count:]
        cross_kernel(where, ins[:2], (ins[2:5], ins[5:8]), ins[8:], (o0, o1, o2), temps, sems)

    return call(
        kernel,
        [jax.ShapeDtypeStruct((tokens, model), BF16)] * 3,
        [*states, *held[0][1:], *held[1][1:], *parts],
        out_specs=[HBM] * 3,
        scratch=[pltpu.VMEM((2, slices, 3, tokens, cols), BF16), pltpu.SemaphoreType.DMA((2 * slices, 3))],
        flops=12 * tokens * DH * model,
        limit=6,
    )


def work(queries, key_rows, values, out_grad, level_weights):
    level_ids = jnp.arange(level_weights.shape[1], dtype=F32)
    level_scale = level_weights * jnp.exp2((1.0 - level_ids) / 2.0)[None, :] / jnp.sqrt(F32(DH * BLOCK))
    heads = level_weights.shape[0]
    tokens, model = queries.shape
    chain = lax.axis_size("seq")
    bits = chain.bit_length() - 1
    plane_bits = min(2, bits)
    slices = 1 << plane_bits
    width = heads // (lax.axis_size("head") * slices)
    local_levels = (tokens // BLOCK).bit_length() - 1
    base = local_levels + 2
    rest = bits - plane_bits
    direct = min(2, rest)

    args = [pltpu.with_memory_space_constraint(x, pltpu.HBM) for x in (queries, key_rows, values, out_grad)]
    sent, *held_there = device_states(1, args, slices, width)
    other = partner(sent, "head", 1)
    own, *held_here = device_states(0, args, slices, width)
    held = (held_here, held_there)
    local = []
    lots = [(half, lot) for half in range(2) for lot in (range(slices // 2), range(slices // 2, slices)) if lot]
    for half, lot in lots:
        local.append((half, tuple(lot), local_grads(half, tuple(lot), level_scale, held[half], slices)))

    state = pltpu.VMEM((2, width, DH, DH), F32)
    load = pltpu.VMEM((2 * width * DH + EXTRA, DH), F32)
    single = pltpu.VMEM((width * DH + EXTRA, DH), F32)
    near = pltpu.VMEM((slices, 2, width, DH, DH), F32)

    keep, *outs = call(chip_kernel, [state] + [load] * (slices - 1), [own, other])
    got = []
    for d in range(1, slices):
        got.append(narrow(outs[d - 1], "seq", d))
    sending = direct if rest == direct else 0
    near_sum, total, *outs = call(
        functools.partial(plane_kernel, plane_bits, base, rest),
        [near, state] + [single] * sending,
        [level_scale, keep, *got],
        specs=[SMEM] + [VMEM] * slices,
        limit=4,
    )
    for index in range(rest - direct):
        both = call(lambda ref, out: pack(out, [ref[0], ref[1]]), [load], [total])[0]
        arrived = narrow(both, "seq", slices << index)
        sending = direct if index + 1 == rest - direct else 0
        near_sum, total, *outs = call(
            functools.partial(merge_kernel, slices, index, base + plane_bits + index, rest),
            [near, state] + [single] * sending,
            [level_scale, near_sum, total, arrived],
            specs=[SMEM] + [VMEM] * 3,
        )
    got, levels, which = [], [], []
    for step in range(1, 1 << direct):
        top = step.bit_length() - 1
        got.append(narrow(outs[top], "seq", (slices << (rest - direct)) * step))
        which.append(rest - direct + top)
        levels.append(base + plane_bits + rest - direct + top)
    keep, *outs = call(
        functools.partial(back_kernel, slices, levels, which),
        [state] + [load] * (slices - 1),
        [level_scale, near_sum, *got],
        specs=[SMEM] + [VMEM] * (1 + len(got)),
        limit=4,
    )
    got = []
    for d in range(1, slices):
        got.append(narrow(outs[d - 1], "seq", d))
    mine, theirs = call(
        functools.partial(core_kernel, local_levels + 1),
        [near, near],
        [level_scale, own, other, keep, *got],
        specs=[SMEM] + [VMEM] * (3 + len(got)),
        limit=4,
    )
    theirs = partner(theirs, "head", 1)
    return tuple(finish((mine, theirs), held, local, model))


def solution(mesh):
    rows = P(("seq", "head"), None)
    return jax.shard_map(
        work,
        mesh=mesh,
        in_specs=(rows, rows, rows, rows, P()),
        out_specs=(rows, rows, rows),
        check_vma=False,
    )
```

```python
import functools

import jax
import jax.numpy as jnp
from jax import lax
from jax.experimental import pallas as pl
from jax.experimental.pallas import tpu as pltpu
from jax.sharding import PartitionSpec as P

DH = 128
BLOCK = 128
EXTRA = 16
TOP = 14.0
PIECE = 32
F32 = jnp.float32
BF16 = jnp.bfloat16
F16 = jnp.float16
NT = (((1,), (1,)), ((), ()))
TN = (((0,), (0,)), ((), ()))
VMEM = pl.BlockSpec(memory_space=pltpu.VMEM)
SMEM = pl.BlockSpec(memory_space=pltpu.SMEM)
HBM = pl.BlockSpec(memory_space=pltpu.HBM)


def dot(a, b, dims=None):
    if dims is None:
        dims = (((1,), (0,)), ((), ()))
    return lax.dot_general(a, b, dims, preferred_element_type=F32)


def split(x):
    hi = x.astype(BF16)
    return hi, (x - hi.astype(F32)).astype(BF16)


def call(kernel, outs, args, specs=None, out_specs=None, scratch=(), flops=0, limit=2, aliases=None):
    moved = sum(x.size * x.dtype.itemsize for x in args)
    return pl.pallas_call(
        kernel,
        in_specs=specs or [VMEM] * len(args),
        out_specs=out_specs or [VMEM] * len(outs),
        out_shape=list(outs),
        scratch_shapes=list(scratch),
        input_output_aliases=aliases or {},
        compiler_params=pltpu.CompilerParams(vmem_limit_bytes=limit << 20),
        cost_estimate=pl.CostEstimate(flops=flops, bytes_accessed=moved, transcendentals=0),
    )(*args)


def partner(array, axis, distance):
    return lax.ppermute(array, axis, [(i, i ^ distance) for i in range(lax.axis_size(axis))])


def narrow(array, axis, distance):
    return partner(array.astype(F16), axis, distance).astype(F32)


def marks_of(value):
    most = jnp.maximum(jnp.max(jnp.abs(value)), 1e-30)
    return TOP - jnp.ceil(jnp.log2(jnp.full((8, DH), most, F32)))


def pack(out_ref, values):
    rows = 0
    marks = []
    for value in values:
        power = marks_of(value)
        flat = value.reshape(-1, DH)
        out_ref[rows : rows + flat.shape[0]] = flat * jnp.exp2(power)[:1]
        rows += flat.shape[0]
        marks.append(power)
    put_marks(out_ref, marks)


def put_marks(out_ref, marks):
    rows = out_ref.shape[0] - EXTRA
    for i in range(EXTRA // 8):
        out_ref[rows + 8 * i : rows + 8 * i + 8] = marks[min(i, len(marks) - 1)]


def mark(ref, index):
    rows = ref.shape[0] - EXTRA
    return ref[rows + 8 * index : rows + 8 * index + 8]


def bound_power(bound):
    return TOP - jnp.ceil(jnp.log2(jnp.maximum(bound, 1e-30)))


def unpack(ref, shape, count):
    size = (ref.shape[0] - EXTRA) // count
    return [
        (ref[i * size : (i + 1) * size] * jnp.exp2(-mark(ref, i)[:1])).reshape(shape) for i in range(count)
    ]


def pieces(width):
    return [(j, r, slice(r, r + PIECE)) for j in range(width) for r in range(0, DH, PIECE)]


def first_head(half, heads):
    return (lax.axis_index("head") ^ half) * heads


def near_place(slices):
    return lax.axis_index("seq") & (slices - 1)


def state_kernel(half, cuts, *refs):
    srcs, (out_ref, q_ref, k_ref, v_ref, o_ref), sems = refs[:4], refs[4:9], refs[9]
    slices, _, width = out_ref.shape[:3]
    held = (q_ref, k_ref, v_ref, o_ref)
    model = q_ref.shape[1]
    place = near_place(slices)
    size = model // cuts
    copies = []
    for c in range(cuts):
        start = pl.multiple_of(first_head(half, model // DH) * DH + c * size, DH)
        for i in range(4):
            copy = pltpu.make_async_copy(
                srcs[i].at[:, pl.ds(start, size)], held[i].at[:, c * size : (c + 1) * size], sems.at[c, i]
            )
            copy.start()
            copies.append(copy)
    for c in range(cuts):
        for i in range(4):
            copies[4 * c + i].wait()
        for head in range(c * size // DH, (c + 1) * size // DH):
            d, j = place ^ (head // width), head % width
            cols = slice(head * DH, (head + 1) * DH)
            out_ref[d, 0, j] = dot(v_ref[:, cols], k_ref[:, cols], TN)
            out_ref[d, 1, j] = dot(o_ref[:, cols], q_ref[:, cols], TN)


def device_states(half, args, slices, width):
    tokens = args[0].shape[0]
    cuts = 2 if slices % 2 == 0 else 1
    return call(
        functools.partial(state_kernel, half, cuts),
        [pltpu.VMEM((slices, 2, width, DH, DH), F32)] + [pltpu.VMEM((tokens, slices * width * DH), BF16)] * 4,
        args,
        specs=[HBM] * 4,
        scratch=[pltpu.SemaphoreType.DMA((cuts, 4))],
        flops=4 * slices * width * tokens * DH * DH,
    )


def local_kernel(half, group, width, scale_ref, q_ref, k_ref, v_ref, o_ref, out_ref):
    tokens = q_ref.shape[0]
    blocks = tokens // BLOCK
    rows = lax.broadcasted_iota(jnp.int32, (BLOCK, BLOCK), 0)
    cols = lax.broadcasted_iota(jnp.int32, (BLOCK, BLOCK), 1)

    def blk(n, m=None):
        return slice(n * BLOCK, (n + 1 if m is None else m) * BLOCK)

    def product(left, right, weight, values, n, low, high, mask):
        raw = dot(left[blk(n)], right[blk(low, high)], NT)
        parts, rest = [], []
        for m in range(low, high):
            part = raw[:, blk(m - low)]
            if m == n:
                parts.append(jnp.where(mask, part * weight(0), 0.0).astype(BF16))
            else:
                hi, lo = split(part * weight((m ^ n).bit_length()))
                parts.append(hi)
                rest.append((m, lo))
        out = dot(jnp.concatenate(parts, axis=1) if len(parts) > 1 else parts[0], values[blk(low, high)])
        for m, lo in rest:
            out = out + dot(lo, values[blk(m)])
        return out

    for j in range(width):
        at = slice((group * width + j) * DH, (group * width + j + 1) * DH)
        to = slice(j * DH, (j + 1) * DH)
        q, k, v, o = q_ref[:, at], k_ref[:, at], v_ref[:, at], o_ref[:, at]
        head = first_head(half, q_ref.shape[1] // DH) + group * width + j

        def weight(level, head=head):
            return scale_ref[head, level]

        for n in range(blocks):
            out_ref[2, blk(n), to] = product(k, q, weight, o, n, n, blocks, rows <= cols)
            out_ref[1, blk(n), to] = product(v, o, weight, q, n, n, blocks, rows <= cols)
            out_ref[0, blk(n), to] = product(o, v, weight, k, n, 0, n + 1, rows >= cols)


def local_grads(half, group, level_scale, held, width):
    tokens = held[0].shape[0]
    return call(
        functools.partial(local_kernel, half, group, width),
        [pltpu.VMEM((3, tokens, width * DH), F32)],
        [level_scale, *held],
        specs=[SMEM] + [VMEM] * 4,
        flops=24 * tokens * BLOCK * width * DH,
    )[0]


def chip_kernel(own_ref, other_ref, keep_ref, *out_refs):
    rows = (keep_ref.shape[0] - EXTRA) // 2
    marks = []
    for t in range(2):
        value = own_ref[0, t] + other_ref[0, t]
        keep_ref[t * rows : (t + 1) * rows] = value.reshape(rows, DH)
        marks.append(marks_of(value))
    put_marks(keep_ref, marks)
    for d, out_ref in enumerate(out_refs, 1):
        pack(out_ref, [own_ref[d, t] + other_ref[d, t] for t in range(2)])


def bit_of(value, index):
    return ((value >> index) & 1).astype(F32)


def head_weight(scale_ref, place, slices, width, j, level):
    return scale_ref[first_head(0, slices * width) + place * width + j, level]


def top_weight(scale_ref):
    return scale_ref[scale_ref.shape[0] - 1, 0]


def plane_kernel(plane_bits, base, rest, wide, scale_ref, keep_ref, *refs):
    slices = 1 << plane_bits
    parts, refs = (keep_ref, *refs[: slices - 1]), refs[slices - 1 :]
    near_ref, bound_ref, refs = refs[0], refs[1], refs[2:]
    total_ref = refs[0] if wide else None
    outs = refs[1:] if wide else refs
    width = near_ref.shape[2]
    place = near_place(slices)
    row = lax.axis_index("seq") // slices
    factors = [[None if e == 0 else jnp.exp2(-mark(parts[e], t)[:1]) for t in range(2)] for e in range(slices)]
    bounds = [
        functools.reduce(jnp.add, [jnp.exp2(TOP - mark(parts[e], t)) for e in range(slices)]) for t in range(2)
    ]
    for t in range(2):
        bound_ref[8 * t : 8 * t + 8] = bounds[t]
    ups = [bit_of(row, rest - len(outs) + i) for i in range(len(outs))]
    factor_out = []
    for out_ref, up in zip(outs, ups):
        power = bound_power(jnp.where(up > 0, bounds[1], bounds[0]))
        put_marks(out_ref, [power])
        factor_out.append(jnp.exp2(power)[:1])
    sides = [[bit_of(place ^ d, b) for b in range(plane_bits)] for d in range(slices)]
    for j, r, rows in pieces(width):
        weights = [head_weight(scale_ref, place, slices, width, j, base + b) for b in range(plane_bits)]
        values = []
        for t in range(2):
            at = (t * width + j) * DH + r
            loaded = [parts[e][at : at + PIECE] for e in range(slices)]
            loaded = [x if f[t] is None else x * f[t] for x, f in zip(loaded, factors)]
            sums = {}
            for b in range(plane_bits + 1):
                for first in range(0, slices, 1 << b):
                    half = 1 << (b - 1) if b else 0
                    sums[b, first] = loaded[first] if b == 0 else sums[b - 1, first] + sums[b - 1, first + half]
            values.append(sums)
        for d in range(slices):
            early, late = [], []
            for b in range(plane_bits):
                first = ((d >> b) ^ 1) << b
                up = sides[d][b]
                early.append((up * weights[b]) * values[0][b, first])
                late.append(((1.0 - up) * weights[b]) * values[1][b, first])
            zero = jnp.zeros((PIECE, DH), F32)
            near_ref[d, 0, j, rows] = functools.reduce(jnp.add, early) if early else zero
            near_ref[d, 1, j, rows] = functools.reduce(jnp.add, late) if late else zero
        total = [values[t][plane_bits, 0] for t in range(2)]
        for t in range(2):
            if wide:
                total_ref[t, j, rows] = total[t]
        at = j * DH + r
        for out_ref, up, factor in zip(outs, ups, factor_out):
            out_ref[at : at + PIECE] = jnp.where(up > 0, total[1], total[0]) * factor


def far_out(outs, total_ref, rest, slices):
    row = lax.axis_index("seq") // slices
    for i, out_ref in enumerate(outs):
        up = bit_of(row, rest - len(outs) + i)
        pack(out_ref, [jnp.where(up > 0, total_ref[1], total_ref[0])])


def merge_kernel(slices, index, level, rest, scale_ref, near_ref, bound_ref, total_ref, got_ref, near_out, bound_out, total_out, *outs):
    width = total_ref.shape[1]
    row = lax.axis_index("seq") // slices
    place = near_place(slices)
    up = bit_of(row, index)
    got = unpack(got_ref, (width, DH, DH), 2)
    for t in range(2):
        bound_out[8 * t : 8 * t + 8] = bound_ref[8 * t : 8 * t + 8] + jnp.exp2(TOP - mark(got_ref, t))
    for j in range(width):
        weight = head_weight(scale_ref, place, slices, width, j, level)
        for d in range(slices):
            near_out[d, 0, j] = near_ref[d, 0, j] + (up * weight) * got[0][j]
            near_out[d, 1, j] = near_ref[d, 1, j] + ((1.0 - up) * weight) * got[1][j]
    for t in range(2):
        total_out[t] = total_ref[t] + got[t]
    far_out(outs, total_out, rest, slices)


def back_kernel(slices, levels, bits, scale_ref, near_ref, bound_ref, *refs):
    count = len(levels)
    gots, (keep_ref, *outs) = refs[:count], refs[count:]
    width = near_ref.shape[2]
    row = lax.axis_index("seq") // slices
    place = near_place(slices)
    ups = [bit_of(row, bit) for bit in bits]
    bounds = [bound_ref[:8], bound_ref[8:]]
    for got_ref, up in zip(gots, ups):
        size = jnp.exp2(TOP - mark(got_ref, 0))
        bounds = [bounds[0] + up * size, bounds[1] + (1.0 - up) * size]
    powers = [bound_power(top_weight(scale_ref) * bound) for bound in bounds]
    factors = [jnp.exp2(power)[:1] for power in powers]
    for out_ref in (keep_ref, *outs):
        put_marks(out_ref, powers)
    opened = [jnp.exp2(-mark(got_ref, 0)[:1]) for got_ref in gots]
    for j, r, rows in pieces(width):
        far = [jnp.zeros((PIECE, DH), F32)] * 2
        at = j * DH + r
        for got_ref, level, up, factor in zip(gots, levels, ups, opened):
            weight = head_weight(scale_ref, place, slices, width, j, level)
            got = got_ref[at : at + PIECE] * factor
            far = [far[0] + (up * weight) * got, far[1] + ((1.0 - up) * weight) * got]
        for d, out_ref in enumerate((keep_ref, *outs)):
            for t in range(2):
                value = near_ref[d, t, j, rows] + far[t]
                to = t * width * DH + at
                out_ref[to : to + PIECE] = value if d == 0 else value * factors[t]


def core_kernel(level, mine, scale_ref, source_ref, keep_ref, *refs):
    parts, out_ref = (keep_ref, *refs[:-1]), refs[-1]
    slices, _, width = source_ref.shape[:3]
    place = near_place(slices)
    second = lax.axis_index("head").astype(F32)
    sides = (second, 1.0 - second) if mine else (1.0 - second, second)
    for d in range(slices):
        factors = [None if d == 0 else jnp.exp2(-mark(parts[d], t)[:1]) for t in range(2)]
        for j, r, rows in pieces(width):
            weight = head_weight(scale_ref, place ^ d, slices, width, j, level)
            for t in range(2):
                at = (t * width + j) * DH + r
                got = parts[d][at : at + PIECE]
                if d:
                    got = got * factors[t]
                out_ref[d, t, j, rows] = got + (sides[t] * weight) * source_ref[d, t, j, rows]


def cross_kernel(half, cuts, state_ref, k_ref, v_ref, o_ref, local_refs, outs, temps, sems):
    slices, _, width = state_ref.shape[:3]
    model = k_ref.shape[1]
    place = near_place(slices)
    size = model // cuts
    copies = []
    for c in range(cuts):
        for head in range(c * size // DH, (c + 1) * size // DH):
            group, j = head // width, head % width
            d = place ^ group
            cs = slice(head * DH, (head + 1) * DH)
            to = slice(j * DH, (j + 1) * DH)
            o, v, k = o_ref[:, cs], v_ref[:, cs], k_ref[:, cs]
            hi, lo = split(state_ref[d, 0, j])
            qg = dot(o, hi) + dot(o, lo)
            hi, lo = split(state_ref[d, 1, j])
            kg = dot(v, hi) + dot(v, lo)
            vg = dot(k, hi, NT) + dot(k, lo, NT)
            for i, cross in enumerate((qg, kg, vg)):
                temps[i, :, cs] = (cross + local_refs[group][i, :, to]).astype(BF16)
        cs = slice(c * size, (c + 1) * size)
        cols = pl.ds(pl.multiple_of(first_head(half, model // DH) * DH + c * size, DH), size)
        for i in range(3):
            copy = pltpu.make_async_copy(temps.at[i, :, cs], outs[i].at[:, cols], sems.at[c, i])
            copy.start()
            copies.append(copy)
    for copy in copies:
        copy.wait()


def finish(half, states, held, local, model, before):
    tokens, cols = held[0].shape
    slices = states.shape[0]
    cuts = 2 if slices % 2 == 0 else 1
    args = [states, *held[1:], *local]
    specs = [VMEM] * len(args) + [HBM] * len(before)

    def kernel(*refs):
        parts = refs[4 : len(args)]
        outs = refs[len(specs) : len(specs) + 3]
        cross_kernel(half, cuts, *refs[:4], parts, outs, refs[-2], refs[-1])

    return call(
        kernel,
        [jax.ShapeDtypeStruct((tokens, model), BF16)] * 3,
        args + list(before),
        specs=specs,
        out_specs=[HBM] * 3,
        scratch=[pltpu.VMEM((3, tokens, cols), BF16), pltpu.SemaphoreType.DMA((cuts, 3))],
        flops=12 * tokens * DH * cols,
        limit=4,
        aliases={len(args) + i: i for i in range(len(before))},
    )


def work(queries, key_rows, values, out_grad, level_weights):
    level_ids = jnp.arange(level_weights.shape[1], dtype=F32)
    level_scale = level_weights * jnp.exp2((1.0 - level_ids) / 2.0)[None, :] / jnp.sqrt(F32(DH * BLOCK))
    heads = level_weights.shape[0]
    tokens, model = queries.shape
    chain = lax.axis_size("seq")
    bits = chain.bit_length() - 1
    plane_bits = min(2, bits)
    slices = 1 << plane_bits
    width = heads // (lax.axis_size("head") * slices)
    local_levels = (tokens // BLOCK).bit_length() - 1
    base = local_levels + 2
    rest = bits - plane_bits
    direct = min(2, rest)

    most = jnp.full((1, level_scale.shape[1]), jnp.max(jnp.abs(level_scale)))
    level_scale = jnp.concatenate([level_scale, most])

    args = [pltpu.with_memory_space_constraint(x, pltpu.HBM) for x in (queries, key_rows, values, out_grad)]
    sent, *held_there = device_states(1, args, slices, width)
    other = partner(sent, "head", 1)
    own, *held_here = device_states(0, args, slices, width)
    held = (held_here, held_there)
    local = [[], []]
    for half in range(2):
        for group in range(slices):
            local[half].append(local_grads(half, group, level_scale, held[half], width))

    state = pltpu.VMEM((2, width, DH, DH), F32)
    load = pltpu.VMEM((2 * width * DH + EXTRA, DH), F32)
    single = pltpu.VMEM((width * DH + EXTRA, DH), F32)
    near = pltpu.VMEM((slices, 2, width, DH, DH), F32)
    bound = pltpu.VMEM((16, DH), F32)

    keep, *outs = call(chip_kernel, [load] * slices, [own, other])
    got = []
    for d in range(1, slices):
        got.append(narrow(outs[d - 1], "seq", d))
    wide = rest > direct
    near_sum, bounds, *outs = call(
        functools.partial(plane_kernel, plane_bits, base, rest, wide),
        [near, bound] + ([state] if wide else [single] * direct),
        [level_scale, keep, *got],
        specs=[SMEM] + [VMEM] * slices,
    )
    total = outs[0] if wide else None
    for index in range(rest - direct):
        both = call(lambda ref, out: pack(out, [ref[0], ref[1]]), [load], [total])[0]
        arrived = narrow(both, "seq", slices << index)
        sending = direct if index + 1 == rest - direct else 0
        near_sum, bounds, total, *outs = call(
            functools.partial(merge_kernel, slices, index, base + plane_bits + index, rest),
            [near, bound, state] + [single] * sending,
            [level_scale, near_sum, bounds, total, arrived],
            specs=[SMEM] + [VMEM] * 4,
        )
    got, levels, which = [], [], []
    for step in range(1, 1 << direct):
        top = step.bit_length() - 1
        got.append(narrow(outs[top], "seq", (slices << (rest - direct)) * step))
        which.append(rest - direct + top)
        levels.append(base + plane_bits + rest - direct + top)
    keep, *outs = call(
        functools.partial(back_kernel, slices, levels, which),
        [load] * slices,
        [level_scale, near_sum, bounds, *got],
        specs=[SMEM] + [VMEM] * (2 + len(got)),
    )
    got = []
    for d in range(1, slices):
        got.append(narrow(outs[d - 1], "seq", d))
    gathered = []
    for mine, source in ((False, own), (True, other)):
        gathered += call(
            functools.partial(core_kernel, local_levels + 1, mine),
            [near],
            [level_scale, source, keep, *got],
            specs=[SMEM] + [VMEM] * (2 + len(got)),
        )
    theirs = partner(gathered[0], "head", 1)
    half_done = finish(0, gathered[1], held[0], local[0], model, [])
    return tuple(finish(1, theirs, held[1], local[1], model, half_done))


def solution(mesh):
    rows = P(("seq", "head"), None)
    return jax.shard_map(
        work,
        mesh=mesh,
        in_specs=(rows, rows, rows, rows, P()),
        out_specs=(rows, rows, rows),
        check_vma=False,
    )
```

```python
import functools

import jax
import jax.numpy as jnp
from jax import lax
from jax.experimental import pallas as pl
from jax.experimental.pallas import tpu as pltpu
from jax.sharding import PartitionSpec as P

DH = 128
BLOCK = 128
EXTRA = 16
TOP = 14.0
PIECE = 32
F32 = jnp.float32
BF16 = jnp.bfloat16
F16 = jnp.float16
NT = (((1,), (1,)), ((), ()))
TN = (((0,), (0,)), ((), ()))
VMEM = pl.BlockSpec(memory_space=pltpu.VMEM)
HBM = pl.BlockSpec(memory_space=pltpu.HBM)


def dot(a, b, dims=None):
    if dims is None:
        dims = (((1,), (0,)), ((), ()))
    return lax.dot_general(a, b, dims, preferred_element_type=F32)


def split(x):
    hi = x.astype(BF16)
    return hi, (x - hi.astype(F32)).astype(BF16)


def call(kernel, outs, args, specs=None, out_specs=None, scratch=(), flops=0, limit=2, aliases=None):
    moved = sum(x.size * x.dtype.itemsize for x in args)
    return pl.pallas_call(
        kernel,
        in_specs=specs or [VMEM] * len(args),
        out_specs=out_specs or [VMEM] * len(outs),
        out_shape=list(outs),
        scratch_shapes=list(scratch),
        input_output_aliases=aliases or {},
        compiler_params=pltpu.CompilerParams(vmem_limit_bytes=limit << 20),
        cost_estimate=pl.CostEstimate(flops=flops, bytes_accessed=moved, transcendentals=0),
    )(*args)


def partner(array, axis, distance):
    return lax.ppermute(array, axis, [(i, i ^ distance) for i in range(lax.axis_size(axis))])


def narrow(array, axis, distance):
    return partner(array.astype(F16), axis, distance).astype(F32)


def marks_of(value):
    most = jnp.maximum(jnp.max(jnp.abs(value)), 1e-30)
    return TOP - jnp.ceil(jnp.log2(jnp.full((8, DH), most, F32)))


def pack(out_ref, values):
    rows = 0
    marks = []
    for value in values:
        power = marks_of(value)
        flat = value.reshape(-1, DH)
        out_ref[rows : rows + flat.shape[0]] = flat * jnp.exp2(power)[:1]
        rows += flat.shape[0]
        marks.append(power)
    put_marks(out_ref, marks)


def put_marks(out_ref, marks):
    rows = out_ref.shape[0] - EXTRA
    for i in range(EXTRA // 8):
        out_ref[rows + 8 * i : rows + 8 * i + 8] = marks[min(i, len(marks) - 1)]


def mark(ref, index):
    rows = ref.shape[0] - EXTRA
    return ref[rows + 8 * index : rows + 8 * index + 8]


def bound_power(bound):
    return TOP - jnp.ceil(jnp.log2(jnp.maximum(bound, 1e-30)))


def unpack(ref, shape, count):
    size = (ref.shape[0] - EXTRA) // count
    return [
        (ref[i * size : (i + 1) * size] * jnp.exp2(-mark(ref, i)[:1])).reshape(shape) for i in range(count)
    ]


def pieces(width):
    return [(j, r, slice(r, r + PIECE)) for j in range(width) for r in range(0, DH, PIECE)]


def first_head(half, heads):
    return (lax.axis_index("head") ^ half) * heads


def near_place(slices):
    return lax.axis_index("seq") & (slices - 1)


def state_kernel(half, cuts, *refs):
    srcs, (out_ref, q_ref, k_ref, v_ref, o_ref), sems = refs[:4], refs[4:9], refs[9]
    slices, _, width = out_ref.shape[:3]
    held = (q_ref, k_ref, v_ref, o_ref)
    model = q_ref.shape[1]
    place = near_place(slices)
    size = model // cuts
    copies = []
    for c in range(cuts):
        start = pl.multiple_of(first_head(half, model // DH) * DH + c * size, DH)
        for i in range(4):
            copy = pltpu.make_async_copy(
                srcs[i].at[:, pl.ds(start, size)], held[i].at[:, c * size : (c + 1) * size], sems.at[c, i]
            )
            copy.start()
            copies.append(copy)
    for c in range(cuts):
        for i in range(4):
            copies[4 * c + i].wait()
        for head in range(c * size // DH, (c + 1) * size // DH):
            d, j = place ^ (head // width), head % width
            cols = slice(head * DH, (head + 1) * DH)
            out_ref[d, 0, j] = dot(v_ref[:, cols], k_ref[:, cols], TN)
            out_ref[d, 1, j] = dot(o_ref[:, cols], q_ref[:, cols], TN)


def device_states(half, args, slices, width):
    tokens = args[0].shape[0]
    cuts = 2 if slices % 2 == 0 else 1
    return call(
        functools.partial(state_kernel, half, cuts),
        [pltpu.VMEM((slices, 2, width, DH, DH), F32)] + [pltpu.VMEM((tokens, slices * width * DH), BF16)] * 4,
        args,
        specs=[HBM] * 4,
        scratch=[pltpu.SemaphoreType.DMA((cuts, 4))],
        flops=4 * slices * width * tokens * DH * DH,
    )


def local_kernel(lot, width, scale_ref, *refs):
    held, out_ref = (refs[:4], refs[4:8]), refs[8]
    tokens, model = refs[0].shape
    blocks = tokens // BLOCK
    rows = lax.broadcasted_iota(jnp.int32, (BLOCK, BLOCK), 0)
    cols = lax.broadcasted_iota(jnp.int32, (BLOCK, BLOCK), 1)

    def blk(n, m=None):
        return slice(n * BLOCK, (n + 1 if m is None else m) * BLOCK)

    def product(left, right, weight, values, n, low, high, mask):
        raw = dot(left[blk(n)], right[blk(low, high)], NT)
        parts, rest = [], []
        for m in range(low, high):
            part = raw[:, blk(m - low)]
            if m == n:
                parts.append(jnp.where(mask, part * weight(0), 0.0).astype(BF16))
            else:
                hi, lo = split(part * weight((m ^ n).bit_length()))
                parts.append(hi)
                rest.append((m, lo))
        out = dot(jnp.concatenate(parts, axis=1) if len(parts) > 1 else parts[0], values[blk(low, high)])
        for m, lo in rest:
            out = out + dot(lo, values[blk(m)])
        return out

    place = near_place(model // (width * DH))
    for index, (half, d) in enumerate(lot):
        group = place ^ d
        for j in range(width):
            at = pl.ds(pl.multiple_of((group * width + j) * DH, DH), DH)
            to = slice(j * DH, (j + 1) * DH)
            q, k, v, o = (ref[:, at] for ref in held[half])
            head = first_head(half, model // DH) + group * width + j

            def weight(level, head=head):
                return scale_ref[head, level : level + 1]

            for n in range(blocks):
                out_ref[index, 2, blk(n), to] = product(k, q, weight, o, n, n, blocks, rows <= cols)
                out_ref[index, 1, blk(n), to] = product(v, o, weight, q, n, n, blocks, rows <= cols)
                out_ref[index, 0, blk(n), to] = product(o, v, weight, k, n, 0, n + 1, rows >= cols)


def local_grads(lot, scales, held, width):
    tokens = held[0][0].shape[0]
    return call(
        functools.partial(local_kernel, lot, width),
        [pltpu.VMEM((len(lot), 3, tokens, width * DH), F32)],
        [scales, *held[0], *held[1]],
        flops=24 * tokens * BLOCK * width * DH * len(lot),
    )[0]


def chip_kernel(own_ref, other_ref, keep_ref, *out_refs):
    rows = (keep_ref.shape[0] - EXTRA) // 2
    marks = []
    for t in range(2):
        value = own_ref[0, t] + other_ref[0, t]
        keep_ref[t * rows : (t + 1) * rows] = value.reshape(rows, DH)
        marks.append(marks_of(value))
    put_marks(keep_ref, marks)
    for d, out_ref in enumerate(out_refs, 1):
        pack(out_ref, [own_ref[d, t] + other_ref[d, t] for t in range(2)])


def bit_of(value, index):
    return ((value >> index) & 1).astype(F32)


def head_weight(scale_ref, place, slices, width, j, level):
    return scale_ref[first_head(0, slices * width) + place * width + j, level : level + 1]


def plane_kernel(plane_bits, base, rest, wide, scale_ref, keep_ref, *refs):
    slices = 1 << plane_bits
    parts, refs = (keep_ref, *refs[: slices - 1]), refs[slices - 1 :]
    near_ref, bound_ref, refs = refs[0], refs[1], refs[2:]
    total_ref = refs[0] if wide else None
    outs = refs[1:] if wide else refs
    width = near_ref.shape[2]
    place = near_place(slices)
    row = lax.axis_index("seq") // slices
    factors = [[None if e == 0 else jnp.exp2(-mark(parts[e], t)[:1]) for t in range(2)] for e in range(slices)]
    bounds = [
        functools.reduce(jnp.add, [jnp.exp2(TOP - mark(parts[e], t)) for e in range(slices)]) for t in range(2)
    ]
    for t in range(2):
        bound_ref[8 * t : 8 * t + 8] = bounds[t]
    ups = [bit_of(row, rest - len(outs) + i) for i in range(len(outs))]
    factor_out = []
    for out_ref, up in zip(outs, ups):
        power = bound_power(jnp.where(up > 0, bounds[1], bounds[0]))
        put_marks(out_ref, [power])
        factor_out.append(jnp.exp2(power)[:1])
    sides = [[bit_of(place ^ d, b) for b in range(plane_bits)] for d in range(slices)]
    for j, r, rows in pieces(width):
        weights = [head_weight(scale_ref, place, slices, width, j, base + b) for b in range(plane_bits)]
        values = []
        for t in range(2):
            at = (t * width + j) * DH + r
            loaded = [parts[e][at : at + PIECE] for e in range(slices)]
            loaded = [x if f[t] is None else x * f[t] for x, f in zip(loaded, factors)]
            sums = {}
            for b in range(plane_bits + 1):
                for first in range(0, slices, 1 << b):
                    half = 1 << (b - 1) if b else 0
                    sums[b, first] = loaded[first] if b == 0 else sums[b - 1, first] + sums[b - 1, first + half]
            values.append(sums)
        for d in range(slices):
            early, late = [], []
            for b in range(plane_bits):
                first = ((d >> b) ^ 1) << b
                up = sides[d][b]
                early.append((up * weights[b]) * values[0][b, first])
                late.append(((1.0 - up) * weights[b]) * values[1][b, first])
            zero = jnp.zeros((PIECE, DH), F32)
            near_ref[d, 0, j, rows] = functools.reduce(jnp.add, early) if early else zero
            near_ref[d, 1, j, rows] = functools.reduce(jnp.add, late) if late else zero
        total = [values[t][plane_bits, 0] for t in range(2)]
        for t in range(2):
            if wide:
                total_ref[t, j, rows] = total[t]
        at = j * DH + r
        for out_ref, up, factor in zip(outs, ups, factor_out):
            out_ref[at : at + PIECE] = jnp.where(up > 0, total[1], total[0]) * factor


def far_out(outs, total_ref, rest, slices):
    row = lax.axis_index("seq") // slices
    for i, out_ref in enumerate(outs):
        up = bit_of(row, rest - len(outs) + i)
        pack(out_ref, [jnp.where(up > 0, total_ref[1], total_ref[0])])


def merge_kernel(slices, index, level, rest, scale_ref, near_ref, bound_ref, total_ref, got_ref, near_out, bound_out, total_out, *outs):
    width = total_ref.shape[1]
    row = lax.axis_index("seq") // slices
    place = near_place(slices)
    up = bit_of(row, index)
    got = unpack(got_ref, (width, DH, DH), 2)
    for t in range(2):
        bound_out[8 * t : 8 * t + 8] = bound_ref[8 * t : 8 * t + 8] + jnp.exp2(TOP - mark(got_ref, t))
    for j in range(width):
        weight = head_weight(scale_ref, place, slices, width, j, level)
        for d in range(slices):
            near_out[d, 0, j] = near_ref[d, 0, j] + (up * weight) * got[0][j]
            near_out[d, 1, j] = near_ref[d, 1, j] + ((1.0 - up) * weight) * got[1][j]
    for t in range(2):
        total_out[t] = total_ref[t] + got[t]
    far_out(outs, total_out, rest, slices)


def back_kernel(slices, levels, bits, scale_ref, near_ref, bound_ref, *refs):
    count = len(levels)
    gots, (keep_ref, *outs) = refs[:count], refs[count:]
    width = near_ref.shape[2]
    row = lax.axis_index("seq") // slices
    place = near_place(slices)
    ups = [bit_of(row, bit) for bit in bits]
    bounds = [bound_ref[:8], bound_ref[8:]]
    for got_ref, up in zip(gots, ups):
        size = jnp.exp2(TOP - mark(got_ref, 0))
        bounds = [bounds[0] + up * size, bounds[1] + (1.0 - up) * size]
    head = first_head(0, scale_ref.shape[0] // lax.axis_size("head")) + place * width
    most = functools.reduce(jnp.maximum, [jnp.abs(scale_ref[head + j]) for j in range(width)])
    most = jnp.max(most, axis=0, keepdims=True)
    powers = [bound_power(most * bound) for bound in bounds]
    factors = [jnp.exp2(power)[:1] for power in powers]
    for out_ref in (keep_ref, *outs):
        put_marks(out_ref, powers)
    opened = [jnp.exp2(-mark(got_ref, 0)[:1]) for got_ref in gots]
    for j, r, rows in pieces(width):
        far = [jnp.zeros((PIECE, DH), F32)] * 2
        at = j * DH + r
        for got_ref, level, up, factor in zip(gots, levels, ups, opened):
            weight = head_weight(scale_ref, place, slices, width, j, level)
            got = got_ref[at : at + PIECE] * factor
            far = [far[0] + (up * weight) * got, far[1] + ((1.0 - up) * weight) * got]
        for d, out_ref in enumerate((keep_ref, *outs)):
            for t in range(2):
                value = near_ref[d, t, j, rows] + far[t]
                to = t * width * DH + at
                out_ref[to : to + PIECE] = value if d == 0 else value * factors[t]


def core_side(mine):
    second = lax.axis_index("head").astype(F32)
    return (second, 1.0 - second) if mine else (1.0 - second, second)


def core_kernel(level, scale_ref, source_ref, keep_ref, *refs):
    parts, out_ref = (keep_ref, *refs[:-1]), refs[-1]
    slices, _, width = source_ref.shape[:3]
    place = near_place(slices)
    sides = core_side(False)
    for d in range(slices):
        factors = [None if d == 0 else jnp.exp2(-mark(parts[d], t)[:1]) for t in range(2)]
        for j, r, rows in pieces(width):
            weight = head_weight(scale_ref, place ^ d, slices, width, j, level)
            for t in range(2):
                at = (t * width + j) * DH + r
                got = parts[d][at : at + PIECE]
                if d:
                    got = got * factors[t]
                out_ref[d, t, j, rows] = got + (sides[t] * weight) * source_ref[d, t, j, rows]


def cross_kernel(half, states_of, k_ref, v_ref, o_ref, local_of, outs, temps, sems):
    slices, width = temps.shape[0], temps.shape[3] // DH
    model = k_ref.shape[1]
    place = near_place(slices)
    copies = []
    for d in range(slices):
        group = place ^ d
        for j in range(width):
            at = pl.ds(pl.multiple_of((group * width + j) * DH, DH), DH)
            to = slice(j * DH, (j + 1) * DH)
            o, v, k = o_ref[:, at], v_ref[:, at], k_ref[:, at]
            early, late = states_of(d, j)
            hi, lo = split(early)
            qg = dot(o, hi) + dot(o, lo)
            hi, lo = split(late)
            kg = dot(v, hi) + dot(v, lo)
            vg = dot(k, hi, NT) + dot(k, lo, NT)
            for i, cross in enumerate((qg, kg, vg)):
                temps[d, i, :, to] = (cross + local_of(d, i, to)).astype(BF16)
        start = first_head(half, model // DH) * DH + group * (width * DH)
        cols = pl.ds(pl.multiple_of(start, DH), width * DH)
        for i in range(3):
            copy = pltpu.make_async_copy(temps.at[d, i], outs[i].at[:, cols], sems.at[d, i])
            copy.start()
            copies.append(copy)
    for copy in copies:
        copy.wait()


def finish(half, source, held, parts, where, scales, level, model, before):
    tokens, cols = held[0].shape
    slices, _, width = source[0].shape[:3]
    count = len(source)
    args = [*source, scales, *held[1:], *parts]
    specs = [VMEM] * len(args) + [HBM] * len(before)

    def kernel(*refs):
        states, scale_ref, held_refs = refs[:count], refs[count], refs[count + 1 : count + 4]
        local_refs, outs = refs[count + 4 : len(args)], refs[len(specs) : len(specs) + 3]
        place = near_place(slices)
        sides = core_side(True)

        def states_of(d, j):
            if count == 1:
                return [states[0][d, t, j] for t in range(2)]
            weight = head_weight(scale_ref, place ^ d, slices, width, j, level)
            out = []
            for t in range(2):
                ref = states[1 + d]
                got = ref[(t * width + j) * DH : (t * width + j + 1) * DH]
                if d:
                    got = got * jnp.exp2(-mark(ref, t)[:1])
                out.append(got + (sides[t] * weight) * states[0][d, t, j])
            return out

        def local_of(d, i, to):
            part, index = where[half, d]
            return local_refs[part][index, i, :, to]

        cross_kernel(half, states_of, *held_refs, local_of, outs, refs[-2], refs[-1])

    return call(
        kernel,
        [jax.ShapeDtypeStruct((tokens, model), BF16)] * 3,
        args + list(before),
        specs=specs,
        out_specs=[HBM] * 3,
        scratch=[pltpu.VMEM((slices, 3, tokens, width * DH), BF16), pltpu.SemaphoreType.DMA((slices, 3))],
        flops=12 * tokens * DH * cols,
        limit=4,
        aliases={len(args) + i: i for i in range(len(before))},
    )


def work(queries, key_rows, values, out_grad, level_weights):
    level_ids = jnp.arange(level_weights.shape[1], dtype=F32)
    level_scale = level_weights * jnp.exp2((1.0 - level_ids) / 2.0)[None, :] / jnp.sqrt(F32(DH * BLOCK))
    heads = level_weights.shape[0]
    tokens, model = queries.shape
    chain = lax.axis_size("seq")
    bits = chain.bit_length() - 1
    plane_bits = min(2, bits)
    slices = 1 << plane_bits
    width = heads // (lax.axis_size("head") * slices)
    local_levels = (tokens // BLOCK).bit_length() - 1
    base = local_levels + 2
    rest = bits - plane_bits
    direct = min(2, rest)

    padded = jnp.pad(level_scale, ((0, 0), (0, -level_scale.shape[1] % 8)))
    scales = jnp.broadcast_to(padded[:, :, None], (*padded.shape, DH))

    args = [pltpu.with_memory_space_constraint(x, pltpu.HBM) for x in (queries, key_rows, values, out_grad)]
    sent, *held_there = device_states(1, args, slices, width)
    other = partner(sent, "head", 1)
    own, *held_here = device_states(0, args, slices, width)
    held = (held_here, held_there)
    every = [(half, d) for half in range(2) for d in range(slices)]
    ends = [0, 3 * len(every) // 8, 6 * len(every) // 8, len(every)]
    where, local = {}, []
    for low, high in zip(ends, ends[1:]):
        if low == high:
            continue
        for i, key in enumerate(every[low:high]):
            where[key] = (len(local), i)
        local.append(local_grads(tuple(every[low:high]), scales, held, width))

    state = pltpu.VMEM((2, width, DH, DH), F32)
    load = pltpu.VMEM((2 * width * DH + EXTRA, DH), F32)
    single = pltpu.VMEM((width * DH + EXTRA, DH), F32)
    near = pltpu.VMEM((slices, 2, width, DH, DH), F32)
    bound = pltpu.VMEM((16, DH), F32)

    keep, *outs = call(chip_kernel, [load] * slices, [own, other])
    got = []
    for d in range(1, slices):
        got.append(narrow(outs[d - 1], "seq", d))
    wide = rest > direct
    near_sum, bounds, *outs = call(
        functools.partial(plane_kernel, plane_bits, base, rest, wide),
        [near, bound] + ([state] if wide else [single] * direct),
        [scales, keep, *got],
    )
    total = outs[0] if wide else None
    for index in range(rest - direct):
        both = call(lambda ref, out: pack(out, [ref[0], ref[1]]), [load], [total])[0]
        arrived = narrow(both, "seq", slices << index)
        sending = direct if index + 1 == rest - direct else 0
        near_sum, bounds, total, *outs = call(
            functools.partial(merge_kernel, slices, index, base + plane_bits + index, rest),
            [near, bound, state] + [single] * sending,
            [scales, near_sum, bounds, total, arrived],
        )
    got, levels, which = [], [], []
    for step in range(1, 1 << direct):
        top = step.bit_length() - 1
        got.append(narrow(outs[top], "seq", (slices << (rest - direct)) * step))
        which.append(rest - direct + top)
        levels.append(base + plane_bits + rest - direct + top)
    keep, *outs = call(
        functools.partial(back_kernel, slices, levels, which), [load] * slices, [scales, near_sum, bounds, *got]
    )
    got = []
    for d in range(1, slices):
        got.append(narrow(outs[d - 1], "seq", d))
    level = local_levels + 1
    theirs = call(functools.partial(core_kernel, level), [near], [scales, own, keep, *got])[0]
    theirs = partner(theirs, "head", 1)
    half_done = finish(0, [other, keep, *got], held[0], local, where, scales, level, model, [])
    return tuple(finish(1, [theirs], held[1], local, where, scales, level, model, half_done))


def solution(mesh):
    rows = P(("seq", "head"), None)
    return jax.shard_map(
        work,
        mesh=mesh,
        in_specs=(rows, rows, rows, rows, P()),
        out_specs=(rows, rows, rows),
        check_vma=False,
    )
```

```python
import functools

import jax
import jax.numpy as jnp
from jax import lax
from jax.experimental import pallas as pl
from jax.experimental.pallas import tpu as pltpu
from jax.sharding import PartitionSpec as P

DH = 128
BLOCK = 128
EXTRA = 16
TOP = 14.0
PIECE = 32
F32 = jnp.float32
BF16 = jnp.bfloat16
F16 = jnp.float16
NT = (((1,), (1,)), ((), ()))
TN = (((0,), (0,)), ((), ()))
VMEM = pl.BlockSpec(memory_space=pltpu.VMEM)
HBM = pl.BlockSpec(memory_space=pltpu.HBM)


def dot(a, b, dims=None):
    if dims is None:
        dims = (((1,), (0,)), ((), ()))
    return lax.dot_general(a, b, dims, preferred_element_type=F32)


def split(x):
    hi = x.astype(BF16)
    return hi, (x - hi.astype(F32)).astype(BF16)


def call(kernel, outs, args, specs=None, out_specs=None, scratch=(), flops=0, limit=2, aliases=None):
    moved = sum(x.size * x.dtype.itemsize for x in args)
    return pl.pallas_call(
        kernel,
        in_specs=specs or [VMEM] * len(args),
        out_specs=out_specs or [VMEM] * len(outs),
        out_shape=list(outs),
        scratch_shapes=list(scratch),
        input_output_aliases=aliases or {},
        compiler_params=pltpu.CompilerParams(vmem_limit_bytes=limit << 20),
        cost_estimate=pl.CostEstimate(flops=flops, bytes_accessed=moved, transcendentals=0),
    )(*args)


def partner(array, axis, distance):
    return lax.ppermute(array, axis, [(i, i ^ distance) for i in range(lax.axis_size(axis))])


def narrow(array, axis, distance):
    return partner(array.astype(F16), axis, distance).astype(F32)


def marks_of(value):
    most = jnp.maximum(jnp.max(jnp.abs(value)), 1e-30)
    return TOP - jnp.ceil(jnp.log2(jnp.full((8, DH), most, F32)))


def pack(out_ref, values):
    rows = 0
    marks = []
    for value in values:
        power = marks_of(value)
        flat = value.reshape(-1, DH)
        out_ref[rows : rows + flat.shape[0]] = flat * jnp.exp2(power)[:1]
        rows += flat.shape[0]
        marks.append(power)
    put_marks(out_ref, marks)


def put_marks(out_ref, marks):
    rows = out_ref.shape[0] - EXTRA
    for i in range(EXTRA // 8):
        out_ref[rows + 8 * i : rows + 8 * i + 8] = marks[min(i, len(marks) - 1)]


def mark(ref, index):
    rows = ref.shape[0] - EXTRA
    return ref[rows + 8 * index : rows + 8 * index + 8]


def bound_power(bound):
    return TOP - jnp.ceil(jnp.log2(jnp.maximum(bound, 1e-30)))


def unpack(ref, shape, count):
    size = (ref.shape[0] - EXTRA) // count
    return [
        (ref[i * size : (i + 1) * size] * jnp.exp2(-mark(ref, i)[:1])).reshape(shape) for i in range(count)
    ]


def pieces(width):
    return [(j, r, slice(r, r + PIECE)) for j in range(width) for r in range(0, DH, PIECE)]


def first_head(half, heads):
    return (lax.axis_index("head") ^ half) * heads


def near_place(slices):
    return lax.axis_index("seq") & (slices - 1)


def state_kernel(half, slices, cuts, counts, *refs):
    srcs, outs, (mark_ref, q_ref, k_ref, v_ref, o_ref, sems) = refs[:4], refs[4 : 4 + len(counts)], refs[4 + len(counts) :]
    width = outs[0].shape[2]
    held = (q_ref, k_ref, v_ref, o_ref)
    model = q_ref.shape[1]
    place = near_place(slices)
    size = model // cuts
    per = slices // cuts
    copies = {}
    for c in reversed(range(cuts)):
        at = pl.multiple_of((place // per ^ c) * size, DH)
        start = pl.multiple_of(first_head(half, model // DH) * DH + at, DH)
        for i in range(4):
            copies[c, i] = pltpu.make_async_copy(
                srcs[i].at[:, pl.ds(start, size)], held[i].at[:, pl.ds(at, size)], sems.at[c, i]
            )
            copies[c, i].start()
    most = [jnp.zeros((8, DH), F32)] * 2
    for d in reversed(range(slices)):
        if d % per == per - 1:
            for i in range(4):
                copies[d // per, i].wait()
        part = sum(d >= sum(counts[: n + 1]) for n in range(len(counts)))
        index = d - sum(counts[:part])
        for j in range(width):
            cols = pl.ds(pl.multiple_of(((place ^ d) * width + j) * DH, DH), DH)
            pairs = (dot(v_ref[:, cols], k_ref[:, cols], TN), dot(o_ref[:, cols], q_ref[:, cols], TN))
            for t in range(2):
                outs[part][index, t, j] = pairs[t]
                if half == 0:
                    most[t] = jnp.maximum(most[t], jnp.max(jnp.abs(pairs[t]).reshape(-1, 8, DH), axis=0))
    for t in range(2):
        mark_ref[8 * t : 8 * t + 8] = jnp.full((8, DH), jnp.max(most[t]), F32)


def device_states(half, args, slices, width, counts):
    tokens = args[0].shape[0]
    cuts = 2 if slices % 2 == 0 else 1
    return call(
        functools.partial(state_kernel, half, slices, cuts, counts),
        [pltpu.VMEM((n, 2, width, DH, DH), F32) for n in counts]
        + [pltpu.VMEM((16, DH), F32)]
        + [pltpu.VMEM((tokens, slices * width * DH), BF16)] * 4,
        args,
        specs=[HBM] * 4,
        scratch=[pltpu.SemaphoreType.DMA((cuts, 4))],
        flops=4 * slices * width * tokens * DH * DH,
    )


def local_kernel(lot, width, scale_ref, *refs):
    held, out_ref = (refs[:4], refs[4:8]), refs[8]
    tokens, model = refs[0].shape
    blocks = tokens // BLOCK
    rows = lax.broadcasted_iota(jnp.int32, (BLOCK, BLOCK), 0)
    cols = lax.broadcasted_iota(jnp.int32, (BLOCK, BLOCK), 1)

    def blk(n, m=None):
        return slice(n * BLOCK, (n + 1 if m is None else m) * BLOCK)

    def product(left, right, weight, values, n, low, high, mask):
        raw = dot(left[blk(n)], right[blk(low, high)], NT)
        parts, rest = [], []
        for m in range(low, high):
            part = raw[:, blk(m - low)]
            if m == n:
                parts.append(jnp.where(mask, part * weight(0), 0.0).astype(BF16))
            else:
                hi, lo = split(part * weight((m ^ n).bit_length()))
                parts.append(hi)
                rest.append((m, lo))
        out = dot(jnp.concatenate(parts, axis=1) if len(parts) > 1 else parts[0], values[blk(low, high)])
        for m, lo in rest:
            out = out + dot(lo, values[blk(m)])
        return out

    place = near_place(model // (width * DH))
    for index, (half, d) in enumerate(lot):
        group = place ^ d
        for j in range(width):
            at = pl.ds(pl.multiple_of((group * width + j) * DH, DH), DH)
            to = slice(j * DH, (j + 1) * DH)
            q, k, v, o = (ref[:, at] for ref in held[half])
            head = first_head(half, model // DH) + group * width + j

            def weight(level, head=head):
                return scale_ref[head, level : level + 1]

            for n in range(blocks):
                out_ref[index, 2, blk(n), to] = product(k, q, weight, o, n, n, blocks, rows <= cols)
                out_ref[index, 1, blk(n), to] = product(v, o, weight, q, n, n, blocks, rows <= cols)
                out_ref[index, 0, blk(n), to] = product(o, v, weight, k, n, 0, n + 1, rows >= cols)


def local_grads(lot, scales, held, width):
    tokens = held[0][0].shape[0]
    return call(
        functools.partial(local_kernel, lot, width),
        [pltpu.VMEM((len(lot), 3, tokens, width * DH), F32)],
        [scales, *held[0], *held[1]],
        flops=24 * tokens * BLOCK * width * DH * len(lot),
    )[0]


def chip_kernel(first, own_ref, other_ref, *out_refs):
    for index, out_ref in enumerate(out_refs):
        d = first + index
        values = [own_ref[d, t] + other_ref[index, t] for t in range(2)]
        if d:
            pack(out_ref, values)
            continue
        rows = (out_ref.shape[0] - EXTRA) // 2
        for t in range(2):
            out_ref[t * rows : (t + 1) * rows] = values[t].reshape(rows, DH)
        put_marks(out_ref, [marks_of(value) for value in values])


def bit_of(value, index):
    return ((value >> index) & 1).astype(F32)


def head_weight(scale_ref, place, slices, width, j, level):
    return scale_ref[first_head(0, slices * width) + place * width + j, level : level + 1]


def plane_kernel(plane_bits, base, rest, wide, scale_ref, keep_ref, *refs):
    slices = 1 << plane_bits
    parts, refs = (keep_ref, *refs[: slices - 1]), refs[slices - 1 :]
    near_ref, bound_ref, refs = refs[0], refs[1], refs[2:]
    total_ref = refs[0] if wide else None
    outs = refs[1:] if wide else refs
    width = near_ref.shape[2]
    place = near_place(slices)
    row = lax.axis_index("seq") // slices
    factors = [[None if e == 0 else jnp.exp2(-mark(parts[e], t)[:1]) for t in range(2)] for e in range(slices)]
    bounds = [
        functools.reduce(jnp.add, [jnp.exp2(TOP - mark(parts[e], t)) for e in range(slices)]) for t in range(2)
    ]
    for t in range(2):
        bound_ref[8 * t : 8 * t + 8] = bounds[t]
    ups = [bit_of(row, rest - len(outs) + i) for i in range(len(outs))]
    factor_out = []
    for out_ref, up in zip(outs, ups):
        power = bound_power(jnp.where(up > 0, bounds[1], bounds[0]))
        put_marks(out_ref, [power])
        factor_out.append(jnp.exp2(power)[:1])
    sides = [[bit_of(place ^ d, b) for b in range(plane_bits)] for d in range(slices)]
    for j, r, rows in pieces(width):
        weights = [head_weight(scale_ref, place, slices, width, j, base + b) for b in range(plane_bits)]
        values = []
        for t in range(2):
            at = (t * width + j) * DH + r
            loaded = [parts[e][at : at + PIECE] for e in range(slices)]
            loaded = [x if f[t] is None else x * f[t] for x, f in zip(loaded, factors)]
            sums = {}
            for b in range(plane_bits + 1):
                for first in range(0, slices, 1 << b):
                    half = 1 << (b - 1) if b else 0
                    sums[b, first] = loaded[first] if b == 0 else sums[b - 1, first] + sums[b - 1, first + half]
            values.append(sums)
        for d in range(slices):
            early, late = [], []
            for b in range(plane_bits):
                first = ((d >> b) ^ 1) << b
                up = sides[d][b]
                early.append((up * weights[b]) * values[0][b, first])
                late.append(((1.0 - up) * weights[b]) * values[1][b, first])
            zero = jnp.zeros((PIECE, DH), F32)
            near_ref[d, 0, j, rows] = functools.reduce(jnp.add, early) if early else zero
            near_ref[d, 1, j, rows] = functools.reduce(jnp.add, late) if late else zero
        total = [values[t][plane_bits, 0] for t in range(2)]
        for t in range(2):
            if wide:
                total_ref[t, j, rows] = total[t]
        at = j * DH + r
        for out_ref, up, factor in zip(outs, ups, factor_out):
            out_ref[at : at + PIECE] = jnp.where(up > 0, total[1], total[0]) * factor


def far_out(outs, total_ref, rest, slices):
    row = lax.axis_index("seq") // slices
    for i, out_ref in enumerate(outs):
        up = bit_of(row, rest - len(outs) + i)
        pack(out_ref, [jnp.where(up > 0, total_ref[1], total_ref[0])])


def merge_kernel(slices, index, level, rest, scale_ref, near_ref, bound_ref, total_ref, got_ref, near_out, bound_out, total_out, *outs):
    width = total_ref.shape[1]
    row = lax.axis_index("seq") // slices
    place = near_place(slices)
    up = bit_of(row, index)
    got = unpack(got_ref, (width, DH, DH), 2)
    for t in range(2):
        bound_out[8 * t : 8 * t + 8] = bound_ref[8 * t : 8 * t + 8] + jnp.exp2(TOP - mark(got_ref, t))
    for j in range(width):
        weight = head_weight(scale_ref, place, slices, width, j, level)
        for d in range(slices):
            near_out[d, 0, j] = near_ref[d, 0, j] + (up * weight) * got[0][j]
            near_out[d, 1, j] = near_ref[d, 1, j] + ((1.0 - up) * weight) * got[1][j]
    for t in range(2):
        total_out[t] = total_ref[t] + got[t]
    far_out(outs, total_out, rest, slices)


def back_kernel(slices, levels, bits, scale_ref, near_ref, bound_ref, *refs):
    count = len(levels)
    gots, (keep_ref, *outs) = refs[:count], refs[count:]
    width = near_ref.shape[2]
    row = lax.axis_index("seq") // slices
    place = near_place(slices)
    ups = [bit_of(row, bit) for bit in bits]
    bounds = [bound_ref[:8], bound_ref[8:]]
    for got_ref, up in zip(gots, ups):
        size = jnp.exp2(TOP - mark(got_ref, 0))
        bounds = [bounds[0] + up * size, bounds[1] + (1.0 - up) * size]
    head = first_head(0, scale_ref.shape[0] // lax.axis_size("head")) + place * width
    most = functools.reduce(jnp.maximum, [jnp.abs(scale_ref[head + j]) for j in range(width)])
    most = jnp.max(most, axis=0, keepdims=True)
    powers = [bound_power(most * bound) for bound in bounds]
    factors = [jnp.exp2(power)[:1] for power in powers]
    for out_ref in (keep_ref, *outs):
        put_marks(out_ref, powers)
    opened = [jnp.exp2(-mark(got_ref, 0)[:1]) for got_ref in gots]
    for j, r, rows in pieces(width):
        far = [jnp.zeros((PIECE, DH), F32)] * 2
        at = j * DH + r
        for got_ref, level, up, factor in zip(gots, levels, ups, opened):
            weight = head_weight(scale_ref, place, slices, width, j, level)
            got = got_ref[at : at + PIECE] * factor
            far = [far[0] + (up * weight) * got, far[1] + ((1.0 - up) * weight) * got]
        for d, out_ref in enumerate((keep_ref, *outs)):
            for t in range(2):
                value = near_ref[d, t, j, rows] + far[t]
                to = t * width * DH + at
                out_ref[to : to + PIECE] = value if d == 0 else value * factors[t]


def core_side(mine):
    second = lax.axis_index("head").astype(F32)
    return (second, 1.0 - second) if mine else (1.0 - second, second)


def near_core_kernel(level, slices, scale_ref, own_ref, keep_ref, out_ref):
    width = out_ref.shape[1]
    place = near_place(slices)
    sides = core_side(False)
    for j, r, rows in pieces(width):
        weight = head_weight(scale_ref, place, slices, width, j, level)
        for t in range(2):
            at = (t * width + j) * DH + r
            out_ref[t, j, rows] = keep_ref[at : at + PIECE] + (sides[t] * weight) * own_ref[0, t, j, rows]


def core_kernel(level, scale_ref, own_ref, most_ref, *refs):
    parts, out_ref = refs[:-1], refs[-1]
    slices, _, width = own_ref.shape[:3]
    place = near_place(slices)
    sides = core_side(False)
    first = first_head(0, scale_ref.shape[0] // lax.axis_size("head"))
    weights = [jnp.abs(scale_ref[first + h, level : level + 1]) for h in range(slices * width)]
    heaviest = functools.reduce(jnp.maximum, weights)
    powers = []
    for t in range(2):
        bound = functools.reduce(jnp.maximum, [jnp.exp2(TOP - mark(part, t)) for part in parts])
        powers.append(bound_power(bound + heaviest * most_ref[8 * t : 8 * t + 8]))
    put_marks(out_ref, powers)
    for d, part in enumerate(parts, 1):
        for t in range(2):
            opened = jnp.exp2(powers[t][:1] - mark(part, t)[:1])
            closed = sides[t] * jnp.exp2(powers[t][:1])
            for j, r, rows in pieces(width):
                weight = head_weight(scale_ref, place ^ d, slices, width, j, level)
                at = (t * width + j) * DH + r
                to = (((d - 1) * 2 + t) * width + j) * DH + r
                out_ref[to : to + PIECE] = part[at : at + PIECE] * opened + (closed * weight) * own_ref[d, t, j, rows]


def finish(items, kinds, states, held, parts, where, scales, level, model, before):
    tokens, cols = held[0][0].shape
    width = parts[0].shape[3] // DH
    slices = cols // (width * DH)
    halves = sorted({half for half, _ in items})
    args = [*states, scales, *[x for half in halves for x in held[half][1:]], *parts]
    specs = [VMEM] * len(args) + [HBM] * len(before)

    def kernel(*refs):
        given = dict(zip(kinds, refs))
        rest = refs[len(kinds) :]
        scale_ref, rest = rest[0], rest[1:]
        held_refs = {half: rest[3 * i : 3 * i + 3] for i, half in enumerate(halves)}
        local_refs, outs = rest[3 * len(halves) :], refs[len(specs) : len(specs) + 3]
        temps, sems = refs[-2], refs[-1]
        place = near_place(slices)
        sides = core_side(True)
        copies = []

        def state_of(half, d, j, t):
            rows = slice((t * width + j) * DH, (t * width + j + 1) * DH)
            if half == 0:
                got = given["got", d][rows]
                if d:
                    got = got * jnp.exp2(-mark(given["got", d], t)[:1])
                weight = head_weight(scale_ref, place ^ d, slices, width, j, level)
                return got + (sides[t] * weight) * given["other", d][given["index", d], t, j]
            if d == 0:
                return given["near", 0][t, j]
            ref = given["far", 0]
            at = (((d - 1) * 2 + t) * width + j) * DH
            return ref[at : at + DH] * jnp.exp2(-mark(ref, t)[:1])

        for d in range(slices):
            other = "other_a" if d == slices - 1 else "other_b"
            if other in given:
                given["other", d] = given[other]
                given["index", d] = 0 if d == slices - 1 else d
        for index, (half, d) in enumerate(items):
            k_ref, v_ref, o_ref = held_refs[half]
            group = place ^ d
            part, at_part = where[half, d]
            for j in range(width):
                at = pl.ds(pl.multiple_of((group * width + j) * DH, DH), DH)
                to = slice(j * DH, (j + 1) * DH)
                o, v, k = o_ref[:, at], v_ref[:, at], k_ref[:, at]
                hi, lo = split(state_of(half, d, j, 0))
                qg = dot(o, hi) + dot(o, lo)
                hi, lo = split(state_of(half, d, j, 1))
                kg = dot(v, hi) + dot(v, lo)
                vg = dot(k, hi, NT) + dot(k, lo, NT)
                for i, cross in enumerate((qg, kg, vg)):
                    temps[index, i, :, to] = (cross + local_refs[part][at_part, i, :, to]).astype(BF16)
            start = first_head(half, cols // DH) * DH + group * (width * DH)
            wide = pl.ds(pl.multiple_of(start, DH), width * DH)
            for i in range(3):
                copy = pltpu.make_async_copy(temps.at[index, i], outs[i].at[:, wide], sems.at[index, i])
                copy.start()
                copies.append(copy)
        for copy in copies:
            copy.wait()

    return call(
        kernel,
        [jax.ShapeDtypeStruct((tokens, model), BF16)] * 3,
        args + list(before),
        specs=specs,
        out_specs=[HBM] * 3,
        scratch=[pltpu.VMEM((len(items), 3, tokens, width * DH), BF16), pltpu.SemaphoreType.DMA((len(items), 3))],
        flops=12 * tokens * DH * width * DH * len(items),
        limit=4,
        aliases={len(args) + i: i for i in range(len(before))},
    )


def work(queries, key_rows, values, out_grad, level_weights):
    level_ids = jnp.arange(level_weights.shape[1], dtype=F32)
    level_scale = level_weights * jnp.exp2((1.0 - level_ids) / 2.0)[None, :] / jnp.sqrt(F32(DH * BLOCK))
    heads = level_weights.shape[0]
    tokens, model = queries.shape
    chain = lax.axis_size("seq")
    bits = chain.bit_length() - 1
    plane_bits = min(2, bits)
    slices = 1 << plane_bits
    width = heads // (lax.axis_size("head") * slices)
    local_levels = (tokens // BLOCK).bit_length() - 1
    base = local_levels + 2
    rest = bits - plane_bits
    direct = min(2, rest)

    padded = jnp.pad(level_scale, ((0, 0), (0, -level_scale.shape[1] % 8)))
    scales = jnp.broadcast_to(padded[:, :, None], (*padded.shape, DH))

    args = [pltpu.with_memory_space_constraint(x, pltpu.HBM) for x in (queries, key_rows, values, out_grad)]
    sent_b, sent_a, _, *held_there = device_states(1, args, slices, width, (slices - 1, 1))
    other_a = partner(sent_a, "head", 1)
    other_b = partner(sent_b, "head", 1)
    own, most, *held_here = device_states(0, args, slices, width, (slices,))
    held = (held_here, held_there)
    every = [(half, d) for half in range(2) for d in range(slices)]
    ends = [0, 3 * len(every) // 8, 6 * len(every) // 8, len(every)]
    where, local = {}, []
    for low, high in zip(ends, ends[1:]):
        if low == high:
            continue
        for i, key in enumerate(every[low:high]):
            where[key] = (len(local), i)
        local.append(local_grads(tuple(every[low:high]), scales, held, width))

    state = pltpu.VMEM((2, width, DH, DH), F32)
    load = pltpu.VMEM((2 * width * DH + EXTRA, DH), F32)
    single = pltpu.VMEM((width * DH + EXTRA, DH), F32)
    near = pltpu.VMEM((slices, 2, width, DH, DH), F32)
    bound = pltpu.VMEM((16, DH), F32)

    last = call(functools.partial(chip_kernel, slices - 1), [load], [own, other_a])
    keep, *outs = call(functools.partial(chip_kernel, 0), [load] * (slices - 1), [own, other_b])
    outs += last
    got = []
    for d in range(1, slices):
        got.append(narrow(outs[d - 1], "seq", d))
    wide = rest > direct
    near_sum, bounds, *outs = call(
        functools.partial(plane_kernel, plane_bits, base, rest, wide),
        [near, bound] + ([state] if wide else [single] * direct),
        [scales, keep, *got],
    )
    total = outs[0] if wide else None
    for index in range(rest - direct):
        both = call(lambda ref, out: pack(out, [ref[0], ref[1]]), [load], [total])[0]
        arrived = narrow(both, "seq", slices << index)
        sending = direct if index + 1 == rest - direct else 0
        near_sum, bounds, total, *outs = call(
            functools.partial(merge_kernel, slices, index, base + plane_bits + index, rest),
            [near, bound, state] + [single] * sending,
            [scales, near_sum, bounds, total, arrived],
        )
    got, levels, which = [], [], []
    for step in range(1, 1 << direct):
        top = step.bit_length() - 1
        got.append(narrow(outs[top], "seq", (slices << (rest - direct)) * step))
        which.append(rest - direct + top)
        levels.append(base + plane_bits + rest - direct + top)
    keep, *outs = call(
        functools.partial(back_kernel, slices, levels, which), [load] * slices, [scales, near_sum, bounds, *got]
    )
    got = []
    for d in range(1, slices):
        got.append(narrow(outs[d - 1], "seq", d))
    level = local_levels + 1
    near_theirs = call(functools.partial(near_core_kernel, level, slices), [state], [scales, own, keep])[0]
    near_theirs = partner(near_theirs, "head", 1)
    rest_rows = pltpu.VMEM((2 * (slices - 1) * width * DH + EXTRA, DH), F32)
    theirs = call(functools.partial(core_kernel, level), [rest_rows], [scales, own, most, *got])[0]
    theirs = narrow(theirs, "head", 1)
    others = ["other_b", "other_a"]
    common = (held, local, where, scales, level, model)
    done = finish([(0, 0), (1, 0)], ["other_b", ("got", 0), ("near", 0)], [other_b, keep, near_theirs], *common, [])
    away = range(1, slices)
    done = finish([(0, d) for d in away], others + [("got", d) for d in away], [other_b, other_a, *got], *common, done)
    return tuple(finish([(1, d) for d in away], [("far", 0)], [theirs], *common, done))


def solution(mesh):
    rows = P(("seq", "head"), None)
    return jax.shard_map(
        work,
        mesh=mesh,
        in_specs=(rows, rows, rows, rows, P()),
        out_specs=(rows, rows, rows),
        check_vma=False,
    )
```

```python
import functools

import jax
import jax.numpy as jnp
from jax import lax
from jax.experimental import pallas as pl
from jax.experimental.pallas import tpu as pltpu
from jax.sharding import PartitionSpec as P

DH = 128
BLOCK = 128
EXTRA = 16
TOP = 14.0
PIECE = 32
F32 = jnp.float32
BF16 = jnp.bfloat16
F16 = jnp.float16
NT = (((1,), (1,)), ((), ()))
TN = (((0,), (0,)), ((), ()))
VMEM = pl.BlockSpec(memory_space=pltpu.VMEM)
HBM = pl.BlockSpec(memory_space=pltpu.HBM)


def dot(a, b, dims=None):
    if dims is None:
        dims = (((1,), (0,)), ((), ()))
    return lax.dot_general(a, b, dims, preferred_element_type=F32)


def split(x):
    hi = x.astype(BF16)
    return hi, (x - hi.astype(F32)).astype(BF16)


def call(kernel, outs, args, specs=None, out_specs=None, scratch=(), flops=0, limit=2, aliases=None):
    moved = sum(x.size * x.dtype.itemsize for x in args)
    return pl.pallas_call(
        kernel,
        in_specs=specs or [VMEM] * len(args),
        out_specs=out_specs or [VMEM] * len(outs),
        out_shape=list(outs),
        scratch_shapes=list(scratch),
        input_output_aliases=aliases or {},
        compiler_params=pltpu.CompilerParams(vmem_limit_bytes=limit << 20),
        cost_estimate=pl.CostEstimate(flops=flops, bytes_accessed=moved, transcendentals=0),
    )(*args)


def partner(array, axis, distance):
    return lax.ppermute(array, axis, [(i, i ^ distance) for i in range(lax.axis_size(axis))])


def narrow(array, axis, distance):
    return partner(array.astype(F16), axis, distance).astype(F32)


def marks_of(value):
    most = jnp.maximum(jnp.max(jnp.abs(value)), 1e-30)
    return TOP - jnp.ceil(jnp.log2(jnp.full((8, DH), most, F32)))


def pack(out_ref, values):
    rows = 0
    marks = []
    for value in values:
        power = marks_of(value)
        flat = value.reshape(-1, DH)
        out_ref[rows : rows + flat.shape[0]] = flat * jnp.exp2(power)[:1]
        rows += flat.shape[0]
        marks.append(power)
    put_marks(out_ref, marks)


def put_marks(out_ref, marks):
    rows = out_ref.shape[0] - EXTRA
    for i in range(EXTRA // 8):
        out_ref[rows + 8 * i : rows + 8 * i + 8] = marks[min(i, len(marks) - 1)]


def mark(ref, index):
    rows = ref.shape[0] - EXTRA
    return ref[rows + 8 * index : rows + 8 * index + 8]


def bound_power(bound):
    return TOP - jnp.ceil(jnp.log2(jnp.maximum(bound, 1e-30)))


def unpack(ref, shape, count):
    size = (ref.shape[0] - EXTRA) // count
    return [
        (ref[i * size : (i + 1) * size] * jnp.exp2(-mark(ref, i)[:1])).reshape(shape) for i in range(count)
    ]


def pieces(width):
    return [(j, r, slice(r, r + PIECE)) for j in range(width) for r in range(0, DH, PIECE)]


def first_head(half, heads):
    return (lax.axis_index("head") ^ half) * heads


def near_place(slices):
    return lax.axis_index("seq") & (slices - 1)


def state_kernel(half, cuts, *refs):
    srcs, refs = refs[:4], refs[4:]
    if half:
        (early_ref, late_ref), held, (out_ref, sems) = refs[:2], refs[2:6], refs[6:]
    else:
        (out_ref, mark_ref), held, (sems,) = refs[:2], refs[2:6], refs[6:]
    q_ref, k_ref, v_ref, o_ref = held
    slices, _, width = out_ref.shape[:3]
    model = q_ref.shape[1]
    place = near_place(slices)
    size = model // cuts
    copies = []
    for c in range(cuts):
        start = pl.multiple_of(first_head(half, model // DH) * DH + c * size, DH)
        for i in range(4):
            copy = pltpu.make_async_copy(
                srcs[i].at[:, pl.ds(start, size)], held[i].at[:, c * size : (c + 1) * size], sems.at[c, i]
            )
            copy.start()
            copies.append(copy)
    most = [jnp.zeros((8, DH), F32)] * 2
    for c in range(cuts):
        for i in range(4):
            copies[4 * c + i].wait()
        for head in range(c * size // DH, (c + 1) * size // DH):
            d, j = place ^ (head // width), head % width
            cols = slice(head * DH, (head + 1) * DH)
            pairs = (dot(v_ref[:, cols], k_ref[:, cols], TN), dot(o_ref[:, cols], q_ref[:, cols], TN))
            for t in range(2):
                out_ref[d, t, j] = pairs[t]
                if half == 0:
                    most[t] = jnp.maximum(most[t], jnp.max(jnp.abs(pairs[t]).reshape(-1, 8, DH), axis=0))
    if half:
        late_ref[...] = out_ref[: slices - 1]
        early_ref[0] = out_ref[slices - 1]
    else:
        for t in range(2):
            mark_ref[8 * t : 8 * t + 8] = jnp.full((8, DH), jnp.max(most[t]), F32)


def device_states(half, args, slices, width):
    tokens = args[0].shape[0]
    cuts = 2 if slices % 2 == 0 else 1

    def states(count):
        return pltpu.VMEM((count, 2, width, DH, DH), F32)

    return call(
        functools.partial(state_kernel, half, cuts),
        ([states(1), states(slices - 1)] if half else [states(slices), pltpu.VMEM((16, DH), F32)])
        + [pltpu.VMEM((tokens, slices * width * DH), BF16)] * 4,
        args,
        specs=[HBM] * 4,
        scratch=([states(slices)] if half else []) + [pltpu.SemaphoreType.DMA((cuts, 4))],
        flops=4 * slices * width * tokens * DH * DH,
    )


def local_kernel(lot, width, scale_ref, *refs):
    held, out_ref = (refs[:4], refs[4:8]), refs[8]
    tokens, model = refs[0].shape
    blocks = tokens // BLOCK
    rows = lax.broadcasted_iota(jnp.int32, (BLOCK, BLOCK), 0)
    cols = lax.broadcasted_iota(jnp.int32, (BLOCK, BLOCK), 1)

    def blk(n, m=None):
        return slice(n * BLOCK, (n + 1 if m is None else m) * BLOCK)

    def product(left, right, weight, values, n, low, high, mask):
        raw = dot(left[blk(n)], right[blk(low, high)], NT)
        parts, rest = [], []
        for m in range(low, high):
            part = raw[:, blk(m - low)]
            if m == n:
                parts.append(jnp.where(mask, part * weight(0), 0.0).astype(BF16))
            else:
                hi, lo = split(part * weight((m ^ n).bit_length()))
                parts.append(hi)
                rest.append((m, lo))
        out = dot(jnp.concatenate(parts, axis=1) if len(parts) > 1 else parts[0], values[blk(low, high)])
        for m, lo in rest:
            out = out + dot(lo, values[blk(m)])
        return out

    place = near_place(model // (width * DH))
    for index, (half, d) in enumerate(lot):
        group = place ^ d
        for j in range(width):
            at = pl.ds(pl.multiple_of((group * width + j) * DH, DH), DH)
            to = slice(j * DH, (j + 1) * DH)
            q, k, v, o = (ref[:, at] for ref in held[half])
            head = first_head(half, model // DH) + group * width + j

            def weight(level, head=head):
                return scale_ref[head, level : level + 1]

            for n in range(blocks):
                out_ref[index, 2, blk(n), to] = product(k, q, weight, o, n, n, blocks, rows <= cols)
                out_ref[index, 1, blk(n), to] = product(v, o, weight, q, n, n, blocks, rows <= cols)
                out_ref[index, 0, blk(n), to] = product(o, v, weight, k, n, 0, n + 1, rows >= cols)


def local_grads(lot, scales, held, width):
    tokens = held[0][0].shape[0]
    return call(
        functools.partial(local_kernel, lot, width),
        [pltpu.VMEM((len(lot), 3, tokens, width * DH), F32)],
        [scales, *held[0], *held[1]],
        flops=24 * tokens * BLOCK * width * DH * len(lot),
    )[0]


def chip_kernel(first, own_ref, other_ref, *out_refs):
    for index, out_ref in enumerate(out_refs):
        d = first + index
        values = [own_ref[d, t] + other_ref[index, t] for t in range(2)]
        if d:
            pack(out_ref, values)
            continue
        rows = (out_ref.shape[0] - EXTRA) // 2
        for t in range(2):
            out_ref[t * rows : (t + 1) * rows] = values[t].reshape(rows, DH)
        put_marks(out_ref, [marks_of(value) for value in values])


def bit_of(value, index):
    return ((value >> index) & 1).astype(F32)


def head_weight(scale_ref, place, slices, width, j, level):
    return scale_ref[first_head(0, slices * width) + place * width + j, level : level + 1]


def plane_kernel(plane_bits, base, rest, wide, scale_ref, keep_ref, *refs):
    slices = 1 << plane_bits
    parts, refs = (keep_ref, *refs[: slices - 1]), refs[slices - 1 :]
    near_ref, bound_ref, refs = refs[0], refs[1], refs[2:]
    total_ref = refs[0] if wide else None
    outs = refs[1:] if wide else refs
    width = near_ref.shape[2]
    place = near_place(slices)
    row = lax.axis_index("seq") // slices
    factors = [[None if e == 0 else jnp.exp2(-mark(parts[e], t)[:1]) for t in range(2)] for e in range(slices)]
    bounds = [
        functools.reduce(jnp.add, [jnp.exp2(TOP - mark(parts[e], t)) for e in range(slices)]) for t in range(2)
    ]
    for t in range(2):
        bound_ref[8 * t : 8 * t + 8] = bounds[t]
    ups = [bit_of(row, rest - len(outs) + i) for i in range(len(outs))]
    factor_out = []
    for out_ref, up in zip(outs, ups):
        power = bound_power(jnp.where(up > 0, bounds[1], bounds[0]))
        put_marks(out_ref, [power])
        factor_out.append(jnp.exp2(power)[:1])
    sides = [[bit_of(place ^ d, b) for b in range(plane_bits)] for d in range(slices)]
    for j, r, rows in pieces(width):
        weights = [head_weight(scale_ref, place, slices, width, j, base + b) for b in range(plane_bits)]
        values = []
        for t in range(2):
            at = (t * width + j) * DH + r
            loaded = [parts[e][at : at + PIECE] for e in range(slices)]
            loaded = [x if f[t] is None else x * f[t] for x, f in zip(loaded, factors)]
            sums = {}
            for b in range(plane_bits + 1):
                for first in range(0, slices, 1 << b):
                    half = 1 << (b - 1) if b else 0
                    sums[b, first] = loaded[first] if b == 0 else sums[b - 1, first] + sums[b - 1, first + half]
            values.append(sums)
        for d in range(slices):
            early, late = [], []
            for b in range(plane_bits):
                first = ((d >> b) ^ 1) << b
                up = sides[d][b]
                early.append((up * weights[b]) * values[0][b, first])
                late.append(((1.0 - up) * weights[b]) * values[1][b, first])
            zero = jnp.zeros((PIECE, DH), F32)
            near_ref[d, 0, j, rows] = functools.reduce(jnp.add, early) if early else zero
            near_ref[d, 1, j, rows] = functools.reduce(jnp.add, late) if late else zero
        total = [values[t][plane_bits, 0] for t in range(2)]
        for t in range(2):
            if wide:
                total_ref[t, j, rows] = total[t]
        at = j * DH + r
        for out_ref, up, factor in zip(outs, ups, factor_out):
            out_ref[at : at + PIECE] = jnp.where(up > 0, total[1], total[0]) * factor


def far_out(outs, total_ref, rest, slices):
    row = lax.axis_index("seq") // slices
    for i, out_ref in enumerate(outs):
        up = bit_of(row, rest - len(outs) + i)
        pack(out_ref, [jnp.where(up > 0, total_ref[1], total_ref[0])])


def merge_kernel(slices, index, level, rest, scale_ref, near_ref, bound_ref, total_ref, got_ref, near_out, bound_out, total_out, *outs):
    width = total_ref.shape[1]
    row = lax.axis_index("seq") // slices
    place = near_place(slices)
    up = bit_of(row, index)
    got = unpack(got_ref, (width, DH, DH), 2)
    for t in range(2):
        bound_out[8 * t : 8 * t + 8] = bound_ref[8 * t : 8 * t + 8] + jnp.exp2(TOP - mark(got_ref, t))
    for j in range(width):
        weight = head_weight(scale_ref, place, slices, width, j, level)
        for d in range(slices):
            near_out[d, 0, j] = near_ref[d, 0, j] + (up * weight) * got[0][j]
            near_out[d, 1, j] = near_ref[d, 1, j] + ((1.0 - up) * weight) * got[1][j]
    for t in range(2):
        total_out[t] = total_ref[t] + got[t]
    far_out(outs, total_out, rest, slices)


def back_kernel(slices, levels, bits, scale_ref, near_ref, bound_ref, *refs):
    count = len(levels)
    gots, (keep_ref, *outs) = refs[:count], refs[count:]
    width = near_ref.shape[2]
    row = lax.axis_index("seq") // slices
    place = near_place(slices)
    ups = [bit_of(row, bit) for bit in bits]
    bounds = [bound_ref[:8], bound_ref[8:]]
    for got_ref, up in zip(gots, ups):
        size = jnp.exp2(TOP - mark(got_ref, 0))
        bounds = [bounds[0] + up * size, bounds[1] + (1.0 - up) * size]
    head = first_head(0, scale_ref.shape[0] // lax.axis_size("head")) + place * width
    most = functools.reduce(jnp.maximum, [jnp.abs(scale_ref[head + j]) for j in range(width)])
    most = jnp.max(most, axis=0, keepdims=True)
    powers = [bound_power(most * bound) for bound in bounds]
    factors = [jnp.exp2(power)[:1] for power in powers]
    for out_ref in (keep_ref, *outs):
        put_marks(out_ref, powers)
    opened = [jnp.exp2(-mark(got_ref, 0)[:1]) for got_ref in gots]
    for j, r, rows in pieces(width):
        far = [jnp.zeros((PIECE, DH), F32)] * 2
        at = j * DH + r
        for got_ref, level, up, factor in zip(gots, levels, ups, opened):
            weight = head_weight(scale_ref, place, slices, width, j, level)
            got = got_ref[at : at + PIECE] * factor
            far = [far[0] + (up * weight) * got, far[1] + ((1.0 - up) * weight) * got]
        for d, out_ref in enumerate((keep_ref, *outs)):
            for t in range(2):
                value = near_ref[d, t, j, rows] + far[t]
                to = t * width * DH + at
                out_ref[to : to + PIECE] = value if d == 0 else value * factors[t]


def core_side(mine):
    second = lax.axis_index("head").astype(F32)
    return (second, 1.0 - second) if mine else (1.0 - second, second)


def near_core_kernel(level, slices, scale_ref, own_ref, keep_ref, out_ref):
    width = out_ref.shape[1]
    place = near_place(slices)
    sides = core_side(False)
    for j, r, rows in pieces(width):
        weight = head_weight(scale_ref, place, slices, width, j, level)
        for t in range(2):
            at = (t * width + j) * DH + r
            out_ref[t, j, rows] = keep_ref[at : at + PIECE] + (sides[t] * weight) * own_ref[0, t, j, rows]


def core_kernel(level, scale_ref, own_ref, most_ref, *refs):
    parts, out_ref = refs[:-1], refs[-1]
    slices, _, width = own_ref.shape[:3]
    place = near_place(slices)
    sides = core_side(False)
    first = first_head(0, scale_ref.shape[0] // lax.axis_size("head"))
    weights = [jnp.abs(scale_ref[first + h, level : level + 1]) for h in range(slices * width)]
    heaviest = functools.reduce(jnp.maximum, weights)
    powers = []
    for t in range(2):
        bound = functools.reduce(jnp.maximum, [jnp.exp2(TOP - mark(part, t)) for part in parts])
        powers.append(bound_power(bound + heaviest * most_ref[8 * t : 8 * t + 8]))
    put_marks(out_ref, powers)
    for d, part in enumerate(parts, 1):
        for t in range(2):
            opened = jnp.exp2(powers[t][:1] - mark(part, t)[:1])
            closed = sides[t] * jnp.exp2(powers[t][:1])
            for j, r, rows in pieces(width):
                weight = head_weight(scale_ref, place ^ d, slices, width, j, level)
                at = (t * width + j) * DH + r
                to = (((d - 1) * 2 + t) * width + j) * DH + r
                out_ref[to : to + PIECE] = part[at : at + PIECE] * opened + (closed * weight) * own_ref[d, t, j, rows]


def finish(items, kinds, states, held, parts, where, scales, level, model, before):
    tokens, cols = held[0][0].shape
    width = parts[0].shape[3] // DH
    slices = cols // (width * DH)
    halves = sorted({half for half, _ in items})
    args = [*states, scales, *[x for half in halves for x in held[half][1:]], *parts]
    specs = [VMEM] * len(args) + [HBM] * len(before)

    def kernel(*refs):
        given = dict(zip(kinds, refs))
        rest = refs[len(kinds) :]
        scale_ref, rest = rest[0], rest[1:]
        held_refs = {half: rest[3 * i : 3 * i + 3] for i, half in enumerate(halves)}
        local_refs, outs = rest[3 * len(halves) :], refs[len(specs) : len(specs) + 3]
        temps, sems = refs[-2], refs[-1]
        place = near_place(slices)
        sides = core_side(True)
        copies = []

        def state_of(half, d, j, t):
            rows = slice((t * width + j) * DH, (t * width + j + 1) * DH)
            if half == 0:
                got = given["got", d][rows]
                if d:
                    got = got * jnp.exp2(-mark(given["got", d], t)[:1])
                weight = head_weight(scale_ref, place ^ d, slices, width, j, level)
                return got + (sides[t] * weight) * given["other", d][given["index", d], t, j]
            if d == 0:
                return given["near", 0][t, j]
            ref = given["far", 0]
            at = (((d - 1) * 2 + t) * width + j) * DH
            return ref[at : at + DH] * jnp.exp2(-mark(ref, t)[:1])

        for d in range(slices):
            other = "other_a" if d == slices - 1 else "other_b"
            if other in given:
                given["other", d] = given[other]
                given["index", d] = 0 if d == slices - 1 else d
        for index, (half, d) in enumerate(items):
            k_ref, v_ref, o_ref = held_refs[half]
            group = place ^ d
            part, at_part = where[half, d]
            for j in range(width):
                at = pl.ds(pl.multiple_of((group * width + j) * DH, DH), DH)
                to = slice(j * DH, (j + 1) * DH)
                o, v, k = o_ref[:, at], v_ref[:, at], k_ref[:, at]
                hi, lo = split(state_of(half, d, j, 0))
                qg = dot(o, hi) + dot(o, lo)
                hi, lo = split(state_of(half, d, j, 1))
                kg = dot(v, hi) + dot(v, lo)
                vg = dot(k, hi, NT) + dot(k, lo, NT)
                for i, cross in enumerate((qg, kg, vg)):
                    temps[index, i, :, to] = (cross + local_refs[part][at_part, i, :, to]).astype(BF16)
            start = first_head(half, cols // DH) * DH + group * (width * DH)
            wide = pl.ds(pl.multiple_of(start, DH), width * DH)
            for i in range(3):
                copy = pltpu.make_async_copy(temps.at[index, i], outs[i].at[:, wide], sems.at[index, i])
                copy.start()
                copies.append(copy)
        for copy in copies:
            copy.wait()

    return call(
        kernel,
        [jax.ShapeDtypeStruct((tokens, model), BF16)] * 3,
        args + list(before),
        specs=specs,
        out_specs=[HBM] * 3,
        scratch=[pltpu.VMEM((len(items), 3, tokens, width * DH), BF16), pltpu.SemaphoreType.DMA((len(items), 3))],
        flops=12 * tokens * DH * width * DH * len(items),
        limit=4,
        aliases={len(args) + i: i for i in range(len(before))},
    )


def work(queries, key_rows, values, out_grad, level_weights):
    level_ids = jnp.arange(level_weights.shape[1], dtype=F32)
    level_scale = level_weights * jnp.exp2((1.0 - level_ids) / 2.0)[None, :] / jnp.sqrt(F32(DH * BLOCK))
    heads = level_weights.shape[0]
    tokens, model = queries.shape
    chain = lax.axis_size("seq")
    bits = chain.bit_length() - 1
    plane_bits = min(2, bits)
    slices = 1 << plane_bits
    width = heads // (lax.axis_size("head") * slices)
    local_levels = (tokens // BLOCK).bit_length() - 1
    base = local_levels + 2
    rest = bits - plane_bits
    direct = min(2, rest)

    padded = jnp.pad(level_scale, ((0, 0), (0, -level_scale.shape[1] % 8)))
    scales = jnp.broadcast_to(padded[:, :, None], (*padded.shape, DH))

    args = [pltpu.with_memory_space_constraint(x, pltpu.HBM) for x in (queries, key_rows, values, out_grad)]
    sent_a, sent_b, *held_there = device_states(1, args, slices, width)
    other_a = partner(sent_a, "head", 1)
    other_b = partner(sent_b, "head", 1)
    own, most, *held_here = device_states(0, args, slices, width)
    held = (held_here, held_there)
    every = [(half, d) for half in range(2) for d in range(slices)]
    ends = [0, 3 * len(every) // 8, 6 * len(every) // 8, len(every)]
    where, local = {}, []
    for low, high in zip(ends, ends[1:]):
        if low == high:
            continue
        for i, key in enumerate(every[low:high]):
            where[key] = (len(local), i)
        local.append(local_grads(tuple(every[low:high]), scales, held, width))

    state = pltpu.VMEM((2, width, DH, DH), F32)
    load = pltpu.VMEM((2 * width * DH + EXTRA, DH), F32)
    single = pltpu.VMEM((width * DH + EXTRA, DH), F32)
    near = pltpu.VMEM((slices, 2, width, DH, DH), F32)
    bound = pltpu.VMEM((16, DH), F32)

    last = call(functools.partial(chip_kernel, slices - 1), [load], [own, other_a])
    keep, *outs = call(functools.partial(chip_kernel, 0), [load] * (slices - 1), [own, other_b])
    outs += last
    got = []
    for d in range(1, slices):
        got.append(narrow(outs[d - 1], "seq", d))
    wide = rest > direct
    near_sum, bounds, *outs = call(
        functools.partial(plane_kernel, plane_bits, base, rest, wide),
        [near, bound] + ([state] if wide else [single] * direct),
        [scales, keep, *got],
    )
    total = outs[0] if wide else None
    for index in range(rest - direct):
        both = call(lambda ref, out: pack(out, [ref[0], ref[1]]), [load], [total])[0]
        arrived = narrow(both, "seq", slices << index)
        sending = direct if index + 1 == rest - direct else 0
        near_sum, bounds, total, *outs = call(
            functools.partial(merge_kernel, slices, index, base + plane_bits + index, rest),
            [near, bound, state] + [single] * sending,
            [scales, near_sum, bounds, total, arrived],
        )
    got, levels, which = [], [], []
    for step in range(1, 1 << direct):
        top = step.bit_length() - 1
        got.append(narrow(outs[top], "seq", (slices << (rest - direct)) * step))
        which.append(rest - direct + top)
        levels.append(base + plane_bits + rest - direct + top)
    keep, *outs = call(
        functools.partial(back_kernel, slices, levels, which), [load] * slices, [scales, near_sum, bounds, *got]
    )
    got = []
    for d in range(1, slices):
        got.append(narrow(outs[d - 1], "seq", d))
    level = local_levels + 1
    near_theirs = call(functools.partial(near_core_kernel, level, slices), [state], [scales, own, keep])[0]
    near_theirs = partner(near_theirs, "head", 1)
    rest_rows = pltpu.VMEM((2 * (slices - 1) * width * DH + EXTRA, DH), F32)
    theirs = call(functools.partial(core_kernel, level), [rest_rows], [scales, own, most, *got])[0]
    theirs = narrow(theirs, "head", 1)
    others = ["other_b", "other_a"]
    common = (held, local, where, scales, level, model)
    done = finish([(0, 0), (1, 0)], ["other_b", ("got", 0), ("near", 0)], [other_b, keep, near_theirs], *common, [])
    away = range(1, slices)
    done = finish([(0, d) for d in away], others + [("got", d) for d in away], [other_b, other_a, *got], *common, done)
    return tuple(finish([(1, d) for d in away], [("far", 0)], [theirs], *common, done))


def solution(mesh):
    rows = P(("seq", "head"), None)
    return jax.shard_map(
        work,
        mesh=mesh,
        in_specs=(rows, rows, rows, rows, P()),
        out_specs=(rows, rows, rows),
        check_vma=False,
    )
```

```python
import functools

import jax
import jax.numpy as jnp
from jax import lax
from jax.experimental import pallas as pl
from jax.experimental.pallas import tpu as pltpu
from jax.sharding import PartitionSpec as P

DH = 128
BLOCK = 128
EXTRA = 16
TOP = 14.0
PIECE = 32
F32 = jnp.float32
BF16 = jnp.bfloat16
F16 = jnp.float16
NT = (((1,), (1,)), ((), ()))
TN = (((0,), (0,)), ((), ()))
VMEM = pl.BlockSpec(memory_space=pltpu.VMEM)
HBM = pl.BlockSpec(memory_space=pltpu.HBM)


def dot(a, b, dims=None):
    if dims is None:
        dims = (((1,), (0,)), ((), ()))
    return lax.dot_general(a, b, dims, preferred_element_type=F32)


def split(x):
    hi = x.astype(BF16)
    return hi, (x - hi.astype(F32)).astype(BF16)


def call(kernel, outs, args, specs=None, out_specs=None, scratch=(), flops=0, limit=2, aliases=None):
    moved = sum(x.size * x.dtype.itemsize for x in args)
    return pl.pallas_call(
        kernel,
        in_specs=specs or [VMEM] * len(args),
        out_specs=out_specs or [VMEM] * len(outs),
        out_shape=list(outs),
        scratch_shapes=list(scratch),
        input_output_aliases=aliases or {},
        compiler_params=pltpu.CompilerParams(vmem_limit_bytes=limit << 20),
        cost_estimate=pl.CostEstimate(flops=flops, bytes_accessed=moved, transcendentals=0),
    )(*args)


def partner(array, axis, distance):
    return lax.ppermute(array, axis, [(i, i ^ distance) for i in range(lax.axis_size(axis))])


def narrow(array, axis, distance):
    return partner(array.astype(F16), axis, distance).astype(F32)


def marks_of(value):
    most = jnp.maximum(jnp.max(jnp.abs(value)), 1e-30)
    return TOP - jnp.ceil(jnp.log2(jnp.full((8, DH), most, F32)))


def pack(out_ref, values):
    rows = 0
    marks = []
    for value in values:
        power = marks_of(value)
        flat = value.reshape(-1, DH)
        out_ref[rows : rows + flat.shape[0]] = flat * jnp.exp2(power)[:1]
        rows += flat.shape[0]
        marks.append(power)
    put_marks(out_ref, marks)


def put_marks(out_ref, marks):
    rows = out_ref.shape[0] - EXTRA
    for i in range(EXTRA // 8):
        out_ref[rows + 8 * i : rows + 8 * i + 8] = marks[min(i, len(marks) - 1)]


def mark(ref, index):
    rows = ref.shape[0] - EXTRA
    return ref[rows + 8 * index : rows + 8 * index + 8]


def bound_power(bound):
    return TOP - jnp.ceil(jnp.log2(jnp.maximum(bound, 1e-30)))


def unpack(ref, shape, count):
    size = (ref.shape[0] - EXTRA) // count
    return [
        (ref[i * size : (i + 1) * size] * jnp.exp2(-mark(ref, i)[:1])).reshape(shape) for i in range(count)
    ]


def pieces(width):
    return [(j, r, slice(r, r + PIECE)) for j in range(width) for r in range(0, DH, PIECE)]


def first_head(half, heads):
    return (lax.axis_index("head") ^ half) * heads


def near_place(slices):
    return lax.axis_index("seq") & (slices - 1)


def form_states(heads, held, out_ref, visit=None):
    q_ref, k_ref, v_ref, o_ref = held
    slices, _, width = out_ref.shape[:3]
    place = near_place(slices)
    for head in heads:
        d, j = place ^ (head // width), head % width
        cols = slice(head * DH, (head + 1) * DH)
        pairs = (dot(v_ref[:, cols], k_ref[:, cols], TN), dot(o_ref[:, cols], q_ref[:, cols], TN))
        for t in range(2):
            out_ref[d, t, j] = pairs[t]
            if visit:
                visit(t, pairs[t])


def first_kernel(cuts, *refs):
    srcs, (early_ref, late_ref), there, here, (out_ref, sems) = refs[:4], refs[4:6], refs[6:10], refs[10:14], refs[14:]
    slices = out_ref.shape[0]
    model = there[0].shape[1]
    size = model // cuts
    copies = []
    for c in range(cuts):
        start = pl.multiple_of(first_head(1, model // DH) * DH + c * size, DH)
        for i in range(4):
            copies.append(
                pltpu.make_async_copy(
                    srcs[i].at[:, pl.ds(start, size)], there[i].at[:, c * size : (c + 1) * size], sems.at[c, i]
                )
            )
    start = pl.multiple_of(first_head(0, model // DH) * DH, DH)
    for i in range(4):
        copies.append(pltpu.make_async_copy(srcs[i].at[:, pl.ds(start, model)], here[i], sems.at[cuts, i]))
    for copy in copies:
        copy.start()
    for c in range(cuts):
        for copy in copies[4 * c : 4 * c + 4]:
            copy.wait()
        form_states(range(c * size // DH, (c + 1) * size // DH), there, out_ref)
    late_ref[...] = out_ref[: slices - 1]
    early_ref[0] = out_ref[slices - 1]
    for copy in copies[4 * cuts :]:
        copy.wait()


def second_kernel(*refs):
    held, (out_ref, mark_ref) = refs[:4], refs[4:]
    most = [jnp.zeros((8, DH), F32)] * 2

    def visit(t, value):
        most[t] = jnp.maximum(most[t], jnp.max(jnp.abs(value).reshape(-1, 8, DH), axis=0))

    form_states(range(held[0].shape[1] // DH), held, out_ref, visit)
    for t in range(2):
        mark_ref[8 * t : 8 * t + 8] = jnp.full((8, DH), jnp.max(most[t]), F32)


def device_states(args, slices, width):
    tokens = args[0].shape[0]
    cuts = 2 if slices % 2 == 0 else 1

    def states(count):
        return pltpu.VMEM((count, 2, width, DH, DH), F32)

    early, late, *held = call(
        functools.partial(first_kernel, cuts),
        [states(1), states(slices - 1)] + [pltpu.VMEM((tokens, slices * width * DH), BF16)] * 8,
        args,
        specs=[HBM] * 4,
        scratch=[states(slices), pltpu.SemaphoreType.DMA((cuts + 1, 4))],
        flops=4 * slices * width * tokens * DH * DH,
    )
    return early, late, held[4:], held[:4]


def own_states(held, slices, width):
    return call(
        second_kernel,
        [pltpu.VMEM((slices, 2, width, DH, DH), F32), pltpu.VMEM((16, DH), F32)],
        held,
        flops=4 * slices * width * held[0].shape[0] * DH * DH,
    )


def local_kernel(lot, width, scale_ref, *refs):
    held, out_ref = (refs[:4], refs[4:8]), refs[8]
    tokens, model = refs[0].shape
    blocks = tokens // BLOCK
    rows = lax.broadcasted_iota(jnp.int32, (BLOCK, BLOCK), 0)
    cols = lax.broadcasted_iota(jnp.int32, (BLOCK, BLOCK), 1)

    def blk(n, m=None):
        return slice(n * BLOCK, (n + 1 if m is None else m) * BLOCK)

    def product(left, right, weight, values, n, low, high, mask):
        raw = dot(left[blk(n)], right[blk(low, high)], NT)
        parts, rest = [], []
        for m in range(low, high):
            part = raw[:, blk(m - low)]
            if m == n:
                parts.append(jnp.where(mask, part * weight(0), 0.0).astype(BF16))
            else:
                hi, lo = split(part * weight((m ^ n).bit_length()))
                parts.append(hi)
                rest.append((m, lo))
        out = dot(jnp.concatenate(parts, axis=1) if len(parts) > 1 else parts[0], values[blk(low, high)])
        for m, lo in rest:
            out = out + dot(lo, values[blk(m)])
        return out

    place = near_place(model // (width * DH))
    for index, (half, d) in enumerate(lot):
        group = place ^ d
        for j in range(width):
            at = pl.ds(pl.multiple_of((group * width + j) * DH, DH), DH)
            to = slice(j * DH, (j + 1) * DH)
            q, k, v, o = (ref[:, at] for ref in held[half])
            head = first_head(half, model // DH) + group * width + j

            def weight(level, head=head):
                return scale_ref[head, level : level + 1]

            for n in range(blocks):
                out_ref[index, 2, blk(n), to] = product(k, q, weight, o, n, n, blocks, rows <= cols)
                out_ref[index, 1, blk(n), to] = product(v, o, weight, q, n, n, blocks, rows <= cols)
                out_ref[index, 0, blk(n), to] = product(o, v, weight, k, n, 0, n + 1, rows >= cols)


def local_grads(lot, scales, held, width):
    tokens = held[0][0].shape[0]
    return call(
        functools.partial(local_kernel, lot, width),
        [pltpu.VMEM((len(lot), 3, tokens, width * DH), F32)],
        [scales, *held[0], *held[1]],
        flops=24 * tokens * BLOCK * width * DH * len(lot),
    )[0]


def chip_kernel(first, own_ref, other_ref, *out_refs):
    for index, out_ref in enumerate(out_refs):
        d = first + index
        values = [own_ref[d, t] + other_ref[index, t] for t in range(2)]
        if d:
            pack(out_ref, values)
            continue
        rows = (out_ref.shape[0] - EXTRA) // 2
        for t in range(2):
            out_ref[t * rows : (t + 1) * rows] = values[t].reshape(rows, DH)
        put_marks(out_ref, [marks_of(value) for value in values])


def bit_of(value, index):
    return ((value >> index) & 1).astype(F32)


def head_weight(scale_ref, place, slices, width, j, level):
    return scale_ref[first_head(0, slices * width) + place * width + j, level : level + 1]


def plane_kernel(plane_bits, base, rest, wide, scale_ref, keep_ref, *refs):
    slices = 1 << plane_bits
    parts, refs = (keep_ref, *refs[: slices - 1]), refs[slices - 1 :]
    near_ref, bound_ref, refs = refs[0], refs[1], refs[2:]
    total_ref = refs[0] if wide else None
    outs = refs[1:] if wide else refs
    width = near_ref.shape[2]
    place = near_place(slices)
    row = lax.axis_index("seq") // slices
    factors = [[None if e == 0 else jnp.exp2(-mark(parts[e], t)[:1]) for t in range(2)] for e in range(slices)]
    bounds = [
        functools.reduce(jnp.add, [jnp.exp2(TOP - mark(parts[e], t)) for e in range(slices)]) for t in range(2)
    ]
    for t in range(2):
        bound_ref[8 * t : 8 * t + 8] = bounds[t]
    ups = [bit_of(row, rest - len(outs) + i) for i in range(len(outs))]
    factor_out = []
    for out_ref, up in zip(outs, ups):
        power = bound_power(jnp.where(up > 0, bounds[1], bounds[0]))
        put_marks(out_ref, [power])
        factor_out.append(jnp.exp2(power)[:1])
    sides = [[bit_of(place ^ d, b) for b in range(plane_bits)] for d in range(slices)]
    for j, r, rows in pieces(width):
        weights = [head_weight(scale_ref, place, slices, width, j, base + b) for b in range(plane_bits)]
        values = []
        for t in range(2):
            at = (t * width + j) * DH + r
            loaded = [parts[e][at : at + PIECE] for e in range(slices)]
            loaded = [x if f[t] is None else x * f[t] for x, f in zip(loaded, factors)]
            sums = {}
            for b in range(plane_bits + 1):
                for first in range(0, slices, 1 << b):
                    half = 1 << (b - 1) if b else 0
                    sums[b, first] = loaded[first] if b == 0 else sums[b - 1, first] + sums[b - 1, first + half]
            values.append(sums)
        for d in range(slices):
            early, late = [], []
            for b in range(plane_bits):
                first = ((d >> b) ^ 1) << b
                up = sides[d][b]
                early.append((up * weights[b]) * values[0][b, first])
                late.append(((1.0 - up) * weights[b]) * values[1][b, first])
            zero = jnp.zeros((PIECE, DH), F32)
            near_ref[d, 0, j, rows] = functools.reduce(jnp.add, early) if early else zero
            near_ref[d, 1, j, rows] = functools.reduce(jnp.add, late) if late else zero
        total = [values[t][plane_bits, 0] for t in range(2)]
        for t in range(2):
            if wide:
                total_ref[t, j, rows] = total[t]
        at = j * DH + r
        for out_ref, up, factor in zip(outs, ups, factor_out):
            out_ref[at : at + PIECE] = jnp.where(up > 0, total[1], total[0]) * factor


def far_out(outs, total_ref, rest, slices):
    row = lax.axis_index("seq") // slices
    for i, out_ref in enumerate(outs):
        up = bit_of(row, rest - len(outs) + i)
        pack(out_ref, [jnp.where(up > 0, total_ref[1], total_ref[0])])


def merge_kernel(slices, index, level, rest, scale_ref, near_ref, bound_ref, total_ref, got_ref, near_out, bound_out, total_out, *outs):
    width = total_ref.shape[1]
    row = lax.axis_index("seq") // slices
    place = near_place(slices)
    up = bit_of(row, index)
    got = unpack(got_ref, (width, DH, DH), 2)
    for t in range(2):
        bound_out[8 * t : 8 * t + 8] = bound_ref[8 * t : 8 * t + 8] + jnp.exp2(TOP - mark(got_ref, t))
    for j in range(width):
        weight = head_weight(scale_ref, place, slices, width, j, level)
        for d in range(slices):
            near_out[d, 0, j] = near_ref[d, 0, j] + (up * weight) * got[0][j]
            near_out[d, 1, j] = near_ref[d, 1, j] + ((1.0 - up) * weight) * got[1][j]
    for t in range(2):
        total_out[t] = total_ref[t] + got[t]
    far_out(outs, total_out, rest, slices)


def back_kernel(slices, levels, bits, scale_ref, near_ref, bound_ref, *refs):
    count = len(levels)
    gots, (keep_ref, *outs) = refs[:count], refs[count:]
    width = near_ref.shape[2]
    row = lax.axis_index("seq") // slices
    place = near_place(slices)
    ups = [bit_of(row, bit) for bit in bits]
    bounds = [bound_ref[:8], bound_ref[8:]]
    for got_ref, up in zip(gots, ups):
        size = jnp.exp2(TOP - mark(got_ref, 0))
        bounds = [bounds[0] + up * size, bounds[1] + (1.0 - up) * size]
    head = first_head(0, scale_ref.shape[0] // lax.axis_size("head")) + place * width
    most = functools.reduce(jnp.maximum, [jnp.abs(scale_ref[head + j]) for j in range(width)])
    most = jnp.max(most, axis=0, keepdims=True)
    powers = [bound_power(most * bound) for bound in bounds]
    factors = [jnp.exp2(power)[:1] for power in powers]
    for out_ref in (keep_ref, *outs):
        put_marks(out_ref, powers)
    opened = [jnp.exp2(-mark(got_ref, 0)[:1]) for got_ref in gots]
    for j, r, rows in pieces(width):
        far = [jnp.zeros((PIECE, DH), F32)] * 2
        at = j * DH + r
        for got_ref, level, up, factor in zip(gots, levels, ups, opened):
            weight = head_weight(scale_ref, place, slices, width, j, level)
            got = got_ref[at : at + PIECE] * factor
            far = [far[0] + (up * weight) * got, far[1] + ((1.0 - up) * weight) * got]
        for d, out_ref in enumerate((keep_ref, *outs)):
            for t in range(2):
                value = near_ref[d, t, j, rows] + far[t]
                to = t * width * DH + at
                out_ref[to : to + PIECE] = value if d == 0 else value * factors[t]


def core_side(mine):
    second = lax.axis_index("head").astype(F32)
    return (second, 1.0 - second) if mine else (1.0 - second, second)


def near_core_kernel(level, slices, scale_ref, own_ref, keep_ref, out_ref):
    width = out_ref.shape[1]
    place = near_place(slices)
    sides = core_side(False)
    for j, r, rows in pieces(width):
        weight = head_weight(scale_ref, place, slices, width, j, level)
        for t in range(2):
            at = (t * width + j) * DH + r
            out_ref[t, j, rows] = keep_ref[at : at + PIECE] + (sides[t] * weight) * own_ref[0, t, j, rows]


def core_kernel(level, scale_ref, own_ref, most_ref, *refs):
    parts, out_ref = refs[:-1], refs[-1]
    slices, _, width = own_ref.shape[:3]
    place = near_place(slices)
    sides = core_side(False)
    first = first_head(0, scale_ref.shape[0] // lax.axis_size("head"))
    weights = [jnp.abs(scale_ref[first + h, level : level + 1]) for h in range(slices * width)]
    heaviest = functools.reduce(jnp.maximum, weights)
    powers = []
    for t in range(2):
        bound = functools.reduce(jnp.maximum, [jnp.exp2(TOP - mark(part, t)) for part in parts])
        powers.append(bound_power(bound + heaviest * most_ref[8 * t : 8 * t + 8]))
    put_marks(out_ref, powers)
    for d, part in enumerate(parts, 1):
        for t in range(2):
            opened = jnp.exp2(powers[t][:1] - mark(part, t)[:1])
            closed = sides[t] * jnp.exp2(powers[t][:1])
            for j, r, rows in pieces(width):
                weight = head_weight(scale_ref, place ^ d, slices, width, j, level)
                at = (t * width + j) * DH + r
                to = (((d - 1) * 2 + t) * width + j) * DH + r
                out_ref[to : to + PIECE] = part[at : at + PIECE] * opened + (closed * weight) * own_ref[d, t, j, rows]


def finish(items, kinds, states, held, parts, where, scales, level, model, before):
    tokens, cols = held[0][0].shape
    width = parts[0].shape[3] // DH
    slices = cols // (width * DH)
    halves = sorted({half for half, _ in items})
    args = [*states, scales, *[x for half in halves for x in held[half][1:]], *parts]
    specs = [VMEM] * len(args) + [HBM] * len(before)

    def kernel(*refs):
        given = dict(zip(kinds, refs))
        rest = refs[len(kinds) :]
        scale_ref, rest = rest[0], rest[1:]
        held_refs = {half: rest[3 * i : 3 * i + 3] for i, half in enumerate(halves)}
        local_refs, outs = rest[3 * len(halves) :], refs[len(specs) : len(specs) + 3]
        temps, sems = refs[-2], refs[-1]
        place = near_place(slices)
        sides = core_side(True)
        copies = []

        def state_of(half, d, j, t):
            rows = slice((t * width + j) * DH, (t * width + j + 1) * DH)
            if half == 0:
                got = given["got", d][rows]
                if d:
                    got = got * jnp.exp2(-mark(given["got", d], t)[:1])
                weight = head_weight(scale_ref, place ^ d, slices, width, j, level)
                return got + (sides[t] * weight) * given["other", d][given["index", d], t, j]
            if d == 0:
                return given["near", 0][t, j]
            ref = given["far", 0]
            at = (((d - 1) * 2 + t) * width + j) * DH
            return ref[at : at + DH] * jnp.exp2(-mark(ref, t)[:1])

        for d in range(slices):
            other = "other_a" if d == slices - 1 else "other_b"
            if other in given:
                given["other", d] = given[other]
                given["index", d] = 0 if d == slices - 1 else d
        for index, (half, d) in enumerate(items):
            k_ref, v_ref, o_ref = held_refs[half]
            group = place ^ d
            part, at_part = where[half, d]
            for j in range(width):
                at = pl.ds(pl.multiple_of((group * width + j) * DH, DH), DH)
                to = slice(j * DH, (j + 1) * DH)
                o, v, k = o_ref[:, at], v_ref[:, at], k_ref[:, at]
                hi, lo = split(state_of(half, d, j, 0))
                qg = dot(o, hi) + dot(o, lo)
                hi, lo = split(state_of(half, d, j, 1))
                kg = dot(v, hi) + dot(v, lo)
                vg = dot(k, hi, NT) + dot(k, lo, NT)
                for i, cross in enumerate((qg, kg, vg)):
                    temps[index, i, :, to] = (cross + local_refs[part][at_part, i, :, to]).astype(BF16)
            start = first_head(half, cols // DH) * DH + group * (width * DH)
            wide = pl.ds(pl.multiple_of(start, DH), width * DH)
            for i in range(3):
                copy = pltpu.make_async_copy(temps.at[index, i], outs[i].at[:, wide], sems.at[index, i])
                copy.start()
                copies.append(copy)
        for copy in copies:
            copy.wait()

    return call(
        kernel,
        [jax.ShapeDtypeStruct((tokens, model), BF16)] * 3,
        args + list(before),
        specs=specs,
        out_specs=[HBM] * 3,
        scratch=[pltpu.VMEM((len(items), 3, tokens, width * DH), BF16), pltpu.SemaphoreType.DMA((len(items), 3))],
        flops=12 * tokens * DH * width * DH * len(items),
        limit=4,
        aliases={len(args) + i: i for i in range(len(before))},
    )


def work(queries, key_rows, values, out_grad, level_weights):
    level_ids = jnp.arange(level_weights.shape[1], dtype=F32)
    level_scale = level_weights * jnp.exp2((1.0 - level_ids) / 2.0)[None, :] / jnp.sqrt(F32(DH * BLOCK))
    heads = level_weights.shape[0]
    tokens, model = queries.shape
    chain = lax.axis_size("seq")
    bits = chain.bit_length() - 1
    plane_bits = min(2, bits)
    slices = 1 << plane_bits
    width = heads // (lax.axis_size("head") * slices)
    local_levels = (tokens // BLOCK).bit_length() - 1
    base = local_levels + 2
    rest = bits - plane_bits
    direct = min(2, rest)

    padded = jnp.pad(level_scale, ((0, 0), (0, -level_scale.shape[1] % 8)))
    scales = jnp.broadcast_to(padded[:, :, None], (*padded.shape, DH))

    args = [pltpu.with_memory_space_constraint(x, pltpu.HBM) for x in (queries, key_rows, values, out_grad)]
    sent_a, sent_b, held_here, held_there = device_states(args, slices, width)
    other_a = partner(sent_a, "head", 1)
    other_b = partner(sent_b, "head", 1)
    own, most = own_states(held_here, slices, width)
    held = (held_here, held_there)
    every = [(half, d) for half in range(2) for d in range(slices)]
    ends = [0, 3 * len(every) // 8, 6 * len(every) // 8, len(every)]
    where, local = {}, []
    for low, high in zip(ends, ends[1:]):
        if low == high:
            continue
        for i, key in enumerate(every[low:high]):
            where[key] = (len(local), i)
        local.append(local_grads(tuple(every[low:high]), scales, held, width))

    state = pltpu.VMEM((2, width, DH, DH), F32)
    load = pltpu.VMEM((2 * width * DH + EXTRA, DH), F32)
    single = pltpu.VMEM((width * DH + EXTRA, DH), F32)
    near = pltpu.VMEM((slices, 2, width, DH, DH), F32)
    bound = pltpu.VMEM((16, DH), F32)

    last = call(functools.partial(chip_kernel, slices - 1), [load], [own, other_a])
    keep, *outs = call(functools.partial(chip_kernel, 0), [load] * (slices - 1), [own, other_b])
    outs += last
    got = []
    for d in range(1, slices):
        got.append(narrow(outs[d - 1], "seq", d))
    wide = rest > direct
    near_sum, bounds, *outs = call(
        functools.partial(plane_kernel, plane_bits, base, rest, wide),
        [near, bound] + ([state] if wide else [single] * direct),
        [scales, keep, *got],
    )
    total = outs[0] if wide else None
    for index in range(rest - direct):
        both = call(lambda ref, out: pack(out, [ref[0], ref[1]]), [load], [total])[0]
        arrived = narrow(both, "seq", slices << index)
        sending = direct if index + 1 == rest - direct else 0
        near_sum, bounds, total, *outs = call(
            functools.partial(merge_kernel, slices, index, base + plane_bits + index, rest),
            [near, bound, state] + [single] * sending,
            [scales, near_sum, bounds, total, arrived],
        )
    got, levels, which = [], [], []
    for step in range(1, 1 << direct):
        top = step.bit_length() - 1
        got.append(narrow(outs[top], "seq", (slices << (rest - direct)) * step))
        which.append(rest - direct + top)
        levels.append(base + plane_bits + rest - direct + top)
    keep, *outs = call(
        functools.partial(back_kernel, slices, levels, which), [load] * slices, [scales, near_sum, bounds, *got]
    )
    got = []
    for d in range(1, slices):
        got.append(narrow(outs[d - 1], "seq", d))
    level = local_levels + 1
    near_theirs = call(functools.partial(near_core_kernel, level, slices), [state], [scales, own, keep])[0]
    near_theirs = partner(near_theirs, "head", 1)
    rest_rows = pltpu.VMEM((2 * (slices - 1) * width * DH + EXTRA, DH), F32)
    theirs = call(functools.partial(core_kernel, level), [rest_rows], [scales, own, most, *got])[0]
    theirs = narrow(theirs, "head", 1)
    others = ["other_b", "other_a"]
    common = (held, local, where, scales, level, model)
    done = finish([(0, 0), (1, 0)], ["other_b", ("got", 0), ("near", 0)], [other_b, keep, near_theirs], *common, [])
    away = range(1, slices)
    done = finish([(0, d) for d in away], others + [("got", d) for d in away], [other_b, other_a, *got], *common, done)
    return tuple(finish([(1, d) for d in away], [("far", 0)], [theirs], *common, done))


def solution(mesh):
    rows = P(("seq", "head"), None)
    return jax.shard_map(
        work,
        mesh=mesh,
        in_specs=(rows, rows, rows, rows, P()),
        out_specs=(rows, rows, rows),
        check_vma=False,
    )
```

```python
import functools

import jax
import jax.numpy as jnp
from jax import lax
from jax.experimental import pallas as pl
from jax.experimental.pallas import tpu as pltpu
from jax.sharding import PartitionSpec as P

DH = 128
BLOCK = 128
EXTRA = 16
TOP = 14.0
PIECE = 32
F32 = jnp.float32
BF16 = jnp.bfloat16
F16 = jnp.float16
NT = (((1,), (1,)), ((), ()))
TN = (((0,), (0,)), ((), ()))
VMEM = pl.BlockSpec(memory_space=pltpu.VMEM)
HBM = pl.BlockSpec(memory_space=pltpu.HBM)


def dot(a, b, dims=None):
    if dims is None:
        dims = (((1,), (0,)), ((), ()))
    return lax.dot_general(a, b, dims, preferred_element_type=F32)


def split(x):
    hi = x.astype(BF16)
    return hi, (x - hi.astype(F32)).astype(BF16)


def call(kernel, outs, args, specs=None, out_specs=None, scratch=(), flops=0, limit=2, aliases=None):
    moved = sum(x.size * x.dtype.itemsize for x in args)
    return pl.pallas_call(
        kernel,
        in_specs=specs or [VMEM] * len(args),
        out_specs=out_specs or [VMEM] * len(outs),
        out_shape=list(outs),
        scratch_shapes=list(scratch),
        input_output_aliases=aliases or {},
        compiler_params=pltpu.CompilerParams(vmem_limit_bytes=limit << 20),
        cost_estimate=pl.CostEstimate(flops=flops, bytes_accessed=moved, transcendentals=0),
    )(*args)


def partner(array, axis, distance):
    return lax.ppermute(array, axis, [(i, i ^ distance) for i in range(lax.axis_size(axis))])


def narrow(array, axis, distance):
    return partner(array.astype(F16), axis, distance).astype(F32)


def marks_of(value):
    most = jnp.maximum(jnp.max(jnp.abs(value)), 1e-30)
    return TOP - jnp.ceil(jnp.log2(jnp.full((8, DH), most, F32)))


def pack(out_ref, values):
    rows = 0
    marks = []
    for value in values:
        power = marks_of(value)
        flat = value.reshape(-1, DH)
        out_ref[rows : rows + flat.shape[0]] = flat * jnp.exp2(power)[:1]
        rows += flat.shape[0]
        marks.append(power)
    put_marks(out_ref, marks)


def put_marks(out_ref, marks):
    rows = out_ref.shape[0] - EXTRA
    for i in range(EXTRA // 8):
        out_ref[rows + 8 * i : rows + 8 * i + 8] = marks[min(i, len(marks) - 1)]


def mark(ref, index):
    rows = ref.shape[0] - EXTRA
    return ref[rows + 8 * index : rows + 8 * index + 8]


def bound_power(bound):
    return TOP - jnp.ceil(jnp.log2(jnp.maximum(bound, 1e-30)))


def unpack(ref, shape, count):
    size = (ref.shape[0] - EXTRA) // count
    return [
        (ref[i * size : (i + 1) * size] * jnp.exp2(-mark(ref, i)[:1])).reshape(shape) for i in range(count)
    ]


def pieces(width):
    return [(j, r, slice(r, r + PIECE)) for j in range(width) for r in range(0, DH, PIECE)]


def first_head(half, heads):
    return (lax.axis_index("head") ^ half) * heads


def near_place(slices):
    return lax.axis_index("seq") & (slices - 1)


def form_states(heads, held, out_ref, visit=None):
    q_ref, k_ref, v_ref, o_ref = held
    slices, _, width = out_ref.shape[:3]
    place = near_place(slices)
    for head in heads:
        d, j = place ^ (head // width), head % width
        cols = slice(head * DH, (head + 1) * DH)
        pairs = (dot(v_ref[:, cols], k_ref[:, cols], TN), dot(o_ref[:, cols], q_ref[:, cols], TN))
        for t in range(2):
            out_ref[d, t, j] = pairs[t]
            if visit:
                visit(t, pairs[t])


def first_kernel(cuts, *refs):
    srcs, (early_ref, late_ref), there, here, (out_ref, sems) = refs[:4], refs[4:6], refs[6:10], refs[10:14], refs[14:]
    slices = out_ref.shape[0]
    model = there[0].shape[1]
    size = model // cuts
    copies = []
    for c in range(cuts):
        start = pl.multiple_of(first_head(1, model // DH) * DH + c * size, DH)
        for i in range(4):
            copies.append(
                pltpu.make_async_copy(
                    srcs[i].at[:, pl.ds(start, size)], there[i].at[:, c * size : (c + 1) * size], sems.at[c, i]
                )
            )
    start = pl.multiple_of(first_head(0, model // DH) * DH, DH)
    for i in range(4):
        copies.append(pltpu.make_async_copy(srcs[i].at[:, pl.ds(start, model)], here[i], sems.at[cuts, i]))
    for copy in copies:
        copy.start()
    for c in range(cuts):
        for copy in copies[4 * c : 4 * c + 4]:
            copy.wait()
        form_states(range(c * size // DH, (c + 1) * size // DH), there, out_ref)
    late_ref[...] = out_ref[: slices - 1]
    early_ref[0] = out_ref[slices - 1]
    for copy in copies[4 * cuts :]:
        copy.wait()


def second_kernel(*refs):
    held, (out_ref, mark_ref) = refs[:4], refs[4:]
    most = [jnp.zeros((8, DH), F32)] * 2

    def visit(t, value):
        most[t] = jnp.maximum(most[t], jnp.max(jnp.abs(value).reshape(-1, 8, DH), axis=0))

    form_states(range(held[0].shape[1] // DH), held, out_ref, visit)
    for t in range(2):
        mark_ref[8 * t : 8 * t + 8] = jnp.full((8, DH), jnp.max(most[t]), F32)


def device_states(args, slices, width):
    tokens = args[0].shape[0]
    cuts = 1

    def states(count):
        return pltpu.VMEM((count, 2, width, DH, DH), F32)

    early, late, *held = call(
        functools.partial(first_kernel, cuts),
        [states(1), states(slices - 1)] + [pltpu.VMEM((tokens, slices * width * DH), BF16)] * 8,
        args,
        specs=[HBM] * 4,
        scratch=[states(slices), pltpu.SemaphoreType.DMA((cuts + 1, 4))],
        flops=4 * slices * width * tokens * DH * DH,
    )
    return early, late, held[4:], held[:4]


def own_states(held, slices, width):
    return call(
        second_kernel,
        [pltpu.VMEM((slices, 2, width, DH, DH), F32), pltpu.VMEM((16, DH), F32)],
        held,
        flops=4 * slices * width * held[0].shape[0] * DH * DH,
    )


def local_kernel(lot, width, scale_ref, *refs):
    held, out_ref = (refs[:4], refs[4:8]), refs[8]
    tokens, model = refs[0].shape
    blocks = tokens // BLOCK
    rows = lax.broadcasted_iota(jnp.int32, (BLOCK, BLOCK), 0)
    cols = lax.broadcasted_iota(jnp.int32, (BLOCK, BLOCK), 1)

    def blk(n, m=None):
        return slice(n * BLOCK, (n + 1 if m is None else m) * BLOCK)

    def spread(raw, weight, mask, cross):
        zero = jnp.zeros((BLOCK, BLOCK), BF16)
        high, low = [], []
        for n in range(blocks):
            tops, rests = [], []
            for m in range(blocks):
                part = raw[blk(n), blk(m)]
                top = rest = zero
                if m == n:
                    top = jnp.where(mask, part * weight(0), 0.0).astype(BF16)
                elif cross(n, m):
                    top, rest = split(part * weight((m ^ n).bit_length()))
                tops.append(top)
                rests.append(rest)
            high.append(jnp.concatenate(tops, axis=1) if blocks > 1 else tops[0])
            if any(cross(n, m) for m in range(blocks)):
                low.append((n, jnp.concatenate(rests, axis=1)))
        return high, low

    def product(high, low, values):
        out = dot(jnp.concatenate(high + [x for _, x in low], axis=0), values)
        rows = [out[blk(n)] for n in range(blocks)]
        for i, (n, _) in enumerate(low):
            rows[n] = rows[n] + out[blk(blocks + i)]
        return rows

    place = near_place(model // (width * DH))
    for index, (half, d) in enumerate(lot):
        group = place ^ d
        for j in range(width):
            at = pl.ds(pl.multiple_of((group * width + j) * DH, DH), DH)
            to = slice(j * DH, (j + 1) * DH)
            q, k, v, o = (ref[:, at] for ref in held[half])
            head = first_head(half, model // DH) + group * width + j

            def weight(level, head=head):
                return scale_ref[head, level : level + 1]

            high, low = spread(dot(k, q, NT), weight, rows <= cols, lambda n, m: m > n)
            for n, value in enumerate(product(high, low, o)):
                out_ref[index, 2, blk(n), to] = value
            high, low = spread(dot(o, v, NT), weight, rows >= cols, lambda n, m: m < n)
            for n, value in enumerate(product(high, low, k)):
                out_ref[index, 0, blk(n), to] = value
            key_grad = dot(jnp.concatenate(high, axis=0), q, TN)
            for n, value in low:
                key_grad = key_grad + dot(value, q[blk(n)], TN)
            out_ref[index, 1, :, to] = key_grad


def local_grads(lot, scales, held, width):
    tokens = held[0][0].shape[0]
    return call(
        functools.partial(local_kernel, lot, width),
        [pltpu.VMEM((len(lot), 3, tokens, width * DH), F32)],
        [scales, *held[0], *held[1]],
        flops=24 * tokens * BLOCK * width * DH * len(lot),
    )[0]


def chip_kernel(first, own_ref, other_ref, *out_refs):
    for index, out_ref in enumerate(out_refs):
        d = first + index
        values = [own_ref[d, t] + other_ref[index, t] for t in range(2)]
        if d:
            pack(out_ref, values)
            continue
        rows = (out_ref.shape[0] - EXTRA) // 2
        for t in range(2):
            out_ref[t * rows : (t + 1) * rows] = values[t].reshape(rows, DH)
        put_marks(out_ref, [marks_of(value) for value in values])


def bit_of(value, index):
    return ((value >> index) & 1).astype(F32)


def head_weight(scale_ref, place, slices, width, j, level):
    return scale_ref[first_head(0, slices * width) + place * width + j, level : level + 1]


def plane_kernel(plane_bits, base, rest, wide, scale_ref, keep_ref, *refs):
    slices = 1 << plane_bits
    parts, refs = (keep_ref, *refs[: slices - 1]), refs[slices - 1 :]
    near_ref, bound_ref, refs = refs[0], refs[1], refs[2:]
    total_ref = refs[0] if wide else None
    outs = refs[1:] if wide else refs
    width = near_ref.shape[2]
    place = near_place(slices)
    row = lax.axis_index("seq") // slices
    factors = [[None if e == 0 else jnp.exp2(-mark(parts[e], t)[:1]) for t in range(2)] for e in range(slices)]
    bounds = [
        functools.reduce(jnp.add, [jnp.exp2(TOP - mark(parts[e], t)) for e in range(slices)]) for t in range(2)
    ]
    for t in range(2):
        bound_ref[8 * t : 8 * t + 8] = bounds[t]
    ups = [bit_of(row, rest - len(outs) + i) for i in range(len(outs))]
    factor_out = []
    for out_ref, up in zip(outs, ups):
        power = bound_power(jnp.where(up > 0, bounds[1], bounds[0]))
        put_marks(out_ref, [power])
        factor_out.append(jnp.exp2(power)[:1])
    sides = [[bit_of(place ^ d, b) for b in range(plane_bits)] for d in range(slices)]
    for j, r, rows in pieces(width):
        weights = [head_weight(scale_ref, place, slices, width, j, base + b) for b in range(plane_bits)]
        values = []
        for t in range(2):
            at = (t * width + j) * DH + r
            loaded = [parts[e][at : at + PIECE] for e in range(slices)]
            loaded = [x if f[t] is None else x * f[t] for x, f in zip(loaded, factors)]
            sums = {}
            for b in range(plane_bits + 1):
                for first in range(0, slices, 1 << b):
                    half = 1 << (b - 1) if b else 0
                    sums[b, first] = loaded[first] if b == 0 else sums[b - 1, first] + sums[b - 1, first + half]
            values.append(sums)
        for d in range(slices):
            early, late = [], []
            for b in range(plane_bits):
                first = ((d >> b) ^ 1) << b
                up = sides[d][b]
                early.append((up * weights[b]) * values[0][b, first])
                late.append(((1.0 - up) * weights[b]) * values[1][b, first])
            zero = jnp.zeros((PIECE, DH), F32)
            near_ref[d, 0, j, rows] = functools.reduce(jnp.add, early) if early else zero
            near_ref[d, 1, j, rows] = functools.reduce(jnp.add, late) if late else zero
        total = [values[t][plane_bits, 0] for t in range(2)]
        for t in range(2):
            if wide:
                total_ref[t, j, rows] = total[t]
        at = j * DH + r
        for out_ref, up, factor in zip(outs, ups, factor_out):
            out_ref[at : at + PIECE] = jnp.where(up > 0, total[1], total[0]) * factor


def far_out(outs, total_ref, rest, slices):
    row = lax.axis_index("seq") // slices
    for i, out_ref in enumerate(outs):
        up = bit_of(row, rest - len(outs) + i)
        pack(out_ref, [jnp.where(up > 0, total_ref[1], total_ref[0])])


def merge_kernel(slices, index, level, rest, scale_ref, near_ref, bound_ref, total_ref, got_ref, near_out, bound_out, total_out, *outs):
    width = total_ref.shape[1]
    row = lax.axis_index("seq") // slices
    place = near_place(slices)
    up = bit_of(row, index)
    got = unpack(got_ref, (width, DH, DH), 2)
    for t in range(2):
        bound_out[8 * t : 8 * t + 8] = bound_ref[8 * t : 8 * t + 8] + jnp.exp2(TOP - mark(got_ref, t))
    for j in range(width):
        weight = head_weight(scale_ref, place, slices, width, j, level)
        for d in range(slices):
            near_out[d, 0, j] = near_ref[d, 0, j] + (up * weight) * got[0][j]
            near_out[d, 1, j] = near_ref[d, 1, j] + ((1.0 - up) * weight) * got[1][j]
    for t in range(2):
        total_out[t] = total_ref[t] + got[t]
    far_out(outs, total_out, rest, slices)


def back_kernel(slices, levels, bits, scale_ref, near_ref, bound_ref, *refs):
    count = len(levels)
    gots, (keep_ref, *outs) = refs[:count], refs[count:]
    width = near_ref.shape[2]
    row = lax.axis_index("seq") // slices
    place = near_place(slices)
    ups = [bit_of(row, bit) for bit in bits]
    bounds = [bound_ref[:8], bound_ref[8:]]
    for got_ref, up in zip(gots, ups):
        size = jnp.exp2(TOP - mark(got_ref, 0))
        bounds = [bounds[0] + up * size, bounds[1] + (1.0 - up) * size]
    head = first_head(0, scale_ref.shape[0] // lax.axis_size("head")) + place * width
    most = functools.reduce(jnp.maximum, [jnp.abs(scale_ref[head + j]) for j in range(width)])
    most = jnp.max(most, axis=0, keepdims=True)
    powers = [bound_power(most * bound) for bound in bounds]
    factors = [jnp.exp2(power)[:1] for power in powers]
    for out_ref in (keep_ref, *outs):
        put_marks(out_ref, powers)
    opened = [jnp.exp2(-mark(got_ref, 0)[:1]) for got_ref in gots]
    for j, r, rows in pieces(width):
        far = [jnp.zeros((PIECE, DH), F32)] * 2
        at = j * DH + r
        for got_ref, level, up, factor in zip(gots, levels, ups, opened):
            weight = head_weight(scale_ref, place, slices, width, j, level)
            got = got_ref[at : at + PIECE] * factor
            far = [far[0] + (up * weight) * got, far[1] + ((1.0 - up) * weight) * got]
        for d, out_ref in enumerate((keep_ref, *outs)):
            for t in range(2):
                value = near_ref[d, t, j, rows] + far[t]
                to = t * width * DH + at
                out_ref[to : to + PIECE] = value if d == 0 else value * factors[t]


def core_side(mine):
    second = lax.axis_index("head").astype(F32)
    return (second, 1.0 - second) if mine else (1.0 - second, second)


def near_core_kernel(level, slices, scale_ref, own_ref, keep_ref, out_ref):
    width = out_ref.shape[1]
    place = near_place(slices)
    sides = core_side(False)
    for j, r, rows in pieces(width):
        weight = head_weight(scale_ref, place, slices, width, j, level)
        for t in range(2):
            at = (t * width + j) * DH + r
            out_ref[t, j, rows] = keep_ref[at : at + PIECE] + (sides[t] * weight) * own_ref[0, t, j, rows]


def core_kernel(level, scale_ref, own_ref, most_ref, *refs):
    parts, out_ref = refs[:-1], refs[-1]
    slices, _, width = own_ref.shape[:3]
    place = near_place(slices)
    sides = core_side(False)
    first = first_head(0, scale_ref.shape[0] // lax.axis_size("head"))
    weights = [jnp.abs(scale_ref[first + h, level : level + 1]) for h in range(slices * width)]
    heaviest = functools.reduce(jnp.maximum, weights)
    powers = []
    for t in range(2):
        bound = functools.reduce(jnp.maximum, [jnp.exp2(TOP - mark(part, t)) for part in parts])
        powers.append(bound_power(bound + heaviest * most_ref[8 * t : 8 * t + 8]))
    put_marks(out_ref, powers)
    for d, part in enumerate(parts, 1):
        for t in range(2):
            opened = jnp.exp2(powers[t][:1] - mark(part, t)[:1])
            closed = sides[t] * jnp.exp2(powers[t][:1])
            for j, r, rows in pieces(width):
                weight = head_weight(scale_ref, place ^ d, slices, width, j, level)
                at = (t * width + j) * DH + r
                to = (((d - 1) * 2 + t) * width + j) * DH + r
                out_ref[to : to + PIECE] = part[at : at + PIECE] * opened + (closed * weight) * own_ref[d, t, j, rows]


def finish(items, kinds, states, held, parts, where, scales, level, model, before):
    tokens, cols = held[0][0].shape
    width = parts[0].shape[3] // DH
    slices = cols // (width * DH)
    halves = sorted({half for half, _ in items})
    args = [*states, scales, *[x for half in halves for x in held[half][1:]], *parts]
    specs = [VMEM] * len(args) + [HBM] * len(before)

    def kernel(*refs):
        given = dict(zip(kinds, refs))
        rest = refs[len(kinds) :]
        scale_ref, rest = rest[0], rest[1:]
        held_refs = {half: rest[3 * i : 3 * i + 3] for i, half in enumerate(halves)}
        local_refs, outs = rest[3 * len(halves) :], refs[len(specs) : len(specs) + 3]
        temps, sems = refs[-2], refs[-1]
        place = near_place(slices)
        sides = core_side(True)
        copies = []

        def state_of(half, d, j, t):
            rows = slice((t * width + j) * DH, (t * width + j + 1) * DH)
            if half == 0:
                got = given["got", d][rows]
                if d:
                    got = got * jnp.exp2(-mark(given["got", d], t)[:1])
                weight = head_weight(scale_ref, place ^ d, slices, width, j, level)
                return got + (sides[t] * weight) * given["other", d][given["index", d], t, j]
            if d == 0:
                return given["near", 0][t, j]
            ref = given["far", 0]
            at = (((d - 1) * 2 + t) * width + j) * DH
            return ref[at : at + DH] * jnp.exp2(-mark(ref, t)[:1])

        for d in range(slices):
            other = "other_a" if d == slices - 1 else "other_b"
            if other in given:
                given["other", d] = given[other]
                given["index", d] = 0 if d == slices - 1 else d
        for index, (half, d) in enumerate(items):
            k_ref, v_ref, o_ref = held_refs[half]
            group = place ^ d
            part, at_part = where[half, d]
            for j in range(width):
                at = pl.ds(pl.multiple_of((group * width + j) * DH, DH), DH)
                to = slice(j * DH, (j + 1) * DH)
                o, v, k = o_ref[:, at], v_ref[:, at], k_ref[:, at]
                hi, lo = split(state_of(half, d, j, 0))
                qg = dot(o, hi) + dot(o, lo)
                hi, lo = split(state_of(half, d, j, 1))
                kg = dot(v, hi) + dot(v, lo)
                vg = dot(k, hi, NT) + dot(k, lo, NT)
                for i, cross in enumerate((qg, kg, vg)):
                    temps[index, i, :, to] = (cross + local_refs[part][at_part, i, :, to]).astype(BF16)
                wide = pl.ds(pl.multiple_of((first_head(half, cols // DH) + group * width + j) * DH, DH), DH)
                for i in range(3):
                    copy = pltpu.make_async_copy(
                        temps.at[index, i, :, to], outs[i].at[:, wide], sems.at[index * width + j, i]
                    )
                    copy.start()
                    copies.append(copy)
        for copy in copies:
            copy.wait()

    return call(
        kernel,
        [jax.ShapeDtypeStruct((tokens, model), BF16)] * 3,
        args + list(before),
        specs=specs,
        out_specs=[HBM] * 3,
        scratch=[pltpu.VMEM((len(items), 3, tokens, width * DH), BF16), pltpu.SemaphoreType.DMA((len(items) * width, 3))],
        flops=12 * tokens * DH * width * DH * len(items),
        limit=4,
        aliases={len(args) + i: i for i in range(len(before))},
    )


def work(queries, key_rows, values, out_grad, level_weights):
    level_ids = jnp.arange(level_weights.shape[1], dtype=F32)
    level_scale = level_weights * jnp.exp2((1.0 - level_ids) / 2.0)[None, :] / jnp.sqrt(F32(DH * BLOCK))
    heads = level_weights.shape[0]
    tokens, model = queries.shape
    chain = lax.axis_size("seq")
    bits = chain.bit_length() - 1
    plane_bits = min(2, bits)
    slices = 1 << plane_bits
    width = heads // (lax.axis_size("head") * slices)
    local_levels = (tokens // BLOCK).bit_length() - 1
    base = local_levels + 2
    rest = bits - plane_bits
    direct = min(2, rest)

    padded = jnp.pad(level_scale, ((0, 0), (0, -level_scale.shape[1] % 8)))
    scales = jnp.broadcast_to(padded[:, :, None], (*padded.shape, DH))

    args = [pltpu.with_memory_space_constraint(x, pltpu.HBM) for x in (queries, key_rows, values, out_grad)]
    sent_a, sent_b, held_here, held_there = device_states(args, slices, width)
    other_a = partner(sent_a, "head", 1)
    other_b = partner(sent_b, "head", 1)
    own, most = own_states(held_here, slices, width)
    held = (held_here, held_there)
    every = [(half, d) for half in range(2) for d in range(slices)]
    ends = [0, 3 * len(every) // 8, 6 * len(every) // 8, len(every)]
    where, local = {}, []
    for low, high in zip(ends, ends[1:]):
        if low == high:
            continue
        for i, key in enumerate(every[low:high]):
            where[key] = (len(local), i)
        local.append(local_grads(tuple(every[low:high]), scales, held, width))

    state = pltpu.VMEM((2, width, DH, DH), F32)
    load = pltpu.VMEM((2 * width * DH + EXTRA, DH), F32)
    single = pltpu.VMEM((width * DH + EXTRA, DH), F32)
    near = pltpu.VMEM((slices, 2, width, DH, DH), F32)
    bound = pltpu.VMEM((16, DH), F32)

    last = call(functools.partial(chip_kernel, slices - 1), [load], [own, other_a])
    keep, *outs = call(functools.partial(chip_kernel, 0), [load] * (slices - 1), [own, other_b])
    outs += last
    got = []
    for d in range(1, slices):
        got.append(narrow(outs[d - 1], "seq", d))
    wide = rest > direct
    near_sum, bounds, *outs = call(
        functools.partial(plane_kernel, plane_bits, base, rest, wide),
        [near, bound] + ([state] if wide else [single] * direct),
        [scales, keep, *got],
    )
    total = outs[0] if wide else None
    for index in range(rest - direct):
        both = call(lambda ref, out: pack(out, [ref[0], ref[1]]), [load], [total])[0]
        arrived = narrow(both, "seq", slices << index)
        sending = direct if index + 1 == rest - direct else 0
        near_sum, bounds, total, *outs = call(
            functools.partial(merge_kernel, slices, index, base + plane_bits + index, rest),
            [near, bound, state] + [single] * sending,
            [scales, near_sum, bounds, total, arrived],
        )
    got, levels, which = [], [], []
    for step in range(1, 1 << direct):
        top = step.bit_length() - 1
        got.append(narrow(outs[top], "seq", (slices << (rest - direct)) * step))
        which.append(rest - direct + top)
        levels.append(base + plane_bits + rest - direct + top)
    keep, *outs = call(
        functools.partial(back_kernel, slices, levels, which), [load] * slices, [scales, near_sum, bounds, *got]
    )
    got = []
    for d in range(1, slices):
        got.append(narrow(outs[d - 1], "seq", d))
    level = local_levels + 1
    near_theirs = call(functools.partial(near_core_kernel, level, slices), [state], [scales, own, keep])[0]
    near_theirs = partner(near_theirs, "head", 1)
    rest_rows = pltpu.VMEM((2 * (slices - 1) * width * DH + EXTRA, DH), F32)
    theirs = call(functools.partial(core_kernel, level), [rest_rows], [scales, own, most, *got])[0]
    theirs = narrow(theirs, "head", 1)
    others = ["other_b", "other_a"]
    common = (held, local, where, scales, level, model)
    done = finish([(0, 0), (1, 0)], ["other_b", ("got", 0), ("near", 0)], [other_b, keep, near_theirs], *common, [])
    away = range(1, slices)
    done = finish([(0, d) for d in away], others + [("got", d) for d in away], [other_b, other_a, *got], *common, done)
    return tuple(finish([(1, d) for d in away], [("far", 0)], [theirs], *common, done))


def solution(mesh):
    rows = P(("seq", "head"), None)
    return jax.shard_map(
        work,
        mesh=mesh,
        in_specs=(rows, rows, rows, rows, P()),
        out_specs=(rows, rows, rows),
        check_vma=False,
    )
```

```python
import functools

import jax
import jax.numpy as jnp
from jax import lax
from jax.experimental import pallas as pl
from jax.experimental.pallas import tpu as pltpu
from jax.sharding import PartitionSpec as P

DH = 128
BLOCK = 128
EXTRA = 16
TOP = 14.0
PIECE = 32
F32 = jnp.float32
BF16 = jnp.bfloat16
F16 = jnp.float16
NT = (((1,), (1,)), ((), ()))
TN = (((0,), (0,)), ((), ()))
VMEM = pl.BlockSpec(memory_space=pltpu.VMEM)
HBM = pl.BlockSpec(memory_space=pltpu.HBM)


def dot(a, b, dims=None):
    if dims is None:
        dims = (((1,), (0,)), ((), ()))
    return lax.dot_general(a, b, dims, preferred_element_type=F32)


def split(x):
    hi = x.astype(BF16)
    return hi, (x - hi.astype(F32)).astype(BF16)


def call(kernel, outs, args, specs=None, out_specs=None, scratch=(), flops=0, limit=2, aliases=None):
    moved = sum(x.size * x.dtype.itemsize for x in args)
    return pl.pallas_call(
        kernel,
        in_specs=specs or [VMEM] * len(args),
        out_specs=out_specs or [VMEM] * len(outs),
        out_shape=list(outs),
        scratch_shapes=list(scratch),
        input_output_aliases=aliases or {},
        compiler_params=pltpu.CompilerParams(vmem_limit_bytes=limit << 20),
        cost_estimate=pl.CostEstimate(flops=flops, bytes_accessed=moved, transcendentals=0),
    )(*args)


def partner(array, axis, distance):
    return lax.ppermute(array, axis, [(i, i ^ distance) for i in range(lax.axis_size(axis))])


def narrow(array, axis, distance):
    return partner(array.astype(F16), axis, distance).astype(F32)


def marks_of(value):
    most = jnp.maximum(jnp.max(jnp.abs(value)), 1e-30)
    return TOP - jnp.ceil(jnp.log2(jnp.full((8, DH), most, F32)))


def pack(out_ref, values):
    rows = 0
    marks = []
    for value in values:
        power = marks_of(value)
        flat = value.reshape(-1, DH)
        out_ref[rows : rows + flat.shape[0]] = flat * jnp.exp2(power)[:1]
        rows += flat.shape[0]
        marks.append(power)
    put_marks(out_ref, marks)


def put_marks(out_ref, marks):
    rows = out_ref.shape[0] - EXTRA
    for i in range(EXTRA // 8):
        out_ref[rows + 8 * i : rows + 8 * i + 8] = marks[min(i, len(marks) - 1)]


def mark(ref, index):
    rows = ref.shape[0] - EXTRA
    return ref[rows + 8 * index : rows + 8 * index + 8]


def bound_power(bound):
    return TOP - jnp.ceil(jnp.log2(jnp.maximum(bound, 1e-30)))


def unpack(ref, shape, count):
    size = (ref.shape[0] - EXTRA) // count
    return [
        (ref[i * size : (i + 1) * size] * jnp.exp2(-mark(ref, i)[:1])).reshape(shape) for i in range(count)
    ]


def pieces(width):
    return [(j, r, slice(r, r + PIECE)) for j in range(width) for r in range(0, DH, PIECE)]


def first_head(half, heads):
    return (lax.axis_index("head") ^ half) * heads


def near_place(slices):
    return lax.axis_index("seq") & (slices - 1)


def form_states(heads, held, out_ref, visit=None):
    q_ref, k_ref, v_ref, o_ref = held
    slices, _, width = out_ref.shape[:3]
    place = near_place(slices)
    for head in heads:
        d, j = place ^ (head // width), head % width
        cols = slice(head * DH, (head + 1) * DH)
        pairs = (dot(v_ref[:, cols], k_ref[:, cols], TN), dot(o_ref[:, cols], q_ref[:, cols], TN))
        for t in range(2):
            out_ref[d, t, j] = pairs[t]
            if visit:
                visit(t, pairs[t])


def first_kernel(cuts, *refs):
    srcs, (early_ref, late_ref), there, here, (out_ref, sems) = refs[:4], refs[4:6], refs[6:10], refs[10:14], refs[14:]
    slices = out_ref.shape[0]
    model = there[0].shape[1]
    size = model // cuts
    copies = []
    for c in range(cuts):
        start = pl.multiple_of(first_head(1, model // DH) * DH + c * size, DH)
        for i in range(4):
            copies.append(
                pltpu.make_async_copy(
                    srcs[i].at[:, pl.ds(start, size)], there[i].at[:, c * size : (c + 1) * size], sems.at[c, i]
                )
            )
    start = pl.multiple_of(first_head(0, model // DH) * DH, DH)
    for i in range(4):
        copies.append(pltpu.make_async_copy(srcs[i].at[:, pl.ds(start, model)], here[i], sems.at[cuts, i]))
    for copy in copies:
        copy.start()
    for c in range(cuts):
        for copy in copies[4 * c : 4 * c + 4]:
            copy.wait()
        form_states(range(c * size // DH, (c + 1) * size // DH), there, out_ref)
    late_ref[...] = out_ref[: slices - 1]
    early_ref[0] = out_ref[slices - 1]
    for copy in copies[4 * cuts :]:
        copy.wait()


def second_kernel(*refs):
    held, (out_ref, mark_ref) = refs[:4], refs[4:]
    most = [jnp.zeros((8, DH), F32)] * 2

    def visit(t, value):
        most[t] = jnp.maximum(most[t], jnp.max(jnp.abs(value).reshape(-1, 8, DH), axis=0))

    form_states(range(held[0].shape[1] // DH), held, out_ref, visit)
    for t in range(2):
        mark_ref[8 * t : 8 * t + 8] = jnp.full((8, DH), jnp.max(most[t]), F32)


def device_states(args, slices, width):
    tokens = args[0].shape[0]
    cuts = 1

    def states(count):
        return pltpu.VMEM((count, 2, width, DH, DH), F32)

    early, late, *held = call(
        functools.partial(first_kernel, cuts),
        [states(1), states(slices - 1)] + [pltpu.VMEM((tokens, slices * width * DH), BF16)] * 8,
        args,
        specs=[HBM] * 4,
        scratch=[states(slices), pltpu.SemaphoreType.DMA((cuts + 1, 4))],
        flops=4 * slices * width * tokens * DH * DH,
    )
    return early, late, held[4:], held[:4]


def own_states(held, slices, width):
    return call(
        second_kernel,
        [pltpu.VMEM((slices, 2, width, DH, DH), F32), pltpu.VMEM((16, DH), F32)],
        held,
        flops=4 * slices * width * held[0].shape[0] * DH * DH,
    )


def local_kernel(lot, width, scale_ref, *refs):
    held, out_ref = (refs[:4], refs[4:8]), refs[8]
    tokens, model = refs[0].shape
    blocks = tokens // BLOCK
    rows = lax.broadcasted_iota(jnp.int32, (BLOCK, BLOCK), 0)
    cols = lax.broadcasted_iota(jnp.int32, (BLOCK, BLOCK), 1)

    def blk(n, m=None):
        return slice(n * BLOCK, (n + 1 if m is None else m) * BLOCK)

    def spread(raw, weight, mask, cross):
        zero = jnp.zeros((BLOCK, BLOCK), BF16)
        high, low = [], []
        for n in range(blocks):
            tops, rests = [], []
            for m in range(blocks):
                part = raw[blk(n), blk(m)]
                top = rest = zero
                if m == n:
                    top = jnp.where(mask, part * weight(0), 0.0).astype(BF16)
                elif cross(n, m):
                    top, rest = split(part * weight((m ^ n).bit_length()))
                tops.append(top)
                rests.append(rest)
            high.append(jnp.concatenate(tops, axis=1) if blocks > 1 else tops[0])
            if any(cross(n, m) for m in range(blocks)):
                low.append((n, jnp.concatenate(rests, axis=1)))
        return high, low

    def product(high, low, values):
        out = dot(jnp.concatenate(high + [x for _, x in low], axis=0), values)
        rows = [out[blk(n)] for n in range(blocks)]
        for i, (n, _) in enumerate(low):
            rows[n] = rows[n] + out[blk(blocks + i)]
        return rows

    place = near_place(model // (width * DH))
    for index, (half, d) in enumerate(lot):
        group = place ^ d
        for j in range(width):
            at = pl.ds(pl.multiple_of((group * width + j) * DH, DH), DH)
            to = slice(j * DH, (j + 1) * DH)
            q, k, v, o = (ref[:, at] for ref in held[half])
            head = first_head(half, model // DH) + group * width + j

            def weight(level, head=head):
                return scale_ref[head, level : level + 1]

            high, low = spread(dot(k, q, NT), weight, rows <= cols, lambda n, m: m > n)
            for n, value in enumerate(product(high, low, o)):
                out_ref[index, 2, blk(n), to] = value
            high, low = spread(dot(o, v, NT), weight, rows >= cols, lambda n, m: m < n)
            for n, value in enumerate(product(high, low, k)):
                out_ref[index, 0, blk(n), to] = value
            key_grad = dot(jnp.concatenate(high, axis=0), q, TN)
            for n, value in low:
                key_grad = key_grad + dot(value, q[blk(n)], TN)
            out_ref[index, 1, :, to] = key_grad


def local_grads(lot, scales, held, width):
    tokens = held[0][0].shape[0]
    return call(
        functools.partial(local_kernel, lot, width),
        [pltpu.VMEM((len(lot), 3, tokens, width * DH), F32)],
        [scales, *held[0], *held[1]],
        flops=24 * tokens * BLOCK * width * DH * len(lot),
    )[0]


def chip_kernel(first, own_ref, other_ref, *out_refs):
    for index, out_ref in enumerate(out_refs):
        d = first + index
        values = [own_ref[d, t] + other_ref[index, t] for t in range(2)]
        if d:
            pack(out_ref, values)
            continue
        rows = (out_ref.shape[0] - EXTRA) // 2
        for t in range(2):
            out_ref[t * rows : (t + 1) * rows] = values[t].reshape(rows, DH)
        put_marks(out_ref, [marks_of(value) for value in values])


def bit_of(value, index):
    return ((value >> index) & 1).astype(F32)


def head_weight(scale_ref, place, slices, width, j, level):
    return scale_ref[first_head(0, slices * width) + place * width + j, level : level + 1]


def plane_kernel(plane_bits, base, rest, wide, scale_ref, keep_ref, *refs):
    slices = 1 << plane_bits
    parts, refs = (keep_ref, *refs[: slices - 1]), refs[slices - 1 :]
    near_ref, bound_ref, refs = refs[0], refs[1], refs[2:]
    total_ref = refs[0] if wide else None
    outs = refs[1:] if wide else refs
    width = near_ref.shape[2]
    place = near_place(slices)
    row = lax.axis_index("seq") // slices
    factors = [[None if e == 0 else jnp.exp2(-mark(parts[e], t)[:1]) for t in range(2)] for e in range(slices)]
    bounds = [
        functools.reduce(jnp.add, [jnp.exp2(TOP - mark(parts[e], t)) for e in range(slices)]) for t in range(2)
    ]
    for t in range(2):
        bound_ref[8 * t : 8 * t + 8] = bounds[t]
    ups = [bit_of(row, rest - len(outs) + i) for i in range(len(outs))]
    factor_out = []
    for out_ref, up in zip(outs, ups):
        power = bound_power(jnp.where(up > 0, bounds[1], bounds[0]))
        put_marks(out_ref, [power])
        factor_out.append(jnp.exp2(power)[:1])
    sides = [[bit_of(place ^ d, b) for b in range(plane_bits)] for d in range(slices)]
    for j, r, rows in pieces(width):
        weights = [head_weight(scale_ref, place, slices, width, j, base + b) for b in range(plane_bits)]
        values = []
        for t in range(2):
            at = (t * width + j) * DH + r
            loaded = [parts[e][at : at + PIECE] for e in range(slices)]
            loaded = [x if f[t] is None else x * f[t] for x, f in zip(loaded, factors)]
            sums = {}
            for b in range(plane_bits + 1):
                for first in range(0, slices, 1 << b):
                    half = 1 << (b - 1) if b else 0
                    sums[b, first] = loaded[first] if b == 0 else sums[b - 1, first] + sums[b - 1, first + half]
            values.append(sums)
        for d in range(slices):
            early, late = [], []
            for b in range(plane_bits):
                first = ((d >> b) ^ 1) << b
                up = sides[d][b]
                early.append((up * weights[b]) * values[0][b, first])
                late.append(((1.0 - up) * weights[b]) * values[1][b, first])
            zero = jnp.zeros((PIECE, DH), F32)
            near_ref[d, 0, j, rows] = functools.reduce(jnp.add, early) if early else zero
            near_ref[d, 1, j, rows] = functools.reduce(jnp.add, late) if late else zero
        total = [values[t][plane_bits, 0] for t in range(2)]
        for t in range(2):
            if wide:
                total_ref[t, j, rows] = total[t]
        at = j * DH + r
        for out_ref, up, factor in zip(outs, ups, factor_out):
            out_ref[at : at + PIECE] = jnp.where(up > 0, total[1], total[0]) * factor


def far_out(outs, total_ref, rest, slices):
    row = lax.axis_index("seq") // slices
    for i, out_ref in enumerate(outs):
        up = bit_of(row, rest - len(outs) + i)
        pack(out_ref, [jnp.where(up > 0, total_ref[1], total_ref[0])])


def merge_kernel(slices, index, level, rest, scale_ref, near_ref, bound_ref, total_ref, got_ref, near_out, bound_out, total_out, *outs):
    width = total_ref.shape[1]
    row = lax.axis_index("seq") // slices
    place = near_place(slices)
    up = bit_of(row, index)
    got = unpack(got_ref, (width, DH, DH), 2)
    for t in range(2):
        bound_out[8 * t : 8 * t + 8] = bound_ref[8 * t : 8 * t + 8] + jnp.exp2(TOP - mark(got_ref, t))
    for j in range(width):
        weight = head_weight(scale_ref, place, slices, width, j, level)
        for d in range(slices):
            near_out[d, 0, j] = near_ref[d, 0, j] + (up * weight) * got[0][j]
            near_out[d, 1, j] = near_ref[d, 1, j] + ((1.0 - up) * weight) * got[1][j]
    for t in range(2):
        total_out[t] = total_ref[t] + got[t]
    far_out(outs, total_out, rest, slices)


def back_kernel(slices, levels, bits, scale_ref, near_ref, bound_ref, *refs):
    count = len(levels)
    gots, (keep_ref, *outs) = refs[:count], refs[count:]
    width = near_ref.shape[2]
    row = lax.axis_index("seq") // slices
    place = near_place(slices)
    ups = [bit_of(row, bit) for bit in bits]
    bounds = [bound_ref[:8], bound_ref[8:]]
    for got_ref, up in zip(gots, ups):
        size = jnp.exp2(TOP - mark(got_ref, 0))
        bounds = [bounds[0] + up * size, bounds[1] + (1.0 - up) * size]
    head = first_head(0, scale_ref.shape[0] // lax.axis_size("head")) + place * width
    most = functools.reduce(jnp.maximum, [jnp.abs(scale_ref[head + j]) for j in range(width)])
    most = jnp.max(most, axis=0, keepdims=True)
    powers = [bound_power(most * bound) for bound in bounds]
    factors = [jnp.exp2(power)[:1] for power in powers]
    for out_ref in (keep_ref, *outs):
        put_marks(out_ref, powers)
    opened = [jnp.exp2(-mark(got_ref, 0)[:1]) for got_ref in gots]
    for j, r, rows in pieces(width):
        far = [jnp.zeros((PIECE, DH), F32)] * 2
        at = j * DH + r
        for got_ref, level, up, factor in zip(gots, levels, ups, opened):
            weight = head_weight(scale_ref, place, slices, width, j, level)
            got = got_ref[at : at + PIECE] * factor
            far = [far[0] + (up * weight) * got, far[1] + ((1.0 - up) * weight) * got]
        for d, out_ref in enumerate((keep_ref, *outs)):
            for t in range(2):
                value = near_ref[d, t, j, rows] + far[t]
                to = t * width * DH + at
                out_ref[to : to + PIECE] = value if d == 0 else value * factors[t]


def core_side(mine):
    second = lax.axis_index("head").astype(F32)
    return (second, 1.0 - second) if mine else (1.0 - second, second)


def near_core_kernel(level, slices, scale_ref, own_ref, keep_ref, out_ref):
    width = out_ref.shape[1]
    place = near_place(slices)
    sides = core_side(False)
    for j, r, rows in pieces(width):
        weight = head_weight(scale_ref, place, slices, width, j, level)
        for t in range(2):
            at = (t * width + j) * DH + r
            out_ref[t, j, rows] = keep_ref[at : at + PIECE] + (sides[t] * weight) * own_ref[0, t, j, rows]


def core_kernel(level, scale_ref, own_ref, most_ref, *refs):
    parts, out_ref = refs[:-1], refs[-1]
    slices, _, width = own_ref.shape[:3]
    place = near_place(slices)
    sides = core_side(False)
    first = first_head(0, scale_ref.shape[0] // lax.axis_size("head"))
    weights = [jnp.abs(scale_ref[first + h, level : level + 1]) for h in range(slices * width)]
    heaviest = functools.reduce(jnp.maximum, weights)
    powers = []
    for t in range(2):
        bound = functools.reduce(jnp.maximum, [jnp.exp2(TOP - mark(part, t)) for part in parts])
        powers.append(bound_power(bound + heaviest * most_ref[8 * t : 8 * t + 8]))
    put_marks(out_ref, powers)
    for d, part in enumerate(parts, 1):
        for t in range(2):
            opened = jnp.exp2(powers[t][:1] - mark(part, t)[:1])
            closed = sides[t] * jnp.exp2(powers[t][:1])
            for j, r, rows in pieces(width):
                weight = head_weight(scale_ref, place ^ d, slices, width, j, level)
                at = (t * width + j) * DH + r
                to = (((d - 1) * 2 + t) * width + j) * DH + r
                out_ref[to : to + PIECE] = part[at : at + PIECE] * opened + (closed * weight) * own_ref[d, t, j, rows]


def finish(items, kinds, states, held, parts, where, scales, level, model, before):
    tokens, cols = held[0][0].shape
    width = parts[0].shape[3] // DH
    slices = cols // (width * DH)
    halves = sorted({half for half, _ in items})
    args = [*states, scales, *[x for half in halves for x in held[half][1:]], *parts]
    specs = [VMEM] * len(args) + [HBM] * len(before)

    def kernel(*refs):
        given = dict(zip(kinds, refs))
        rest = refs[len(kinds) :]
        scale_ref, rest = rest[0], rest[1:]
        held_refs = {half: rest[3 * i : 3 * i + 3] for i, half in enumerate(halves)}
        local_refs, outs = rest[3 * len(halves) :], refs[len(specs) : len(specs) + 3]
        temps, sems = refs[-2], refs[-1]
        place = near_place(slices)
        sides = core_side(True)
        copies = []

        def state_of(half, d, j, t):
            rows = slice((t * width + j) * DH, (t * width + j + 1) * DH)
            if half == 0:
                got = given["got", d][rows]
                if d:
                    got = got * jnp.exp2(-mark(given["got", d], t)[:1])
                weight = head_weight(scale_ref, place ^ d, slices, width, j, level)
                return got + (sides[t] * weight) * given["other", d][given["index", d], t, j]
            if d == 0:
                return given["near", 0][t, j]
            ref = given["far", 0]
            at = (((d - 1) * 2 + t) * width + j) * DH
            return ref[at : at + DH] * jnp.exp2(-mark(ref, t)[:1])

        for d in range(slices):
            other = "other_a" if d == slices - 1 else "other_b"
            if other in given:
                given["other", d] = given[other]
                given["index", d] = 0 if d == slices - 1 else d
        for index, (half, d) in enumerate(items):
            k_ref, v_ref, o_ref = held_refs[half]
            group = place ^ d
            part, at_part = where[half, d]
            for j in range(width):
                at = pl.ds(pl.multiple_of((group * width + j) * DH, DH), DH)
                to = slice(j * DH, (j + 1) * DH)
                o, v, k = o_ref[:, at], v_ref[:, at], k_ref[:, at]
                hi, lo = split(state_of(half, d, j, 0))
                qg = dot(o, hi) + dot(o, lo)
                hi, lo = split(state_of(half, d, j, 1))
                kg = dot(v, hi) + dot(v, lo)
                vg = dot(k, hi, NT) + dot(k, lo, NT)
                for i, cross in enumerate((qg, kg, vg)):
                    temps[index, i, :, to] = (cross + local_refs[part][at_part, i, :, to]).astype(BF16)
            start = first_head(half, cols // DH) * DH + group * (width * DH)
            wide = pl.ds(pl.multiple_of(start, DH), width * DH)
            for i in range(3):
                copy = pltpu.make_async_copy(temps.at[index, i], outs[i].at[:, wide], sems.at[index, i])
                copy.start()
                copies.append(copy)
        for copy in copies:
            copy.wait()

    return call(
        kernel,
        [jax.ShapeDtypeStruct((tokens, model), BF16)] * 3,
        args + list(before),
        specs=specs,
        out_specs=[HBM] * 3,
        scratch=[pltpu.VMEM((len(items), 3, tokens, width * DH), BF16), pltpu.SemaphoreType.DMA((len(items), 3))],
        flops=12 * tokens * DH * width * DH * len(items),
        limit=4,
        aliases={len(args) + i: i for i in range(len(before))},
    )


def work(queries, key_rows, values, out_grad, level_weights):
    level_ids = jnp.arange(level_weights.shape[1], dtype=F32)
    level_scale = level_weights * jnp.exp2((1.0 - level_ids) / 2.0)[None, :] / jnp.sqrt(F32(DH * BLOCK))
    heads = level_weights.shape[0]
    tokens, model = queries.shape
    chain = lax.axis_size("seq")
    bits = chain.bit_length() - 1
    plane_bits = min(2, bits)
    slices = 1 << plane_bits
    width = heads // (lax.axis_size("head") * slices)
    local_levels = (tokens // BLOCK).bit_length() - 1
    base = local_levels + 2
    rest = bits - plane_bits
    direct = min(2, rest)

    padded = jnp.pad(level_scale, ((0, 0), (0, -level_scale.shape[1] % 8)))
    scales = jnp.broadcast_to(padded[:, :, None], (*padded.shape, DH))

    args = [pltpu.with_memory_space_constraint(x, pltpu.HBM) for x in (queries, key_rows, values, out_grad)]
    sent_a, sent_b, held_here, held_there = device_states(args, slices, width)
    other_a = partner(sent_a, "head", 1)
    other_b = partner(sent_b, "head", 1)
    own, most = own_states(held_here, slices, width)
    held = (held_here, held_there)
    every = [(half, d) for half in range(2) for d in range(slices)]
    ends = [0, 3 * len(every) // 8, 6 * len(every) // 8, len(every)]
    where, local = {}, []
    for low, high in zip(ends, ends[1:]):
        if low == high:
            continue
        for i, key in enumerate(every[low:high]):
            where[key] = (len(local), i)
        local.append(local_grads(tuple(every[low:high]), scales, held, width))

    state = pltpu.VMEM((2, width, DH, DH), F32)
    load = pltpu.VMEM((2 * width * DH + EXTRA, DH), F32)
    single = pltpu.VMEM((width * DH + EXTRA, DH), F32)
    near = pltpu.VMEM((slices, 2, width, DH, DH), F32)
    bound = pltpu.VMEM((16, DH), F32)

    last = call(functools.partial(chip_kernel, slices - 1), [load], [own, other_a])
    keep, *outs = call(functools.partial(chip_kernel, 0), [load] * (slices - 1), [own, other_b])
    outs += last
    got = []
    for d in range(1, slices):
        got.append(narrow(outs[d - 1], "seq", d))
    wide = rest > direct
    near_sum, bounds, *outs = call(
        functools.partial(plane_kernel, plane_bits, base, rest, wide),
        [near, bound] + ([state] if wide else [single] * direct),
        [scales, keep, *got],
    )
    total = outs[0] if wide else None
    for index in range(rest - direct):
        both = call(lambda ref, out: pack(out, [ref[0], ref[1]]), [load], [total])[0]
        arrived = narrow(both, "seq", slices << index)
        sending = direct if index + 1 == rest - direct else 0
        near_sum, bounds, total, *outs = call(
            functools.partial(merge_kernel, slices, index, base + plane_bits + index, rest),
            [near, bound, state] + [single] * sending,
            [scales, near_sum, bounds, total, arrived],
        )
    got, levels, which = [], [], []
    for step in range(1, 1 << direct):
        top = step.bit_length() - 1
        got.append(narrow(outs[top], "seq", (slices << (rest - direct)) * step))
        which.append(rest - direct + top)
        levels.append(base + plane_bits + rest - direct + top)
    keep, *outs = call(
        functools.partial(back_kernel, slices, levels, which), [load] * slices, [scales, near_sum, bounds, *got]
    )
    got = []
    for d in range(1, slices):
        got.append(narrow(outs[d - 1], "seq", d))
    level = local_levels + 1
    near_theirs = call(functools.partial(near_core_kernel, level, slices), [state], [scales, own, keep])[0]
    near_theirs = partner(near_theirs, "head", 1)
    rest_rows = pltpu.VMEM((2 * (slices - 1) * width * DH + EXTRA, DH), F32)
    theirs = call(functools.partial(core_kernel, level), [rest_rows], [scales, own, most, *got])[0]
    theirs = narrow(theirs, "head", 1)
    others = ["other_b", "other_a"]
    common = (held, local, where, scales, level, model)
    done = finish([(0, 0), (1, 0)], ["other_b", ("got", 0), ("near", 0)], [other_b, keep, near_theirs], *common, [])
    away = range(1, slices)
    done = finish([(0, d) for d in away], others + [("got", d) for d in away], [other_b, other_a, *got], *common, done)
    return tuple(finish([(1, d) for d in away], [("far", 0)], [theirs], *common, done))


def solution(mesh):
    rows = P(("seq", "head"), None)
    return jax.shard_map(
        work,
        mesh=mesh,
        in_specs=(rows, rows, rows, rows, P()),
        out_specs=(rows, rows, rows),
        check_vma=False,
    )
```
